32 devices in a mesh: table: 16 (over z, y, x), mp: 2 (over core).
Axes of the slice: x: 2, y: 2, z: 4, core: 2. Of those that a mesh axis runs over, the one named last changes fastest.
Arguments:
- hash_tables: bfloat16 [2, 16384, 4096], P(None, 'table', 'mp'), may hold values from -6 to 6
- byte_table: bfloat16 [256, 4096], P(None, 'mp'), may hold values from -6 to 6
- byte_ids: int32 [4096], P('table'), may hold values from 0 to 255
- hash_owner: int32 [2, 4096, 1], P(None, 'table'), may hold values from 0 to 15; in each aligned block of 256 rows (0 to 255, 256 to 511, ..., all dimensions but the last counted through in order) at most 32 rows name the same one
- hash_offset: int32 [2, 4096], P(None, 'table'), may hold values from 0 to 1023
- gain: float32 [4096], replicated, may hold values from 0.25 to 1.75
- proj_weight: bfloat16 [4096, 4096], P('table', 'mp'), may hold values from -0.09375 to 0.09375
- cotangent: bfloat16 [4096, 4096], P('table', 'mp'), may hold values from -6 to 6
Outputs:
- projected: bfloat16 [4096, 4096], P('table', 'mp')
- table_grads: bfloat16 [2, 16384, 4096], P(None, 'table', 'mp')
The draws below stay inside these ranges and needn't reach their ends.
Inputs may be any that keep to these rules, and one draw needn't show every extreme that they name: `hash_owner`: within the 256 bytes of one device and one table, no owner is named more than 32 times, a bound that some of these blocks reach.
All inputs are finite; a program needn't handle non-finite values.
Results may differ from the reference program's by a relative error of at most 0.0058.
Values may be sent and summed in bfloat16 or wider, within the bound.
A program may use at most 128 MiB of HBM per device.

```python
import math
import jax
import jax.numpy as jnp
import numpy as np
from jax import lax

D = 4096
NGRAMS = 2
ROWS_DEV = 1024
VOCAB = 256
TOK_DEV = 256
TOKENS = 4096
ROWS = 16384
CAP = 32
N_TABLE = 16


def plant(drawn, own_key, least, largest):
    spot = [jax.random.randint(jax.random.fold_in(own_key, axis), (), 0, length) for axis, length in enumerate(drawn.shape)]
    longest = drawn.shape.index(max(drawn.shape))
    beside = spot[:longest] + [(spot[longest] + 1) % drawn.shape[longest]] + spot[longest + 1:]
    return drawn.at[tuple(spot)].set(least).at[tuple(beside)].set(largest)


def steps_of(rng, dims, split, least, top_value):
    level = 1.0
    for dim, parts in split:
        steps = jax.random.uniform(jax.random.fold_in(jax.random.fold_in(rng, 6), dim), (parts,), jnp.float32, least / len(split), top_value / len(split))
        level = level * jnp.repeat(jnp.exp(steps), dims[dim] // parts).reshape((-1,) + (1,) * (len(dims) - 1 - dim))
    return level


def cumulative_ranks(number_of, lean):
    portions = [(1 << 20) // math.isqrt(grade ** lean) + 1 for grade in range(1, number_of + 1)]
    deviation = 1 + sum(portions) // (1 << 30)
    return np.cumsum(np.array([max(1, weight // deviation) for weight in portions]))


def ranked(stream_key, dims, amount, slope):
    table = cumulative_ranks(amount, slope)
    lot = jax.random.randint(jax.random.fold_in(stream_key, 1), dims, 0, int(table[amount - 1]))
    standing = jnp.searchsorted(jnp.asarray(table, jnp.int32), lot, side="right")
    return jax.random.permutation(jax.random.fold_in(stream_key, 2), amount)[standing].astype(jnp.int32)


def assign_block(stream_key, own, number, rows, amount, top, limit, lean):
    sequence = jax.random.permutation(stream_key, amount)
    packed, usual = load_shares(amount, rows * top, limit, lean, True), load_shares(amount, rows * top, limit, lean, False)
    places = jnp.arange(amount)

    def named(lengths, turn):
        used = int((lengths > 0).sum())
        fixed = max(1, used // 4)
        moved = fixed + (places - fixed + turn * (used - fixed)) % max(1, amount - fixed)
        return jnp.zeros((amount,), jnp.int32).at[sequence[jnp.where(places < fixed, places, moved)]].set(jnp.asarray(lengths, jnp.int32))

    lengths = jnp.where(number % 4 == 0, named(packed, number // 4), named(usual, number - number // 4 - 1))
    mixed = jax.random.permutation(jax.random.fold_in(own, 3), amount)
    donor, receiver = mixed[0:amount // 2 * 2:2], mixed[1:amount // 2 * 2:2]
    room = jnp.minimum(lengths[donor] - 1, limit - lengths[receiver]) // 2
    room = jnp.where((donor == sequence[0]) | (receiver == sequence[0]) | (lengths[receiver] == 0), 0, jnp.maximum(room, 0))
    moved = jax.random.randint(jax.random.fold_in(own, 4), (amount // 2,), 0, 1 << 20) % (room + 1)
    lengths = lengths.at[donor].add(-moved).at[receiver].add(moved)
    members = jnp.searchsorted(jnp.cumsum(lengths), jnp.arange(rows * top), side="right").astype(jnp.int32)
    grid = members.reshape(top, rows).T
    grid = grid[jax.random.permutation(jax.random.fold_in(own, 1), rows)]
    turn = jax.random.randint(jax.random.fold_in(own, 2), (rows, 1), 0, top)
    return jnp.take_along_axis(grid, (jnp.arange(top)[None, :] + turn) % top, axis=1)


def load_shares(number_of, total, limit, slope, full):
    portions = [(1 << 20) // math.isqrt(grade ** slope) + 1 for grade in range(1, number_of + 1)]
    largest = limit if full else min(limit, max(-(-total // number_of), total * portions[0] // sum(portions)))
    least = 1 if total - largest >= number_of - 1 else 0
    counts, surplus = [largest] + [least] * (number_of - 1), total - largest - least * (number_of - 1)
    while surplus > 0:
        movable = [i for i in range(1, number_of) if counts[i] < largest] or [i for i in range(1, number_of) if counts[i] < limit]
        mass, remaining = sum([portions[i] for i in movable]), surplus
        for i in movable:
            extra = min(limit - counts[i], max(1, remaining * portions[i] // mass), surplus)
            counts[i] = counts[i] + extra
            surplus = surplus - extra
    return np.array(counts)


def noise(stream_key, shape, scale, reach, pieces=(), kind=jnp.bfloat16):
    array = jax.random.normal(stream_key, shape, jnp.float32) * scale
    if len(pieces) > 0:
        array = steps_of(stream_key, shape, pieces, -0.22, 0.18) * array
    return jnp.clip(array, min=-reach, max=reach).astype(kind)


def setup_inputs(seed: int = 0) -> dict:
    keys = jax.random.split(jax.random.key(seed), 9)
    hash_tables = noise(keys[0], (NGRAMS, ROWS, D), 1.0, 6.0, ((1, 16), (2, 2)))
    byte_table = noise(keys[1], (VOCAB, D), 1.0, 6.0, ((1, 2),))
    byte_ids = plant(ranked(keys[2], (TOKENS,), VOCAB, 2), jax.random.fold_in(keys[2], 3), 0, VOCAB - 1).astype(jnp.int32)
    hash_owner_keys = jax.random.split(jax.random.fold_in(keys[3], 1), NGRAMS * TOKENS // TOK_DEV)
    hash_owner_turns = jax.random.permutation(jax.random.fold_in(keys[3], 3), NGRAMS * TOKENS // TOK_DEV)
    hash_owner = jax.vmap(lambda own, number: assign_block(jax.random.fold_in(keys[3], 2), own, number, TOK_DEV, N_TABLE, 1, CAP, 2))(hash_owner_keys, hash_owner_turns).reshape((NGRAMS, TOKENS, 1))
    hash_offset = plant(jax.random.randint(keys[4], (NGRAMS, TOKENS), 0, ROWS_DEV), jax.random.fold_in(keys[4], 1), 0, ROWS_DEV - 1).astype(jnp.int32)
    gain = jnp.clip(1.0 + 0.15 * jax.random.normal(keys[5], (D,), jnp.float32), 0.25, 1.75)
    proj_weight = noise(keys[6], (D, D), D ** -0.5, 0.09375, ((0, 16), (1, 2)))
    cotangent = noise(keys[7], (TOKENS, D), 1.0, 6.0, ((0, 16), (1, 2)))
    return {"hash_tables": hash_tables, "byte_table": byte_table, "byte_ids": byte_ids, "hash_owner": hash_owner, "hash_offset": hash_offset, "gain": gain, "proj_weight": proj_weight, "cotangent": cotangent}


eps = 1e-05

def reference(hash_tables, byte_table, byte_ids, hash_owner, hash_offset, gain, proj_weight, cotangent):
    hashed = (hash_owner[:, :, 0] * ROWS_DEV + hash_offset).astype(jnp.int32)
    summed = byte_table[byte_ids].astype(jnp.float32)
    for k in range(NGRAMS):
        summed = summed + hash_tables[k][hashed[k]].astype(jnp.float32)
    embedded = summed.astype(jnp.bfloat16)
    values = embedded.astype(jnp.float32)
    scale = lax.rsqrt(lax.optimization_barrier(jnp.mean(values * values, axis=1, keepdims=True)) + eps)
    normed = (values * scale * gain[None, :]).astype(jnp.bfloat16)
    projected = jnp.dot(normed, proj_weight, preferred_element_type=jnp.float32).astype(jnp.bfloat16)
    dnormed = lax.dot_general(cotangent, proj_weight, (((1,), (1,)), ((), ())), preferred_element_type=jnp.float32)
    scaled = dnormed * gain[None, :]
    inner = lax.optimization_barrier(jnp.mean(values * scaled, axis=1, keepdims=True))
    dembed = (scale * scaled - values * scale * scale * scale * inner).astype(jnp.bfloat16)
    grads = []
    for k in range(NGRAMS):
        total = jnp.zeros((ROWS, D), jnp.float32).at[hashed[k]].add(dembed.astype(jnp.float32))
        grads.append(total.astype(jnp.bfloat16))
    return (projected, jnp.stack(grads))
```

```python
import functools

import jax
import jax.numpy as jnp
from jax import lax
from jax.experimental import pallas as pl
from jax.experimental.pallas import tpu as pltpu
from jax.sharding import PartitionSpec as P

eps = 1e-05
MESH = pl.DeviceIdType.MESH
ANY = pl.BlockSpec(memory_space=pl.ANY)
WHOLE = pl.BlockSpec(memory_space=pltpu.VMEM)
VMEM_LIMIT = 58 * 2**20


def piece(i, size):
    return pl.ds(pl.multiple_of(i * size, size), size)


def greet_all(n):
    me = lax.axis_index("table")
    other = 1 - lax.axis_index("mp")
    barrier = pltpu.get_barrier_semaphore()
    for j in range(1, n):
        pl.semaphore_signal(
            barrier, inc=1, device_id={"table": lax.rem(me + j, n)}, device_id_type=MESH
        )
    pl.semaphore_signal(barrier, inc=1, device_id={"mp": other}, device_id_type=MESH)
    pl.semaphore_wait(barrier, n)
    return other


def remote(src, dst, send, recv, to):
    return pltpu.make_async_remote_copy(
        src_ref=src,
        dst_ref=dst,
        send_sem=send,
        recv_sem=recv,
        device_id=to,
        device_id_type=MESH,
    )


def factors(n):
    major = 1
    while major * major < n:
        major *= 2
    return major, n // major


def snake(i):
    return (i // 2) * 2 + (i % 2 + i // 2) % 2


def gather_steps(n):
    major, minor = factors(n)
    return 2 * (major - 1) + (2 * major - 1) * 2 * (minor // 2)


def run_gather(n, out_ref, depth, send, recv, between, done):
    major, minor = factors(n)
    half = minor // 2
    side = lax.rem(lax.axis_index("table"), 2)
    me = lax.axis_index("table") // 2
    row, place = me // minor, snake(me % minor)
    spot = [0]
    sends = []

    def always(body):
        body()

    def when(condition):
        return always if condition is None else pl.when(condition)

    def on_ring(r, shift):
        return r * minor + snake(lax.rem(place + shift + minor, minor))

    def copy_of(origin, part, to):
        size = depth if part is None else depth // 2
        offset = 0 if part is None else part * size
        at = pl.ds(pl.multiple_of(origin * depth + offset, size), size)
        copy = remote(
            out_ref.at[at],
            out_ref.at[at],
            send.at[spot[0]],
            recv.at[spot[0]],
            {"table": to * 2 + side},
        )
        spot[0] += 1
        return copy

    def has(shift):
        return jnp.logical_and(row + shift >= 0, row + shift < major)

    def line_go(step):
        copies = []
        for way in (1, -1):
            origin = lax.rem(row - way * (step - 1) + major, major)
            to = lax.rem(row + way + major, major)
            copy = copy_of(origin * minor + me % minor, None, to * minor + me % minor)
            leaves = jnp.logical_and(has(-way * (step - 1)), has(way))
            pl.when(leaves)(copy.start)
            sends.append((leaves, copy))
            copies.append((has(-way * step), copy))
        return copies

    def ring_go(block, present, step):
        pieces = (0, 1) if step == half else (None, None)
        pair = (
            copy_of(on_ring(block, 1 - step), pieces[0], on_ring(row, 1)),
            copy_of(on_ring(block, step - 1), pieces[1], on_ring(row, -1)),
        )
        for copy in pair:
            when(present)(copy.start)
            sends.append((present, copy))
        return pair

    blocks = [(row, None)]
    stage = [1]
    flight = line_go(1)
    rings = [ring_go(row, None, 1)]
    between(0)

    def advance(i):
        block, present = blocks[i]
        step = stage[i]
        stage[i] += 1
        for copy in rings[i]:
            when(present)(copy.wait_recv)
        if step < half:
            rings[i] = ring_go(block, present, step + 1)
        else:
            done(block, when(present))

    for step in range(1, major):
        for present, copy in flight:
            pl.when(present)(copy.wait_recv)
        if step + 1 < major:
            flight = line_go(step + 1)
        known = len(blocks)
        for way in (1, -1):
            block = lax.rem(row - way * step + major, major)
            blocks.append((block, has(-way * step)))
            stage.append(1)
            rings.append(ring_go(*blocks[-1], 1))
        between(step)
        for i in range(known):
            if stage[i] <= half:
                advance(i)
    between(major)
    for _ in range(half):
        for i in range(len(blocks)):
            if stage[i] <= half:
                advance(i)
    return [(when(present), copy) for present, copy in sends]


def rows_of(ref, d, capacity):
    return ref.at[:, piece(d, capacity)]


def gather_kernel(
    n, w_ref, asks_ref, table_ref, cot_ref, mark_ref, picks_ref, bytes_ref, gain_ref,
    w_out, asked_out, normed_ref, dembed_ref,
    w_all, asked, table, looked, y_ref, cots, part, beside, own, away, across, half_ref,
    sums, ws, wr, qs, qr, xs, xr, ts, ps, pr, cs, cr, gs, gr, ms, mr, local,
):
    other = greet_all(n)
    core = 1 - other
    major, minor = factors(n)
    me = lax.axis_index("table")
    side = lax.rem(me, 2)
    mate = {"table": me + 1 - 2 * side}
    twin = {"mp": other}
    depth = w_ref.shape[0]
    ngram, rows, width = table_ref.shape
    tokens = cot_ref.shape[0]
    quarter = width // 2
    capacity = looked.shape[1] // n
    lines, fast = factors(n // 2)
    each = lines // 2
    span = fast * 2 * depth
    tile = width // 4

    w_swap = remote(
        w_ref.at[:, piece(1 - side, quarter)], w_all.at[piece(me, depth)],
        ps.at[0], pr.at[0], mate,
    )
    c_swap = remote(
        cot_ref.at[:, piece(1 - side, quarter)], cots.at[piece(side, tokens)],
        ps.at[1], pr.at[1], mate,
    )
    keep = (
        pltpu.make_async_copy(
            w_ref.at[:, piece(side, quarter)], w_all.at[piece(me, depth)], local.at[0]
        ),
        pltpu.make_async_copy(
            cot_ref.at[:, piece(side, quarter)], cots.at[piece(side, tokens)], local.at[1]
        ),
    )
    loads = [
        pltpu.make_async_copy(table_ref.at[k], table.at[k], ts.at[k]) for k in range(ngram)
    ]
    questions = []
    for j in range(1, n):
        to = lax.rem(me + j, n)
        questions.append(
            remote(asks_ref.at[to], asked.at[me], qs.at[j], qr.at[j], {"table": to})
        )
    for copy in questions:
        copy.start()
    w_swap.start()
    for load in loads:
        load.start()
    for copy in keep:
        copy.start()
    c_swap.start()
    asked[me] = asks_ref[me]

    near, far = [], []
    for along in range(major):
        for over in range(minor):
            if along == 0 and over == 0:
                continue
            to = lax.rem(me // minor + along, major) * minor + lax.rem(me + over, minor)
            spot = along * minor + over
            (far if along else near).append(
                remote(
                    rows_of(looked, to, capacity), rows_of(y_ref, me, capacity),
                    xs.at[spot], xr.at[spot], {"table": to},
                )
            )
    mine = pltpu.make_async_copy(
        rows_of(looked, me, capacity), rows_of(y_ref, me, capacity), local.at[2]
    )
    group = 128 // capacity

    def look_up():
        for copy in questions:
            copy.wait_recv()
        for load in loads:
            load.wait()
        for q in range(n // group):
            for k in range(ngram):
                wanted = asked[q * group, k : k + 1, :]
                for i in range(1, group):
                    wanted = wanted + asked[q * group + i, k : k + 1, :]
                place = lax.broadcasted_iota(jnp.int32, (rows, 128), 0) + 1
                hit = (place == wanted).astype(jnp.float32).astype(jnp.bfloat16)

                @pl.loop(0, 4)
                def _(c):
                    columns = piece(c, tile)
                    found = lax.dot_general(
                        hit,
                        table[k, :, columns],
                        (((0,), (0,)), ((), ())),
                        preferred_element_type=jnp.float32,
                    )
                    looked[k, q * 128 : (q + 1) * 128, columns] = found.astype(looked.dtype)

    def between(i):
        if i == 0:
            for copy in far:
                copy.start()
            c_swap.wait_recv()
            keep[1].wait()
        if i == major:
            embed()

    totals = remote(sums.at[0], sums.at[1], ms.at[0], mr.at[0], twin)
    inners = remote(sums.at[2], sums.at[3], ms.at[1], mr.at[1], twin)

    def embed():
        mine.wait()
        for copy in near + far:
            copy.wait_recv()
        slots = n * capacity
        sums[0] = jnp.zeros(sums.shape[1:], jnp.float32)

        @pl.loop(0, 4)
        def _(c):
            columns = piece(c, tile)
            total = jnp.dot(
                picks_ref[...], bytes_ref[:, columns], preferred_element_type=jnp.float32
            )
            for k in range(ngram):
                total = total + jnp.dot(
                    mark_ref[:, k * slots : (k + 1) * slots],
                    y_ref[k, :, columns],
                    preferred_element_type=jnp.float32,
                )
            rounded = total.astype(half_ref.dtype)
            half_ref[:, columns] = rounded
            values = rounded.astype(jnp.float32)
            sums[0] += jnp.broadcast_to(
                jnp.sum(values * values, axis=1, keepdims=True), sums.shape[1:]
            )

        totals.start()

    chunk = min(512, span)

    def put_of(block):
        at = piece(block, span)
        return pltpu.make_async_copy(w_all.at[at], w_out.at[at], local.at[3 + block])

    def to_twin(block):
        return remote(
            part.at[:, piece(block, span)],
            beside.at[:, piece(lax.rem(block, each), span)],
            cs.at[lax.rem(block, each)],
            cr.at[lax.rem(block, each)],
            twin,
        )

    def to_mate(spot):
        at = piece(spot, span)
        return remote(away.at[:, at], across.at[:, at], gs.at[spot], gr.at[spot], mate)

    def finish(block):
        spot = lax.rem(block, each)

        @pl.when(block // each == core)
        def _():
            to_twin(block).wait_recv()

            @pl.loop(0, span // chunk)
            def _(c):
                come = pl.ds(pl.multiple_of(block * span + c * chunk, chunk), chunk)
                go = pl.ds(pl.multiple_of(spot * span + c * chunk, chunk), chunk)
                theirs, ours = piece(1 - side, tokens), piece(side, tokens)
                away[:, go] = (part[theirs, come] + beside[theirs, go]).astype(away.dtype)
                own[:, go] = part[ours, come] + beside[ours, go]

            to_mate(spot).start()

    waiting = []

    def done(block, when):
        @when
        def _():
            put_of(block).start()

            @pl.loop(0, span // chunk)
            def _(c):
                some = pl.ds(pl.multiple_of(block * span + c * chunk, chunk), chunk)
                part[:, some] = lax.dot_general(
                    cots[...],
                    w_all[some, :],
                    (((1,), (1,)), ((), ())),
                    preferred_element_type=jnp.float32,
                )

            pl.when(block // each == other)(to_twin(block).start)

        waiting.append((block, when))
        if len(waiting) > 1:
            settle()

    def settle():
        block, when = waiting.pop(0)
        when(functools.partial(finish, block))

    look_up()
    mine.start()
    for copy in near:
        copy.start()
    keep[0].wait()
    w_swap.wait_recv()
    started = run_gather(n // 2, w_all, 2 * depth, ws, wr, between, done)
    while waiting:
        settle()

    totals.wait_recv()
    full_width = 2 * width
    sums[4] = lax.rsqrt((sums[0] + sums[1]) / full_width + eps)
    sums[2] = jnp.zeros(sums.shape[1:], jnp.float32)
    for spot in range(each):
        to_mate(spot).wait_recv()

    @pl.loop(0, 4)
    def _(c):
        columns = piece(c, tile)
        gain = gain_ref[:, pl.ds(pl.multiple_of(core * width + c * tile, tile), tile)]
        scaled = (own[:, columns] + across[:, columns].astype(jnp.float32)) * gain
        own[:, columns] = scaled
        values = half_ref[:, columns].astype(jnp.float32)
        sums[2] += jnp.broadcast_to(
            jnp.sum(values * scaled, axis=1, keepdims=True), sums.shape[1:]
        )

    inners.start()

    @pl.loop(0, 4)
    def _(c):
        columns = piece(c, tile)
        gain = gain_ref[:, pl.ds(pl.multiple_of(core * width + c * tile, tile), tile)]
        values = half_ref[:, columns].astype(jnp.float32)
        normed_ref[:, columns] = (values * sums[4][:, :1] * gain).astype(normed_ref.dtype)

    inners.wait_recv()

    @pl.loop(0, 4)
    def _(c):
        columns = piece(c, tile)
        scale = sums[4][:, :1]
        inner = (sums[2][:, :1] + sums[3][:, :1]) / full_width
        values = half_ref[:, columns].astype(jnp.float32)
        dembed_ref[:, columns] = (
            scale * own[:, columns] - values * scale * scale * scale * inner
        ).astype(dembed_ref.dtype)

    asked_out[...] = asked[...]
    for copy in questions + near + far + [w_swap, c_swap, totals, inners]:
        copy.wait_send()
    for spot in range(each):
        to_twin(other * each + spot).wait_send()
        to_mate(spot).wait_send()
    for when, copy in started:
        when(copy.wait_send)
    for block in range(lines):
        put_of(block).wait()


def gather_and_exchange(w, asks, table, cot, mark, picks, codes, gain, capacity, n):
    steps = gather_steps(n // 2)
    lines = factors(n // 2)[0]
    ngram, _, width = table.shape
    tokens = cot.shape[0]
    depth = w.shape[0]
    half = (tokens, width)
    f32, bf16 = jnp.float32, jnp.bfloat16
    dma = pltpu.SemaphoreType.DMA
    return pl.pallas_call(
        functools.partial(gather_kernel, n),
        out_shape=(
            jax.ShapeDtypeStruct((n * depth, width // 2), w.dtype),
            jax.ShapeDtypeStruct(asks.shape, asks.dtype),
            jax.ShapeDtypeStruct(half, bf16),
            jax.ShapeDtypeStruct(half, bf16),
        ),
        in_specs=[ANY, WHOLE, ANY, ANY, WHOLE, WHOLE, WHOLE, WHOLE],
        out_specs=(ANY, WHOLE, WHOLE, WHOLE),
        scratch_shapes=[
            pltpu.VMEM((n * depth, width // 2), w.dtype),
            pltpu.VMEM(asks.shape, asks.dtype),
            pltpu.VMEM(table.shape, table.dtype),
            pltpu.VMEM((ngram, n * capacity, width), table.dtype),
            pltpu.VMEM((ngram, n * capacity, width), table.dtype),
            pltpu.VMEM((2 * tokens, width // 2), cot.dtype),
            pltpu.VMEM((2 * tokens, n * depth), f32),
            pltpu.VMEM((2 * tokens, width), f32),
            pltpu.VMEM(half, f32),
            pltpu.VMEM(half, bf16),
            pltpu.VMEM(half, bf16),
            pltpu.VMEM(half, bf16),
            pltpu.VMEM((5, tokens, 128), f32),
            dma((steps,)),
            dma((steps,)),
            dma((n,)),
            dma((n,)),
            dma((n,)),
            dma((n,)),
            dma((ngram,)),
            dma((2,)),
            dma((2,)),
            dma((lines // 2,)),
            dma((lines // 2,)),
            dma((lines // 2,)),
            dma((lines // 2,)),
            dma((2,)),
            dma((2,)),
            dma((3 + lines,)),
        ],
        compiler_params=pltpu.CompilerParams(
            collective_id=1, has_side_effects=True, vmem_limit_bytes=VMEM_LIMIT
        ),
    )(w, asks, table, cot, mark, picks, codes, gain)


def spread_kernel(
    n, dembed_ref, normed_ref, mark_ref, w_ref,
    arrived, proj_ref,
    w_all, sent, full, away, across, xs, xr, ns, nr, ps, pr, local,
):
    other = greet_all(n)
    core = 1 - other
    major, minor = factors(n)
    me = lax.axis_index("table")
    side = lax.rem(me, 2)
    mate = {"table": me + 1 - 2 * side}
    twin = {"mp": other}
    ngram, slots, width = sent.shape
    tokens = dembed_ref.shape[0]
    quarter = width // 2
    capacity = slots // n
    tile = width // 4
    load = pltpu.make_async_copy(w_ref, w_all, local.at[0])
    load.start()

    def at_of(whose):
        return full.at[piece(whose, tokens), piece(core, width)]

    swap = remote(normed_ref, at_of(side), ns.at[0], nr.at[0], mate)
    lend = remote(normed_ref, at_of(side), ns.at[1], nr.at[1], twin)
    pass_on = remote(at_of(1 - side), at_of(1 - side), ns.at[2], nr.at[2], twin)
    keep = pltpu.make_async_copy(normed_ref, at_of(side), local.at[1])
    swap.start()
    lend.start()
    keep.start()

    order = [along for along in range(major) if along] + [0]
    copies = []
    for along in order:
        for over in range(minor):
            if along == 0 and over == 0:
                continue
            to = lax.rem(me // minor + along, major) * minor + lax.rem(me + over, minor)
            spot = along * minor + over
            copies.append(
                remote(
                    rows_of(sent, to, capacity), rows_of(arrived, me, capacity),
                    xs.at[spot], xr.at[spot], {"table": to},
                )
            )
    mine = pltpu.make_async_copy(
        rows_of(sent, me, capacity), rows_of(arrived, me, capacity), local.at[2]
    )

    for k in range(ngram):
        @pl.loop(0, 4)
        def _(c):
            columns = piece(c, tile)
            sent[k, :, columns] = lax.dot_general(
                mark_ref[:, k * slots : (k + 1) * slots],
                dembed_ref[:, columns],
                (((0,), (0,)), ((), ())),
                preferred_element_type=jnp.float32,
            ).astype(sent.dtype)

    for copy in copies:
        copy.start()
    mine.start()

    swap.wait_recv()
    pass_on.start()
    load.wait()
    keep.wait()
    lend.wait_recv()
    pass_on.wait_recv()
    step = min(256, quarter)

    @pl.loop(0, quarter // step)
    def _(c):
        columns = piece(c, step)
        away[:, columns] = jnp.dot(
            full[piece(1 - side, tokens), :],
            w_all[:, columns],
            preferred_element_type=jnp.float32,
        ).astype(away.dtype)

    back = remote(away, across, ps.at[0], pr.at[0], mate)
    back.start()

    @pl.loop(0, quarter // step)
    def _(c):
        columns = piece(c, step)
        there = pl.ds(pl.multiple_of(side * quarter + c * step, step), step)
        proj_ref[:, there] = jnp.dot(
            full[piece(side, tokens), :],
            w_all[:, columns],
            preferred_element_type=jnp.float32,
        ).astype(proj_ref.dtype)

    back.wait_recv()
    proj_ref[:, piece(1 - side, quarter)] = across[...]
    mine.wait()
    for copy in copies:
        copy.wait_recv()
    for copy in copies + [swap, lend, pass_on, back]:
        copy.wait_send()


def spread(dembed, normed, mark, w, ngram, capacity, n):
    tokens, width = dembed.shape
    dma = pltpu.SemaphoreType.DMA
    bf16 = jnp.bfloat16
    return pl.pallas_call(
        functools.partial(spread_kernel, n),
        out_shape=(
            jax.ShapeDtypeStruct((ngram, n * capacity, width), bf16),
            jax.ShapeDtypeStruct((tokens, width), bf16),
        ),
        in_specs=[WHOLE, WHOLE, WHOLE, ANY],
        out_specs=(ANY, WHOLE),
        scratch_shapes=[
            pltpu.VMEM(w.shape, w.dtype),
            pltpu.VMEM((ngram, n * capacity, width), bf16),
            pltpu.VMEM((2 * tokens, 2 * width), bf16),
            pltpu.VMEM((tokens, width // 2), bf16),
            pltpu.VMEM((tokens, width // 2), bf16),
            dma((n,)),
            dma((n,)),
            dma((3,)),
            dma((3,)),
            dma((1,)),
            dma((1,)),
            dma((3,)),
        ],
        compiler_params=pltpu.CompilerParams(
            collective_id=2, has_side_effects=True, vmem_limit_bytes=VMEM_LIMIT
        ),
    )(dembed, normed, mark, w)


def on_device(
    hash_tables, byte_table, byte_ids, hash_owner, hash_offset, gain, proj_weight, cotangent
):
    groups = lax.axis_size("table")
    ngram, rows_dev, width = hash_tables.shape
    tokens = byte_ids.shape[0]
    capacity = 2 * tokens // groups
    span = groups * capacity
    places = jnp.arange(span, dtype=jnp.int32)
    owners = hash_owner[:, :, 0]
    named = owners[:, :, None] == jnp.arange(groups, dtype=jnp.int32)
    named = named.astype(jnp.float32)
    order = jnp.arange(tokens, dtype=jnp.int32)
    earlier = (order[:, None] > order[None, :]).astype(jnp.bfloat16)
    before = jnp.einsum(
        "ts,ksg->ktg", earlier, named.astype(jnp.bfloat16), preferred_element_type=jnp.float32
    )
    slots = owners * capacity + jnp.sum(before * named, axis=2).astype(jnp.int32)
    marks = slots[:, :, None] == places
    wanted = jnp.sum(jnp.where(marks, hash_offset[:, :, None] + 1, 0), axis=1)
    requests = wanted.reshape(ngram, groups, capacity)
    shared = 128 // capacity
    lane = jnp.arange(128, dtype=jnp.int32)
    stacked = jnp.tile(jnp.transpose(requests, (1, 0, 2)), (1, 1, shared))
    stacked = jnp.where(lane // capacity == lax.axis_index("table") % shared, stacked, 0)
    levels = -(-ngram // 8) * 8
    stacked = jnp.pad(stacked, ((0, 0), (0, levels - ngram), (0, 0)))
    mark = jnp.transpose(marks, (1, 0, 2)).reshape(tokens, ngram * span).astype(jnp.bfloat16)
    codes = jnp.arange(byte_table.shape[0], dtype=jnp.int32)
    picks = (byte_ids[:, None] == codes[None, :]).astype(jnp.bfloat16)
    weight, asked, normed, dembed = gather_and_exchange(
        proj_weight, stacked, hash_tables, cotangent, mark, picks, byte_table, gain[None, :],
        capacity, groups,
    )
    arrived, projected = spread(dembed, normed, mark, weight, ngram, capacity, groups)
    asked = jnp.sum(asked.reshape(groups // shared, shared, levels, 128)[:, :, :ngram], axis=1) - 1
    asked = jnp.transpose(asked, (1, 0, 2)).reshape(ngram, span)
    rows = jnp.arange(rows_dev, dtype=jnp.int32)
    hits = (asked[:, :, None] == rows[None, None, :]).astype(jnp.bfloat16)
    grads = lax.dot_general(
        hits, arrived, (((1,), (1,)), ((0,), (0,))), preferred_element_type=jnp.float32
    ).astype(jnp.bfloat16)
    return (projected, grads)


def solution(mesh):
    return jax.shard_map(
        on_device,
        mesh=mesh,
        in_specs=(
            P(None, "table", "mp"),
            P(None, "mp"),
            P("table"),
            P(None, "table", None),
            P(None, "table"),
            P(),
            P("table", "mp"),
            P("table", "mp"),
        ),
        out_specs=(P("table", "mp"), P(None, "table", "mp")),
        check_vma=False,
    )
```

```python
import functools

import jax
import jax.numpy as jnp
from jax import lax
from jax.experimental import pallas as pl
from jax.experimental.pallas import tpu as pltpu
from jax.sharding import PartitionSpec as P

eps = 1e-05
MESH = pl.DeviceIdType.MESH
ANY = pl.BlockSpec(memory_space=pl.ANY)
WHOLE = pl.BlockSpec(memory_space=pltpu.VMEM)
VMEM_LIMIT = 58 * 2**20


def piece(i, size):
    return pl.ds(pl.multiple_of(i * size, size), size)


def greet_all(n):
    me = lax.axis_index("table")
    other = 1 - lax.axis_index("mp")
    barrier = pltpu.get_barrier_semaphore()
    for j in range(1, n):
        pl.semaphore_signal(
            barrier, inc=1, device_id={"table": lax.rem(me + j, n)}, device_id_type=MESH
        )
    pl.semaphore_signal(barrier, inc=1, device_id={"mp": other}, device_id_type=MESH)
    pl.semaphore_wait(barrier, n)
    return other


def remote(src, dst, send, recv, to):
    return pltpu.make_async_remote_copy(
        src_ref=src,
        dst_ref=dst,
        send_sem=send,
        recv_sem=recv,
        device_id=to,
        device_id_type=MESH,
    )


def factors(n):
    major = 1
    while major * major < n:
        major *= 2
    return major, n // major


def snake(i):
    return (i // 2) * 2 + (i % 2 + i // 2) % 2


def gather_steps(n):
    major, minor = factors(n)
    return 2 * (major - 1) + (2 * major - 1) * 2 * (minor // 2)


def run_gather(n, out_ref, depth, send, recv, between, done):
    major, minor = factors(n)
    half = minor // 2
    side = lax.rem(lax.axis_index("table"), 2)
    me = lax.axis_index("table") // 2
    row, place = me // minor, snake(me % minor)
    spot = [0]
    sends = []

    def always(body):
        body()

    def when(condition):
        return always if condition is None else pl.when(condition)

    def on_ring(r, shift):
        return r * minor + snake(lax.rem(place + shift + minor, minor))

    def copy_of(origin, part, to):
        size = depth if part is None else depth // 2
        offset = 0 if part is None else part * size
        at = pl.ds(pl.multiple_of(origin * depth + offset, size), size)
        copy = remote(
            out_ref.at[at],
            out_ref.at[at],
            send.at[spot[0]],
            recv.at[spot[0]],
            {"table": to * 2 + side},
        )
        spot[0] += 1
        return copy

    def has(shift):
        return jnp.logical_and(row + shift >= 0, row + shift < major)

    def line_go(step):
        copies = []
        for way in (1, -1):
            origin = lax.rem(row - way * (step - 1) + major, major)
            to = lax.rem(row + way + major, major)
            copy = copy_of(origin * minor + me % minor, None, to * minor + me % minor)
            leaves = jnp.logical_and(has(-way * (step - 1)), has(way))
            pl.when(leaves)(copy.start)
            sends.append((leaves, copy))
            copies.append((has(-way * step), copy))
        return copies

    def ring_go(block, present, step):
        pieces = (0, 1) if step == half else (None, None)
        pair = (
            copy_of(on_ring(block, 1 - step), pieces[0], on_ring(row, 1)),
            copy_of(on_ring(block, step - 1), pieces[1], on_ring(row, -1)),
        )
        for copy in pair:
            when(present)(copy.start)
            sends.append((present, copy))
        return pair

    blocks = [(row, None)]
    stage = [1]
    flight = line_go(1)
    rings = [ring_go(row, None, 1)]
    between(0)

    def advance(i):
        block, present = blocks[i]
        step = stage[i]
        stage[i] += 1
        for copy in rings[i]:
            when(present)(copy.wait_recv)
        if step < half:
            rings[i] = ring_go(block, present, step + 1)
        else:
            done(block, when(present))

    for step in range(1, major):
        for present, copy in flight:
            pl.when(present)(copy.wait_recv)
        if step + 1 < major:
            flight = line_go(step + 1)
        known = len(blocks)
        for way in (1, -1):
            block = lax.rem(row - way * step + major, major)
            blocks.append((block, has(-way * step)))
            stage.append(1)
            rings.append(ring_go(*blocks[-1], 1))
        between(step)
        for i in range(known):
            if stage[i] <= half:
                advance(i)
    between(major)
    for _ in range(half):
        for i in range(len(blocks)):
            if stage[i] <= half:
                advance(i)
    return [(when(present), copy) for present, copy in sends]


def rows_of(ref, d, capacity):
    return ref.at[:, piece(d, capacity)]


def slot_marks(slots, first, amount):
    spot = lax.broadcasted_iota(jnp.int32, (amount, slots.shape[1]), 0) + first
    return (spot == slots).astype(jnp.float32).astype(jnp.bfloat16)


def gather_kernel(
    n, w_ref, asks_ref, slots_ref, table_ref, cot_ref, picks_ref, bytes_ref, gain_ref,
    w_out, asked_out, places_ref, normed_ref, dembed_ref,
    w_all, asked, table, looked, y_ref, cots, part, beside, own, away, across, half_ref,
    sums, chain, places, ws, wr, qs, qr, xs, xr, zs, zr, ts, ps, pr, cs, cr, gs, gr, ms, mr, ls, lr,
    local, still,
):
    other = greet_all(n)
    core = 1 - other
    major, minor = factors(n)
    me = lax.axis_index("table")
    row, place = me // minor, lax.rem(me, minor)
    side = lax.rem(me, 2)
    mate = {"table": me + 1 - 2 * side}
    twin = {"mp": other}
    depth = w_ref.shape[0]
    ngram, rows, width = table_ref.shape
    tokens = cot_ref.shape[0]
    quarter = width // 2
    capacity = looked.shape[1] // n
    plane = minor * capacity
    lines, fast = factors(n // 2)
    each = lines // 2
    span = fast * 2 * depth
    tile = width // 4

    def has(shift):
        return jnp.logical_and(row + shift >= 0, row + shift < major)

    w_swap = remote(
        w_ref.at[:, piece(1 - side, quarter)], w_all.at[piece(me, depth)],
        ps.at[0], pr.at[0], mate,
    )
    c_swap = remote(
        cot_ref.at[:, piece(1 - side, quarter)], cots.at[piece(side, tokens)],
        ps.at[1], pr.at[1], mate,
    )
    keep = (
        pltpu.make_async_copy(
            w_ref.at[:, piece(side, quarter)], w_all.at[piece(me, depth)], local.at[0]
        ),
        pltpu.make_async_copy(
            cot_ref.at[:, piece(side, quarter)], cots.at[piece(side, tokens)], local.at[1]
        ),
    )
    loads = [
        pltpu.make_async_copy(table_ref.at[k], table.at[k], ts.at[k]) for k in range(ngram)
    ]
    questions = []
    for j in range(1, n):
        to = lax.rem(me + j, n)
        questions.append(
            remote(asks_ref.at[to], asked.at[me], qs.at[j], qr.at[j], {"table": to})
        )
    tellings = []
    for j in range(1, major):
        to = lax.rem(row + j, major) * minor + place
        tellings.append(
            remote(slots_ref, places.at[row], ls.at[j], lr.at[j], {"table": to})
        )
    for copy in questions + tellings:
        copy.start()
    w_swap.start()
    for load in loads:
        load.start()
    for copy in keep:
        copy.start()
    c_swap.start()
    asked[me] = asks_ref[me]
    places[row] = slots_ref[...]

    def plane_copies(d):
        copies = []
        for j in range(1, minor):
            to = lax.rem(place + j, minor)
            copies.append(
                remote(
                    rows_of(looked, d * minor + to, capacity),
                    rows_of(y_ref, d * minor + place, capacity),
                    xs.at[d * minor + j], xr.at[d * minor + j], {"table": row * minor + to},
                )
            )
        return copies

    def stay(d):
        return pltpu.make_async_copy(
            rows_of(looked, d * minor + place, capacity),
            rows_of(y_ref, d * minor + place, capacity),
            still.at[d],
        )

    ends = [(d, way) for d in range(major - 1, 0, -1) for way in (1, -1)]

    def target(d, way):
        return lax.rem(row + way * d + major, major)

    def plane_go(d):
        for copy in plane_copies(d) + [stay(d)]:
            copy.start()

    group = 128 // capacity

    def look_up():
        for copy in questions:
            copy.wait_recv()
        for load in loads:
            load.wait()
        for q in range(n // group):
            for k in range(ngram):
                wanted = asked[q * group, k : k + 1, :]
                for i in range(1, group):
                    wanted = wanted + asked[q * group + i, k : k + 1, :]
                spot = lax.broadcasted_iota(jnp.int32, (rows, 128), 0) + 1
                hit = (spot == wanted).astype(jnp.float32).astype(jnp.bfloat16)

                @pl.loop(0, 4)
                def _(c):
                    columns = piece(c, tile)
                    found = lax.dot_general(
                        hit,
                        table[k, :, columns],
                        (((0,), (0,)), ((), ())),
                        preferred_element_type=jnp.float32,
                    )
                    looked[k, q * 128 : (q + 1) * 128, columns] = found.astype(looked.dtype)

    def arrive(d):
        for copy in plane_copies(d):
            copy.wait_recv()
        stay(d).wait()

    def part_of(d, columns):
        total = None
        for k in range(ngram):
            mark = slot_marks(places[d, k : k + 1, :], row * plane, plane)
            term = lax.dot_general(
                mark,
                y_ref[k, piece(d, plane), columns],
                (((0,), (0,)), ((), ())),
                preferred_element_type=jnp.float32,
            )
            total = term if total is None else total + term
        return total

    def chain_copy(d, way):
        to = lax.rem(row + way + major, major) * minor + place
        spot = (d - 1) * 2 + (0 if way == 1 else 1)
        land = major if d == 1 and way == -1 else target(d, way)
        return remote(
            chain.at[target(d, way)], chain.at[land], zs.at[spot], zr.at[spot], {"table": to}
        )

    def hop(d, way):
        @pl.when(has(way * d))
        def _():
            end = target(d, way)
            arrive(end)

            @pl.when(has(-way))
            def _():
                if d < major - 1:
                    chain_copy(d + 1, way).wait_recv()

            @pl.loop(0, 4)
            def _(c):
                columns = piece(c, tile)
                total = part_of(end, columns) + chain[end, :, columns].astype(jnp.float32)
                chain[end, :, columns] = total.astype(chain.dtype)

            chain_copy(d, way).start()

    def between(i):
        if i == 0:
            for j, (d, way) in enumerate(ends):
                pl.when(has(way * d))(functools.partial(plane_go, target(d, way)))
            plane_go(row)
            for way in (1, -1):
                @pl.when(jnp.logical_not(has(-way)))
                def _():
                    for d in range(0, major):
                        land = major if d == 0 and way == -1 else target(d, way)
                        chain[land] = jnp.zeros(chain.shape[1:], chain.dtype)

            for copy in tellings:
                copy.wait_recv()
            c_swap.wait_recv()
            keep[1].wait()
        elif i < major:
            for way in (1, -1):
                hop(major - i, way)
        else:
            embed()

    totals = remote(sums.at[0], sums.at[1], ms.at[0], mr.at[0], twin)
    inners = remote(sums.at[2], sums.at[3], ms.at[1], mr.at[1], twin)

    def embed():
        arrive(row)
        for way in (1, -1):
            pl.when(has(-way))(chain_copy(1, way).wait_recv)
        sums[0] = jnp.zeros(sums.shape[1:], jnp.float32)

        @pl.loop(0, 4)
        def _(c):
            columns = piece(c, tile)
            total = jnp.dot(
                picks_ref[...], bytes_ref[:, columns], preferred_element_type=jnp.float32
            )
            total = total + part_of(row, columns)
            total = total + chain[row, :, columns].astype(jnp.float32)
            total = total + chain[major, :, columns].astype(jnp.float32)
            rounded = total.astype(half_ref.dtype)
            half_ref[:, columns] = rounded
            values = rounded.astype(jnp.float32)
            sums[0] += jnp.broadcast_to(
                jnp.sum(values * values, axis=1, keepdims=True), sums.shape[1:]
            )

        totals.start()

    chunk = min(512, span)

    def put_of(block):
        at = piece(block, span)
        return pltpu.make_async_copy(w_all.at[at], w_out.at[at], local.at[3 + block])

    def to_twin(block):
        return remote(
            part.at[:, piece(block, span)],
            beside.at[:, piece(lax.rem(block, each), span)],
            cs.at[lax.rem(block, each)],
            cr.at[lax.rem(block, each)],
            twin,
        )

    def to_mate(spot):
        at = piece(spot, span)
        return remote(away.at[:, at], across.at[:, at], gs.at[spot], gr.at[spot], mate)

    def finish(block):
        spot = lax.rem(block, each)

        @pl.when(block // each == core)
        def _():
            to_twin(block).wait_recv()

            @pl.loop(0, span // chunk)
            def _(c):
                come = pl.ds(pl.multiple_of(block * span + c * chunk, chunk), chunk)
                go = pl.ds(pl.multiple_of(spot * span + c * chunk, chunk), chunk)
                theirs, ours = piece(1 - side, tokens), piece(side, tokens)
                away[:, go] = (part[theirs, come] + beside[theirs, go]).astype(away.dtype)
                own[:, go] = part[ours, come] + beside[ours, go]

            to_mate(spot).start()

    waiting = []

    def done(block, when):
        @when
        def _():
            put_of(block).start()

            @pl.loop(0, span // chunk)
            def _(c):
                some = pl.ds(pl.multiple_of(block * span + c * chunk, chunk), chunk)
                part[:, some] = lax.dot_general(
                    cots[...],
                    w_all[some, :],
                    (((1,), (1,)), ((), ())),
                    preferred_element_type=jnp.float32,
                )

            pl.when(block // each == other)(to_twin(block).start)

        waiting.append((block, when))
        if len(waiting) > 1:
            settle()

    def settle():
        block, when = waiting.pop(0)
        when(functools.partial(finish, block))

    look_up()
    keep[0].wait()
    w_swap.wait_recv()
    started = run_gather(n // 2, w_all, 2 * depth, ws, wr, between, done)
    while waiting:
        settle()

    totals.wait_recv()
    full_width = 2 * width
    sums[4] = lax.rsqrt((sums[0] + sums[1]) / full_width + eps)
    sums[2] = jnp.zeros(sums.shape[1:], jnp.float32)
    for spot in range(each):
        to_mate(spot).wait_recv()

    @pl.loop(0, 4)
    def _(c):
        columns = piece(c, tile)
        gain = gain_ref[:, pl.ds(pl.multiple_of(core * width + c * tile, tile), tile)]
        scaled = (own[:, columns] + across[:, columns].astype(jnp.float32)) * gain
        own[:, columns] = scaled
        values = half_ref[:, columns].astype(jnp.float32)
        sums[2] += jnp.broadcast_to(
            jnp.sum(values * scaled, axis=1, keepdims=True), sums.shape[1:]
        )

    inners.start()

    @pl.loop(0, 4)
    def _(c):
        columns = piece(c, tile)
        gain = gain_ref[:, pl.ds(pl.multiple_of(core * width + c * tile, tile), tile)]
        values = half_ref[:, columns].astype(jnp.float32)
        normed_ref[:, columns] = (values * sums[4][:, :1] * gain).astype(normed_ref.dtype)

    inners.wait_recv()

    @pl.loop(0, 4)
    def _(c):
        columns = piece(c, tile)
        scale = sums[4][:, :1]
        inner = (sums[2][:, :1] + sums[3][:, :1]) / full_width
        values = half_ref[:, columns].astype(jnp.float32)
        dembed_ref[:, columns] = (
            scale * own[:, columns] - values * scale * scale * scale * inner
        ).astype(dembed_ref.dtype)

    asked_out[...] = asked[...]
    places_ref[...] = places[...]
    for copy in questions + tellings + [w_swap, c_swap, totals, inners]:
        copy.wait_send()
    for d in range(major):
        for copy in plane_copies(d):
            copy.wait_send()
    for d, way in ends:
        pl.when(has(way * d))(chain_copy(d, way).wait_send)
    for spot in range(each):
        to_twin(other * each + spot).wait_send()
        to_mate(spot).wait_send()
    for when, copy in started:
        when(copy.wait_send)
    for block in range(lines):
        put_of(block).wait()


def gather_and_exchange(w, asks, slots, table, cot, picks, codes, gain, capacity, n):
    steps = gather_steps(n // 2)
    lines = factors(n // 2)[0]
    major, _ = factors(n)
    ngram, _, width = table.shape
    tokens = cot.shape[0]
    depth = w.shape[0]
    half = (tokens, width)
    f32, bf16 = jnp.float32, jnp.bfloat16
    dma = pltpu.SemaphoreType.DMA
    return pl.pallas_call(
        functools.partial(gather_kernel, n),
        out_shape=(
            jax.ShapeDtypeStruct((n * depth, width // 2), w.dtype),
            jax.ShapeDtypeStruct(asks.shape, asks.dtype),
            jax.ShapeDtypeStruct((major, *slots.shape), slots.dtype),
            jax.ShapeDtypeStruct(half, bf16),
            jax.ShapeDtypeStruct(half, bf16),
        ),
        in_specs=[ANY, WHOLE, WHOLE, ANY, ANY, WHOLE, WHOLE, WHOLE],
        out_specs=(ANY, WHOLE, WHOLE, WHOLE, WHOLE),
        scratch_shapes=[
            pltpu.VMEM((n * depth, width // 2), w.dtype),
            pltpu.VMEM(asks.shape, asks.dtype),
            pltpu.VMEM(table.shape, table.dtype),
            pltpu.VMEM((ngram, n * capacity, width), table.dtype),
            pltpu.VMEM((ngram, n * capacity, width), table.dtype),
            pltpu.VMEM((2 * tokens, width // 2), cot.dtype),
            pltpu.VMEM((2 * tokens, n * depth), f32),
            pltpu.VMEM((2 * tokens, width), f32),
            pltpu.VMEM(half, f32),
            pltpu.VMEM(half, bf16),
            pltpu.VMEM(half, bf16),
            pltpu.VMEM(half, bf16),
            pltpu.VMEM((5, tokens, 128), f32),
            pltpu.VMEM((major + 1, *half), bf16),
            pltpu.VMEM((major, *slots.shape), slots.dtype),
            dma((steps,)),
            dma((steps,)),
            dma((n,)),
            dma((n,)),
            dma((n,)),
            dma((n,)),
            dma((2 * (major - 1),)),
            dma((2 * (major - 1),)),
            dma((ngram,)),
            dma((2,)),
            dma((2,)),
            dma((lines // 2,)),
            dma((lines // 2,)),
            dma((lines // 2,)),
            dma((lines // 2,)),
            dma((2,)),
            dma((2,)),
            dma((major,)),
            dma((major,)),
            dma((3 + lines,)),
            dma((major,)),
        ],
        compiler_params=pltpu.CompilerParams(
            collective_id=1, has_side_effects=True, vmem_limit_bytes=VMEM_LIMIT
        ),
    )(w, asks, slots, table, cot, picks, codes, gain)


def spread_kernel(
    n, dembed_ref, normed_ref, places_ref, w_ref,
    arrived, proj_ref,
    w_all, line, sent, full, away, across, ls, lr, xs, xr, ns, nr, ps, pr, local, still,
):
    other = greet_all(n)
    core = 1 - other
    major, minor = factors(n)
    me = lax.axis_index("table")
    row, place = me // minor, lax.rem(me, minor)
    side = lax.rem(me, 2)
    mate = {"table": me + 1 - 2 * side}
    twin = {"mp": other}
    ngram, slots, width = sent.shape
    tokens = dembed_ref.shape[0]
    quarter = width // 2
    capacity = slots // n
    plane = minor * capacity
    tile = width // 4

    def has(shift):
        return jnp.logical_and(row + shift >= 0, row + shift < major)

    def line_copy(step, way):
        origin = lax.rem(row - way * (step - 1) + major, major)
        to = lax.rem(row + way + major, major) * minor + place
        spot = (step - 1) * 2 + (0 if way == 1 else 1)
        return remote(
            dembed_ref if step == 1 else line.at[origin], line.at[origin],
            ls.at[spot], lr.at[spot], {"table": to},
        )

    def leaves(step, way):
        return jnp.logical_and(has(-way * (step - 1)), has(way))

    for way in (1, -1):
        pl.when(leaves(1, way))(line_copy(1, way).start)
    load = pltpu.make_async_copy(w_ref, w_all, local.at[0])
    load.start()

    def at_of(whose):
        return full.at[piece(whose, tokens), piece(core, width)]

    swap = remote(normed_ref, at_of(side), ns.at[0], nr.at[0], mate)
    lend = remote(normed_ref, at_of(side), ns.at[1], nr.at[1], twin)
    pass_on = remote(at_of(1 - side), at_of(1 - side), ns.at[2], nr.at[2], twin)
    keep = pltpu.make_async_copy(normed_ref, at_of(side), local.at[1])
    swap.start()
    lend.start()
    keep.start()

    def give_copies(i, origin):
        copies = []
        for j in range(1, minor):
            to = lax.rem(place + j, minor)
            copies.append(
                remote(
                    rows_of(sent, origin * minor + to, capacity),
                    rows_of(arrived, origin * minor + place, capacity),
                    xs.at[i * minor + j], xr.at[i * minor + j], {"table": row * minor + to},
                )
            )
        return copies

    def stay(origin):
        return pltpu.make_async_copy(
            rows_of(sent, origin * minor + place, capacity),
            rows_of(arrived, origin * minor + place, capacity),
            still.at[origin],
        )

    def give(i, origin, rows_ref):
        for k in range(ngram):
            mark = slot_marks(places_ref[origin, k : k + 1, :], row * plane, plane)

            @pl.loop(0, 4)
            def _(c):
                columns = piece(c, tile)
                sent[k, piece(origin, plane), columns] = jnp.dot(
                    mark, rows_ref[:, columns], preferred_element_type=jnp.float32
                ).astype(sent.dtype)

        for copy in give_copies(i, origin) + [stay(origin)]:
            copy.start()

    back = remote(away, across, ps.at[0], pr.at[0], mate)
    step = min(256, quarter)

    def project():
        load.wait()
        keep.wait()
        lend.wait_recv()
        pass_on.wait_recv()

        @pl.loop(0, quarter // step)
        def _(c):
            columns = piece(c, step)
            away[:, columns] = jnp.dot(
                full[piece(1 - side, tokens), :],
                w_all[:, columns],
                preferred_element_type=jnp.float32,
            ).astype(away.dtype)

        back.start()

        @pl.loop(0, quarter // step)
        def _(c):
            columns = piece(c, step)
            there = pl.ds(pl.multiple_of(side * quarter + c * step, step), step)
            proj_ref[:, there] = jnp.dot(
                full[piece(side, tokens), :],
                w_all[:, columns],
                preferred_element_type=jnp.float32,
            ).astype(proj_ref.dtype)

    give(0, row, dembed_ref)
    swap.wait_recv()
    pass_on.start()
    blocks = [(0, row, None)]
    for s in range(1, major):
        for way in (1, -1):
            pl.when(has(-way * s))(line_copy(s, way).wait_recv)
        for way in (1, -1):
            if s + 1 < major:
                pl.when(leaves(s + 1, way))(line_copy(s + 1, way).start)
        for way in (1, -1):
            i, origin = len(blocks), lax.rem(row - way * s + major, major)
            present = has(-way * s)
            blocks.append((i, origin, present))

            @pl.when(present)
            def _():
                give(i, origin, line.at[origin])

        if s == 1:
            project()

    back.wait_recv()
    proj_ref[:, piece(1 - side, quarter)] = across[...]
    for i, origin, present in blocks:

        def end():
            for copy in give_copies(i, origin):
                copy.wait_recv()
                copy.wait_send()
            stay(origin).wait()

        if present is None:
            end()
        else:
            pl.when(present)(end)
    for copy in (swap, lend, pass_on, back):
        copy.wait_send()
    for s in range(1, major):
        for way in (1, -1):
            pl.when(leaves(s, way))(line_copy(s, way).wait_send)


def spread(dembed, normed, places, w, ngram, capacity, n):
    tokens, width = dembed.shape
    major, minor = factors(n)
    blocks = 2 * major - 1
    dma = pltpu.SemaphoreType.DMA
    bf16 = jnp.bfloat16
    return pl.pallas_call(
        functools.partial(spread_kernel, n),
        out_shape=(
            jax.ShapeDtypeStruct((ngram, n * capacity, width), bf16),
            jax.ShapeDtypeStruct((tokens, width), bf16),
        ),
        in_specs=[WHOLE, WHOLE, WHOLE, ANY],
        out_specs=(ANY, WHOLE),
        scratch_shapes=[
            pltpu.VMEM(w.shape, w.dtype),
            pltpu.VMEM((major, tokens, width), bf16),
            pltpu.VMEM((ngram, n * capacity, width), bf16),
            pltpu.VMEM((2 * tokens, 2 * width), bf16),
            pltpu.VMEM((tokens, width // 2), bf16),
            pltpu.VMEM((tokens, width // 2), bf16),
            dma((2 * (major - 1),)),
            dma((2 * (major - 1),)),
            dma((blocks * minor,)),
            dma((blocks * minor,)),
            dma((3,)),
            dma((3,)),
            dma((1,)),
            dma((1,)),
            dma((2,)),
            dma((major,)),
        ],
        compiler_params=pltpu.CompilerParams(
            collective_id=2, has_side_effects=True, vmem_limit_bytes=VMEM_LIMIT
        ),
    )(dembed, normed, places, w)


def on_device(
    hash_tables, byte_table, byte_ids, hash_owner, hash_offset, gain, proj_weight, cotangent
):
    groups = lax.axis_size("table")
    ngram, rows_dev, width = hash_tables.shape
    tokens = byte_ids.shape[0]
    capacity = 2 * tokens // groups
    span = groups * capacity
    places = jnp.arange(span, dtype=jnp.int32)
    owners = hash_owner[:, :, 0]
    named = owners[:, :, None] == jnp.arange(groups, dtype=jnp.int32)
    named = named.astype(jnp.float32)
    order = jnp.arange(tokens, dtype=jnp.int32)
    earlier = (order[:, None] > order[None, :]).astype(jnp.bfloat16)
    before = jnp.einsum(
        "ts,ksg->ktg", earlier, named.astype(jnp.bfloat16), preferred_element_type=jnp.float32
    )
    slots = owners * capacity + jnp.sum(before * named, axis=2).astype(jnp.int32)
    marks = slots[:, :, None] == places
    wanted = jnp.sum(jnp.where(marks, hash_offset[:, :, None] + 1, 0), axis=1)
    requests = wanted.reshape(ngram, groups, capacity)
    shared = 128 // capacity
    lane = jnp.arange(128, dtype=jnp.int32)
    stacked = jnp.tile(jnp.transpose(requests, (1, 0, 2)), (1, 1, shared))
    stacked = jnp.where(lane // capacity == lax.axis_index("table") % shared, stacked, 0)
    levels = -(-ngram // 8) * 8
    stacked = jnp.pad(stacked, ((0, 0), (0, levels - ngram), (0, 0)))
    slots = jnp.pad(slots, ((0, levels - ngram), (0, 0)))
    codes = jnp.arange(byte_table.shape[0], dtype=jnp.int32)
    picks = (byte_ids[:, None] == codes[None, :]).astype(jnp.bfloat16)
    weight, asked, line_slots, normed, dembed = gather_and_exchange(
        proj_weight, stacked, slots, hash_tables, cotangent, picks, byte_table, gain[None, :],
        capacity, groups,
    )
    arrived, projected = spread(dembed, normed, line_slots, weight, ngram, capacity, groups)
    asked = jnp.sum(asked.reshape(groups // shared, shared, levels, 128)[:, :, :ngram], axis=1) - 1
    asked = jnp.transpose(asked, (1, 0, 2)).reshape(ngram, span)
    rows = jnp.arange(rows_dev, dtype=jnp.int32)
    hits = (asked[:, :, None] == rows[None, None, :]).astype(jnp.bfloat16)
    grads = lax.dot_general(
        hits, arrived, (((1,), (1,)), ((0,), (0,))), preferred_element_type=jnp.float32
    ).astype(jnp.bfloat16)
    return (projected, grads)


def solution(mesh):
    return jax.shard_map(
        on_device,
        mesh=mesh,
        in_specs=(
            P(None, "table", "mp"),
            P(None, "mp"),
            P("table"),
            P(None, "table", None),
            P(None, "table"),
            P(),
            P("table", "mp"),
            P("table", "mp"),
        ),
        out_specs=(P("table", "mp"), P(None, "table", "mp")),
        check_vma=False,
    )
```

```python
import functools

import jax
import jax.numpy as jnp
from jax import lax
from jax.experimental import pallas as pl
from jax.experimental.pallas import tpu as pltpu
from jax.sharding import PartitionSpec as P

eps = 1e-05
MESH = pl.DeviceIdType.MESH
ANY = pl.BlockSpec(memory_space=pl.ANY)
WHOLE = pl.BlockSpec(memory_space=pltpu.VMEM)
VMEM_LIMIT = 58 * 2**20
EARLY = 7


def piece(i, size):
    return pl.ds(pl.multiple_of(i * size, size), size)


def greet_all(n):
    me = lax.axis_index("table")
    other = 1 - lax.axis_index("mp")
    barrier = pltpu.get_barrier_semaphore()
    for j in range(1, n):
        pl.semaphore_signal(
            barrier, inc=1, device_id={"table": lax.rem(me + j, n)}, device_id_type=MESH
        )
    pl.semaphore_signal(barrier, inc=1, device_id={"mp": other}, device_id_type=MESH)
    pl.semaphore_wait(barrier, n)
    return other


def remote(src, dst, send, recv, to):
    return pltpu.make_async_remote_copy(
        src_ref=src,
        dst_ref=dst,
        send_sem=send,
        recv_sem=recv,
        device_id=to,
        device_id_type=MESH,
    )


def factors(n):
    major = 1
    while major * major < n:
        major *= 2
    return major, n // major


def snake(i):
    return (i // 2) * 2 + (i % 2 + i // 2) % 2


def gather_steps(n):
    major, minor = factors(n)
    return 4 * major + 2 + (2 * major - 1) * 2 * (minor // 2)


def early_rows(depth, minor):
    return depth * EARLY // 32 * 2 if minor == 2 else 0


def run_gather(n, out_ref, depth, send, recv, begun, swapped, between, done, last):
    major, minor = factors(n)
    half = minor // 2
    early = early_rows(depth, minor)
    side = lax.rem(lax.axis_index("table"), 2)
    me = lax.axis_index("table") // 2
    row, place = me // minor, snake(me % minor)
    spot = [0]
    sends = []

    def always(body):
        body()

    def when(condition):
        return always if condition is None else pl.when(condition)

    def on_ring(r, shift):
        return r * minor + snake(lax.rem(place + shift + minor, minor))

    def copy_of(origin, offset, size, to):
        at = pl.ds(pl.multiple_of(origin * depth + offset, 16), size)
        copy = remote(
            out_ref.at[at],
            out_ref.at[at],
            send.at[spot[0]],
            recv.at[spot[0]],
            {"table": to * 2 + side},
        )
        spot[0] += 1
        return copy

    def has(shift):
        return jnp.logical_and(row + shift >= 0, row + shift < major)

    def line_go(step, over, offset, size):
        copies = []
        for way in (1, -1):
            origin = lax.rem(row - way * (step - 1) + major, major)
            to = lax.rem(row + way + major, major)
            column = me % minor if over == 0 else minor - 1 - me % minor
            copy = copy_of(origin * minor + column, offset, size, to * minor + me % minor)
            leaves = jnp.logical_and(has(-way * (step - 1)), has(way))
            pl.when(leaves)(copy.start)
            sends.append((leaves, copy))
            copies.append((has(-way * step), copy))
        return copies

    def ring_go(block, present, step, parts=None):
        if parts is None and step < half:
            parts = ((0, depth), (0, depth))
        elif parts is None:
            size = (depth - early) // 2
            parts = ((0, size), (depth - size, size))
        pair = (
            copy_of(on_ring(block, 1 - step), *parts[0], on_ring(row, 1)),
            copy_of(on_ring(block, step - 1), *parts[1], on_ring(row, -1)),
        )
        for copy in pair:
            when(present)(copy.start)
            sends.append((present, copy))
        return pair

    def start(copy):
        copy.start()
        sends.append((None, copy))
        return copy

    def land(copies):
        for present, copy in copies:
            pl.when(present)(copy.wait_recv)

    blocks = [(row, None)]
    stage = [1]
    low = depth // 2
    flight = line_go(1, 0, side * low, low)
    if early:
        first = [start(copy_of(me, side * low, low, on_ring(row, 1)))]
        begun()
        swapped()
        flight += line_go(1, 0, (1 - side) * low, low)
        first.append(start(copy_of(me, (1 - side) * low, low, on_ring(row, 1))))
        rings = [tuple(first)]
    else:
        begun()
        swapped()
        flight += line_go(1, 0, (1 - side) * low, low)
        rings = [ring_go(row, None, 1)]
    between(0)
    extra = []
    middle = (depth - early) // 2

    def advance(i):
        block, present = blocks[i]
        step = stage[i]
        stage[i] += 1
        for copy in rings[i]:
            when(present)(copy.wait_recv)
        if step < half:
            rings[i] = ring_go(block, present, step + 1)
        else:
            done(block, when(present))

    for step in range(1, major):
        land(flight)
        if step + 1 < major:
            flight = line_go(step + 1, 0, 0, depth)
        known = len(blocks)
        for way in (1, -1):
            block = lax.rem(row - way * step + major, major)
            blocks.append((block, has(-way * step)))
            stage.append(1)
            rings.append(ring_go(*blocks[-1], 1))
        if early:
            if step == 1:
                advance(0)
            land(extra)
            extra = line_go(step, 1, middle, early)
        between(step)
        for i in range(known):
            if stage[i] <= half:
                advance(i)
    land(extra)
    for _ in range(half):
        for i in range(len(blocks)):
            if stage[i] <= half:
                advance(i)
    last()
    return [(when(present), copy) for present, copy in sends]


def rows_of(ref, d, capacity):
    return ref.at[:, piece(d, capacity)]


def slot_marks(slots, first, amount):
    spot = lax.broadcasted_iota(jnp.int32, (amount, slots.shape[1]), 0) + first
    return (spot == slots).astype(jnp.float32).astype(jnp.bfloat16)


def gather_kernel(
    n, w_ref, asks_ref, slots_ref, table_ref, cot_ref, picks_ref, bytes_ref, gain_ref,
    w_out, asked_out, places_ref, normed_ref, dembed_ref,
    w_all, asked, table, looked, y_ref, cots, part, beside, own, away, across, half_ref,
    sums, chain, places, ws, wr, qs, qr, xs, xr, zs, zr, ts, ps, pr, cs, cr, gs, gr, ms, mr, ls, lr,
    local, still,
):
    other = greet_all(n)
    core = 1 - other
    major, minor = factors(n)
    me = lax.axis_index("table")
    row, place = me // minor, lax.rem(me, minor)
    side = lax.rem(me, 2)
    mate = {"table": me + 1 - 2 * side}
    twin = {"mp": other}
    depth = w_ref.shape[0]
    ngram, rows, width = table_ref.shape
    tokens = cot_ref.shape[0]
    quarter = width // 2
    capacity = looked.shape[1] // n
    plane = minor * capacity
    lines, fast = factors(n // 2)
    each = lines // 2
    span = fast * 2 * depth
    tile = width // 4

    def has(shift):
        return jnp.logical_and(row + shift >= 0, row + shift < major)

    w_swap = remote(
        w_ref.at[:, piece(1 - side, quarter)], w_all.at[piece(me, depth)],
        ps.at[0], pr.at[0], mate,
    )
    c_swap = remote(
        cot_ref.at[:, piece(1 - side, quarter)], cots.at[piece(side, tokens)],
        ps.at[1], pr.at[1], mate,
    )
    keep = (
        pltpu.make_async_copy(
            w_ref.at[:, piece(side, quarter)], w_all.at[piece(me, depth)], local.at[0]
        ),
        pltpu.make_async_copy(
            cot_ref.at[:, piece(side, quarter)], cots.at[piece(side, tokens)], local.at[1]
        ),
    )
    loads = [
        pltpu.make_async_copy(table_ref.at[k], table.at[k], ts.at[k]) for k in range(ngram)
    ]
    questions = []
    for j in range(1, n):
        to = lax.rem(me + j, n)
        questions.append(
            remote(asks_ref.at[to], asked.at[me], qs.at[j], qr.at[j], {"table": to})
        )
    tellings = []
    for j in range(1, major):
        to = lax.rem(row + j, major) * minor + place
        tellings.append(
            remote(slots_ref, places.at[row], ls.at[j], lr.at[j], {"table": to})
        )
    for copy in questions + tellings:
        copy.start()
    w_swap.start()
    for load in loads:
        load.start()
    for copy in keep:
        copy.start()
    c_swap.start()
    asked[me] = asks_ref[me]
    places[row] = slots_ref[...]

    def plane_copies(d):
        copies = []
        for j in range(1, minor):
            to = lax.rem(place + j, minor)
            copies.append(
                remote(
                    rows_of(looked, d * minor + to, capacity),
                    rows_of(y_ref, d * minor + place, capacity),
                    xs.at[d * minor + j], xr.at[d * minor + j], {"table": row * minor + to},
                )
            )
        return copies

    def stay(d):
        return pltpu.make_async_copy(
            rows_of(looked, d * minor + place, capacity),
            rows_of(y_ref, d * minor + place, capacity),
            still.at[d],
        )

    ends = [(d, way) for d in range(major - 1, 0, -1) for way in (1, -1)]

    def target(d, way):
        return lax.rem(row + way * d + major, major)

    def plane_go(d):
        for copy in plane_copies(d) + [stay(d)]:
            copy.start()

    group = 128 // capacity

    def look_up():
        for copy in questions:
            copy.wait_recv()
        for load in loads:
            load.wait()
        for q in range(n // group):
            for k in range(ngram):
                wanted = asked[q * group, k : k + 1, :]
                for i in range(1, group):
                    wanted = wanted + asked[q * group + i, k : k + 1, :]
                spot = lax.broadcasted_iota(jnp.int32, (rows, 128), 0) + 1
                hit = (spot == wanted).astype(jnp.float32).astype(jnp.bfloat16)

                @pl.loop(0, 4)
                def _(c):
                    columns = piece(c, tile)
                    found = lax.dot_general(
                        hit,
                        table[k, :, columns],
                        (((0,), (0,)), ((), ())),
                        preferred_element_type=jnp.float32,
                    )
                    looked[k, q * 128 : (q + 1) * 128, columns] = found.astype(looked.dtype)

    def arrive(d):
        for copy in plane_copies(d):
            copy.wait_recv()
        stay(d).wait()

    def part_of(d, columns):
        total = None
        for k in range(ngram):
            mark = slot_marks(places[d, k : k + 1, :], row * plane, plane)
            term = lax.dot_general(
                mark,
                y_ref[k, piece(d, plane), columns],
                (((0,), (0,)), ((), ())),
                preferred_element_type=jnp.float32,
            )
            total = term if total is None else total + term
        return total

    def chain_copy(d, way):
        to = lax.rem(row + way + major, major) * minor + place
        spot = (d - 1) * 2 + (0 if way == 1 else 1)
        land = major if d == 1 and way == -1 else target(d, way)
        return remote(
            chain.at[target(d, way)], chain.at[land], zs.at[spot], zr.at[spot], {"table": to}
        )

    def hop(d, way):
        @pl.when(has(way * d))
        def _():
            end = target(d, way)
            arrive(end)

            @pl.when(has(-way))
            def _():
                if d < major - 1:
                    chain_copy(d + 1, way).wait_recv()

            @pl.loop(0, 4)
            def _(c):
                columns = piece(c, tile)
                total = part_of(end, columns) + chain[end, :, columns].astype(jnp.float32)
                chain[end, :, columns] = total.astype(chain.dtype)

            chain_copy(d, way).start()

    def hand_out(d):
        if d == 0:
            plane_go(row)
        else:
            for way in (1, -1):
                pl.when(has(way * d))(functools.partial(plane_go, target(d, way)))

    def between(i):
        if i == 0:
            hand_out(major - 1)
            for way in (1, -1):
                @pl.when(jnp.logical_not(has(-way)))
                def _():
                    for d in range(0, major):
                        land = major if d == 0 and way == -1 else target(d, way)
                        chain[land] = jnp.zeros(chain.shape[1:], chain.dtype)

            for copy in tellings:
                copy.wait_recv()
            c_swap.wait_recv()
            keep[1].wait()
        else:
            for way in (1, -1):
                hop(major - i, way)
            hand_out(major - 1 - i)

    totals = remote(sums.at[0], sums.at[1], ms.at[0], mr.at[0], twin)
    inners = remote(sums.at[2], sums.at[3], ms.at[1], mr.at[1], twin)

    def embed():
        arrive(row)
        for way in (1, -1):
            pl.when(has(-way))(chain_copy(1, way).wait_recv)
        sums[0] = jnp.zeros(sums.shape[1:], jnp.float32)

        @pl.loop(0, 4)
        def _(c):
            columns = piece(c, tile)
            total = jnp.dot(
                picks_ref[...], bytes_ref[:, columns], preferred_element_type=jnp.float32
            )
            total = total + part_of(row, columns)
            total = total + chain[row, :, columns].astype(jnp.float32)
            total = total + chain[major, :, columns].astype(jnp.float32)
            rounded = total.astype(half_ref.dtype)
            half_ref[:, columns] = rounded
            values = rounded.astype(jnp.float32)
            sums[0] += jnp.broadcast_to(
                jnp.sum(values * values, axis=1, keepdims=True), sums.shape[1:]
            )

        totals.start()

    chunk = min(512, span)

    def put_of(block):
        at = piece(block, span)
        return pltpu.make_async_copy(w_all.at[at], w_out.at[at], local.at[3 + block])

    def to_twin(block):
        return remote(
            part.at[:, piece(block, span)],
            beside.at[:, piece(lax.rem(block, each), span)],
            cs.at[lax.rem(block, each)],
            cr.at[lax.rem(block, each)],
            twin,
        )

    def to_mate(spot):
        at = piece(spot, span)
        return remote(away.at[:, at], across.at[:, at], gs.at[spot], gr.at[spot], mate)

    def finish(block):
        spot = lax.rem(block, each)

        @pl.when(block // each == core)
        def _():
            to_twin(block).wait_recv()

            @pl.loop(0, span // chunk)
            def _(c):
                come = pl.ds(pl.multiple_of(block * span + c * chunk, chunk), chunk)
                go = pl.ds(pl.multiple_of(spot * span + c * chunk, chunk), chunk)
                theirs, ours = piece(1 - side, tokens), piece(side, tokens)
                away[:, go] = (part[theirs, come] + beside[theirs, go]).astype(away.dtype)
                own[:, go] = part[ours, come] + beside[ours, go]

            to_mate(spot).start()

    waiting = []

    def done(block, when):
        @when
        def _():
            put_of(block).start()

            @pl.loop(0, span // chunk)
            def _(c):
                some = pl.ds(pl.multiple_of(block * span + c * chunk, chunk), chunk)
                part[:, some] = lax.dot_general(
                    cots[...],
                    w_all[some, :],
                    (((1,), (1,)), ((), ())),
                    preferred_element_type=jnp.float32,
                )

            pl.when(block // each == other)(to_twin(block).start)

        waiting.append((block, when))
        if len(waiting) > 1:
            settle()

    def settle():
        block, when = waiting.pop(0)
        when(functools.partial(finish, block))

    keep[0].wait()
    started = run_gather(
        n // 2, w_all, 2 * depth, ws, wr, look_up, w_swap.wait_recv, between, done, embed
    )
    while waiting:
        settle()

    totals.wait_recv()
    full_width = 2 * width
    sums[4] = lax.rsqrt((sums[0] + sums[1]) / full_width + eps)
    sums[2] = jnp.zeros(sums.shape[1:], jnp.float32)
    for spot in range(each):
        to_mate(spot).wait_recv()

    @pl.loop(0, 4)
    def _(c):
        columns = piece(c, tile)
        gain = gain_ref[:, pl.ds(pl.multiple_of(core * width + c * tile, tile), tile)]
        scaled = (own[:, columns] + across[:, columns].astype(jnp.float32)) * gain
        own[:, columns] = scaled
        values = half_ref[:, columns].astype(jnp.float32)
        sums[2] += jnp.broadcast_to(
            jnp.sum(values * scaled, axis=1, keepdims=True), sums.shape[1:]
        )

    inners.start()

    @pl.loop(0, 4)
    def _(c):
        columns = piece(c, tile)
        gain = gain_ref[:, pl.ds(pl.multiple_of(core * width + c * tile, tile), tile)]
        values = half_ref[:, columns].astype(jnp.float32)
        normed_ref[:, columns] = (values * sums[4][:, :1] * gain).astype(normed_ref.dtype)

    inners.wait_recv()

    @pl.loop(0, 4)
    def _(c):
        columns = piece(c, tile)
        scale = sums[4][:, :1]
        inner = (sums[2][:, :1] + sums[3][:, :1]) / full_width
        values = half_ref[:, columns].astype(jnp.float32)
        dembed_ref[:, columns] = (
            scale * own[:, columns] - values * scale * scale * scale * inner
        ).astype(dembed_ref.dtype)

    asked_out[...] = asked[...]
    places_ref[...] = places[...]
    for copy in questions + tellings + [w_swap, c_swap, totals, inners]:
        copy.wait_send()
    for d in range(major):
        for copy in plane_copies(d):
            copy.wait_send()
    for d, way in ends:
        pl.when(has(way * d))(chain_copy(d, way).wait_send)
    for spot in range(each):
        to_twin(other * each + spot).wait_send()
        to_mate(spot).wait_send()
    for when, copy in started:
        when(copy.wait_send)
    for block in range(lines):
        put_of(block).wait()


def gather_and_exchange(w, asks, slots, table, cot, picks, codes, gain, capacity, n):
    steps = gather_steps(n // 2)
    lines = factors(n // 2)[0]
    major, _ = factors(n)
    ngram, _, width = table.shape
    tokens = cot.shape[0]
    depth = w.shape[0]
    half = (tokens, width)
    f32, bf16 = jnp.float32, jnp.bfloat16
    dma = pltpu.SemaphoreType.DMA
    return pl.pallas_call(
        functools.partial(gather_kernel, n),
        out_shape=(
            jax.ShapeDtypeStruct((n * depth, width // 2), w.dtype),
            jax.ShapeDtypeStruct(asks.shape, asks.dtype),
            jax.ShapeDtypeStruct((major, *slots.shape), slots.dtype),
            jax.ShapeDtypeStruct(half, bf16),
            jax.ShapeDtypeStruct(half, bf16),
        ),
        in_specs=[ANY, WHOLE, WHOLE, ANY, ANY, WHOLE, WHOLE, WHOLE],
        out_specs=(ANY, WHOLE, WHOLE, WHOLE, WHOLE),
        scratch_shapes=[
            pltpu.VMEM((n * depth, width // 2), w.dtype),
            pltpu.VMEM(asks.shape, asks.dtype),
            pltpu.VMEM(table.shape, table.dtype),
            pltpu.VMEM((ngram, n * capacity, width), table.dtype),
            pltpu.VMEM((ngram, n * capacity, width), table.dtype),
            pltpu.VMEM((2 * tokens, width // 2), cot.dtype),
            pltpu.VMEM((2 * tokens, n * depth), f32),
            pltpu.VMEM((2 * tokens, width), f32),
            pltpu.VMEM(half, f32),
            pltpu.VMEM(half, bf16),
            pltpu.VMEM(half, bf16),
            pltpu.VMEM(half, bf16),
            pltpu.VMEM((5, tokens, 128), f32),
            pltpu.VMEM((major + 1, *half), bf16),
            pltpu.VMEM((major, *slots.shape), slots.dtype),
            dma((steps,)),
            dma((steps,)),
            dma((n,)),
            dma((n,)),
            dma((n,)),
            dma((n,)),
            dma((2 * (major - 1),)),
            dma((2 * (major - 1),)),
            dma((ngram,)),
            dma((2,)),
            dma((2,)),
            dma((lines // 2,)),
            dma((lines // 2,)),
            dma((lines // 2,)),
            dma((lines // 2,)),
            dma((2,)),
            dma((2,)),
            dma((major,)),
            dma((major,)),
            dma((3 + lines,)),
            dma((major,)),
        ],
        compiler_params=pltpu.CompilerParams(
            collective_id=1, has_side_effects=True, vmem_limit_bytes=VMEM_LIMIT
        ),
    )(w, asks, slots, table, cot, picks, codes, gain)


def spread_kernel(
    n, dembed_ref, normed_ref, places_ref, w_ref,
    arrived, proj_ref,
    w_all, line, sent, full, away, across, ls, lr, xs, xr, ns, nr, ps, pr, local, still,
):
    other = greet_all(n)
    core = 1 - other
    major, minor = factors(n)
    me = lax.axis_index("table")
    row, place = me // minor, lax.rem(me, minor)
    side = lax.rem(me, 2)
    mate = {"table": me + 1 - 2 * side}
    twin = {"mp": other}
    ngram, slots, width = sent.shape
    tokens = dembed_ref.shape[0]
    quarter = width // 2
    capacity = slots // n
    plane = minor * capacity
    tile = width // 4

    def has(shift):
        return jnp.logical_and(row + shift >= 0, row + shift < major)

    def line_copy(step, way):
        origin = lax.rem(row - way * (step - 1) + major, major)
        to = lax.rem(row + way + major, major) * minor + place
        spot = (step - 1) * 2 + (0 if way == 1 else 1)
        return remote(
            dembed_ref if step == 1 else line.at[origin], line.at[origin],
            ls.at[spot], lr.at[spot], {"table": to},
        )

    def leaves(step, way):
        return jnp.logical_and(has(-way * (step - 1)), has(way))

    for way in (1, -1):
        pl.when(leaves(1, way))(line_copy(1, way).start)
    load = pltpu.make_async_copy(w_ref, w_all, local.at[0])
    load.start()

    def at_of(whose):
        return full.at[piece(whose, tokens), piece(core, width)]

    swap = remote(normed_ref, at_of(side), ns.at[0], nr.at[0], mate)
    lend = remote(normed_ref, at_of(side), ns.at[1], nr.at[1], twin)
    pass_on = remote(at_of(1 - side), at_of(1 - side), ns.at[2], nr.at[2], twin)
    keep = pltpu.make_async_copy(normed_ref, at_of(side), local.at[1])
    swap.start()
    lend.start()
    keep.start()

    def give_copies(i, origin):
        copies = []
        for j in range(1, minor):
            to = lax.rem(place + j, minor)
            copies.append(
                remote(
                    rows_of(sent, origin * minor + to, capacity),
                    rows_of(arrived, origin * minor + place, capacity),
                    xs.at[i * minor + j], xr.at[i * minor + j], {"table": row * minor + to},
                )
            )
        return copies

    def stay(origin):
        return pltpu.make_async_copy(
            rows_of(sent, origin * minor + place, capacity),
            rows_of(arrived, origin * minor + place, capacity),
            still.at[origin],
        )

    def give(i, origin, rows_ref):
        for k in range(ngram):
            mark = slot_marks(places_ref[origin, k : k + 1, :], row * plane, plane)

            @pl.loop(0, 4)
            def _(c):
                columns = piece(c, tile)
                sent[k, piece(origin, plane), columns] = jnp.dot(
                    mark, rows_ref[:, columns], preferred_element_type=jnp.float32
                ).astype(sent.dtype)

        for copy in give_copies(i, origin) + [stay(origin)]:
            copy.start()

    back = remote(away, across, ps.at[0], pr.at[0], mate)
    step = min(256, quarter)

    def project():
        load.wait()
        keep.wait()
        lend.wait_recv()
        pass_on.wait_recv()

        @pl.loop(0, quarter // step)
        def _(c):
            columns = piece(c, step)
            away[:, columns] = jnp.dot(
                full[piece(1 - side, tokens), :],
                w_all[:, columns],
                preferred_element_type=jnp.float32,
            ).astype(away.dtype)

        back.start()

        @pl.loop(0, quarter // step)
        def _(c):
            columns = piece(c, step)
            there = pl.ds(pl.multiple_of(side * quarter + c * step, step), step)
            proj_ref[:, there] = jnp.dot(
                full[piece(side, tokens), :],
                w_all[:, columns],
                preferred_element_type=jnp.float32,
            ).astype(proj_ref.dtype)

    give(0, row, dembed_ref)
    swap.wait_recv()
    pass_on.start()
    blocks = [(0, row, None)]
    for s in range(1, major):
        for way in (1, -1):
            pl.when(has(-way * s))(line_copy(s, way).wait_recv)
        for way in (1, -1):
            if s + 1 < major:
                pl.when(leaves(s + 1, way))(line_copy(s + 1, way).start)
        for way in (1, -1):
            i, origin = len(blocks), lax.rem(row - way * s + major, major)
            present = has(-way * s)
            blocks.append((i, origin, present))

            @pl.when(present)
            def _():
                give(i, origin, line.at[origin])

        if s == 1:
            project()

    back.wait_recv()
    proj_ref[:, piece(1 - side, quarter)] = across[...]
    for i, origin, present in blocks:

        def end():
            for copy in give_copies(i, origin):
                copy.wait_recv()
                copy.wait_send()
            stay(origin).wait()

        if present is None:
            end()
        else:
            pl.when(present)(end)
    for copy in (swap, lend, pass_on, back):
        copy.wait_send()
    for s in range(1, major):
        for way in (1, -1):
            pl.when(leaves(s, way))(line_copy(s, way).wait_send)


def spread(dembed, normed, places, w, ngram, capacity, n):
    tokens, width = dembed.shape
    major, minor = factors(n)
    blocks = 2 * major - 1
    dma = pltpu.SemaphoreType.DMA
    bf16 = jnp.bfloat16
    return pl.pallas_call(
        functools.partial(spread_kernel, n),
        out_shape=(
            jax.ShapeDtypeStruct((ngram, n * capacity, width), bf16),
            jax.ShapeDtypeStruct((tokens, width), bf16),
        ),
        in_specs=[WHOLE, WHOLE, WHOLE, ANY],
        out_specs=(ANY, WHOLE),
        scratch_shapes=[
            pltpu.VMEM(w.shape, w.dtype),
            pltpu.VMEM((major, tokens, width), bf16),
            pltpu.VMEM((ngram, n * capacity, width), bf16),
            pltpu.VMEM((2 * tokens, 2 * width), bf16),
            pltpu.VMEM((tokens, width // 2), bf16),
            pltpu.VMEM((tokens, width // 2), bf16),
            dma((2 * (major - 1),)),
            dma((2 * (major - 1),)),
            dma((blocks * minor,)),
            dma((blocks * minor,)),
            dma((3,)),
            dma((3,)),
            dma((1,)),
            dma((1,)),
            dma((2,)),
            dma((major,)),
        ],
        compiler_params=pltpu.CompilerParams(
            collective_id=2, has_side_effects=True, vmem_limit_bytes=VMEM_LIMIT
        ),
    )(dembed, normed, places, w)


def on_device(
    hash_tables, byte_table, byte_ids, hash_owner, hash_offset, gain, proj_weight, cotangent
):
    groups = lax.axis_size("table")
    ngram, rows_dev, width = hash_tables.shape
    tokens = byte_ids.shape[0]
    capacity = 2 * tokens // groups
    span = groups * capacity
    places = jnp.arange(span, dtype=jnp.int32)
    owners = hash_owner[:, :, 0]
    named = owners[:, :, None] == jnp.arange(groups, dtype=jnp.int32)
    named = named.astype(jnp.float32)
    order = jnp.arange(tokens, dtype=jnp.int32)
    earlier = (order[:, None] > order[None, :]).astype(jnp.bfloat16)
    before = jnp.einsum(
        "ts,ksg->ktg", earlier, named.astype(jnp.bfloat16), preferred_element_type=jnp.float32
    )
    slots = owners * capacity + jnp.sum(before * named, axis=2).astype(jnp.int32)
    marks = slots[:, :, None] == places
    wanted = jnp.sum(jnp.where(marks, hash_offset[:, :, None] + 1, 0), axis=1)
    requests = wanted.reshape(ngram, groups, capacity)
    shared = 128 // capacity
    lane = jnp.arange(128, dtype=jnp.int32)
    stacked = jnp.tile(jnp.transpose(requests, (1, 0, 2)), (1, 1, shared))
    stacked = jnp.where(lane // capacity == lax.axis_index("table") % shared, stacked, 0)
    levels = -(-ngram // 8) * 8
    stacked = jnp.pad(stacked, ((0, 0), (0, levels - ngram), (0, 0)))
    slots = jnp.pad(slots, ((0, levels - ngram), (0, 0)))
    codes = jnp.arange(byte_table.shape[0], dtype=jnp.int32)
    picks = (byte_ids[:, None] == codes[None, :]).astype(jnp.bfloat16)
    weight, asked, line_slots, normed, dembed = gather_and_exchange(
        proj_weight, stacked, slots, hash_tables, cotangent, picks, byte_table, gain[None, :],
        capacity, groups,
    )
    arrived, projected = spread(dembed, normed, line_slots, weight, ngram, capacity, groups)
    asked = jnp.sum(asked.reshape(groups // shared, shared, levels, 128)[:, :, :ngram], axis=1) - 1
    asked = jnp.transpose(asked, (1, 0, 2)).reshape(ngram, span)
    rows = jnp.arange(rows_dev, dtype=jnp.int32)
    hits = (asked[:, :, None] == rows[None, None, :]).astype(jnp.bfloat16)
    grads = lax.dot_general(
        hits, arrived, (((1,), (1,)), ((0,), (0,))), preferred_element_type=jnp.float32
    ).astype(jnp.bfloat16)
    return (projected, grads)


def solution(mesh):
    return jax.shard_map(
        on_device,
        mesh=mesh,
        in_specs=(
            P(None, "table", "mp"),
            P(None, "mp"),
            P("table"),
            P(None, "table", None),
            P(None, "table"),
            P(),
            P("table", "mp"),
            P("table", "mp"),
        ),
        out_specs=(P("table", "mp"), P(None, "table", "mp")),
        check_vma=False,
    )
```

```python
import functools

import jax
import jax.numpy as jnp
from jax import lax
from jax.experimental import pallas as pl
from jax.experimental.pallas import tpu as pltpu
from jax.sharding import PartitionSpec as P

eps = 1e-05
MESH = pl.DeviceIdType.MESH
ANY = pl.BlockSpec(memory_space=pl.ANY)
WHOLE = pl.BlockSpec(memory_space=pltpu.VMEM)
VMEM_LIMIT = 61 * 2**20
EARLY = 7


def piece(i, size):
    return pl.ds(pl.multiple_of(i * size, size), size)


def greet_all(n, meanwhile=None):
    me = lax.axis_index("table")
    other = 1 - lax.axis_index("mp")
    barrier = pltpu.get_barrier_semaphore()
    for j in range(1, n):
        pl.semaphore_signal(
            barrier, inc=1, device_id={"table": lax.rem(me + j, n)}, device_id_type=MESH
        )
    pl.semaphore_signal(barrier, inc=1, device_id={"mp": other}, device_id_type=MESH)
    if meanwhile is not None:
        meanwhile()
    pl.semaphore_wait(barrier, n)
    return other


def remote(src, dst, send, recv, to):
    return pltpu.make_async_remote_copy(
        src_ref=src,
        dst_ref=dst,
        send_sem=send,
        recv_sem=recv,
        device_id=to,
        device_id_type=MESH,
    )


def factors(n):
    major = 1
    while major * major < n:
        major *= 2
    return major, n // major


def snake(i):
    return (i // 2) * 2 + (i % 2 + i // 2) % 2


def gather_steps(n):
    major, minor = factors(n)
    return 4 * major + 2 + (2 * major - 1) * 2 * (minor // 2)


def early_rows(depth, minor):
    return depth * EARLY // 32 * 2 if minor == 2 else 0


def run_gather(n, out_ref, depth, send, recv, begun, swapped, between, done, last):
    major, minor = factors(n)
    half = minor // 2
    early = early_rows(depth, minor)
    side = lax.rem(lax.axis_index("table"), 2)
    me = lax.axis_index("table") // 2
    row, place = me // minor, snake(me % minor)
    spot = [0]
    sends = []

    def always(body):
        body()

    def when(condition):
        return always if condition is None else pl.when(condition)

    def on_ring(r, shift):
        return r * minor + snake(lax.rem(place + shift + minor, minor))

    def copy_of(origin, offset, size, to):
        at = pl.ds(pl.multiple_of(origin * depth + offset, 16), size)
        copy = remote(
            out_ref.at[at],
            out_ref.at[at],
            send.at[spot[0]],
            recv.at[spot[0]],
            {"table": to * 2 + side},
        )
        spot[0] += 1
        return copy

    def has(shift):
        return jnp.logical_and(row + shift >= 0, row + shift < major)

    def line_go(step, over, offset, size):
        copies = []
        for way in (1, -1):
            origin = lax.rem(row - way * (step - 1) + major, major)
            to = lax.rem(row + way + major, major)
            column = me % minor if over == 0 else minor - 1 - me % minor
            copy = copy_of(origin * minor + column, offset, size, to * minor + me % minor)
            leaves = jnp.logical_and(has(-way * (step - 1)), has(way))
            pl.when(leaves)(copy.start)
            sends.append((leaves, copy))
            copies.append((has(-way * step), copy))
        return copies

    def ring_go(block, present, step, parts=None):
        if parts is None and step < half:
            parts = ((0, depth), (0, depth))
        elif parts is None:
            size = (depth - early) // 2
            parts = ((0, size), (depth - size, size))
        pair = (
            copy_of(on_ring(block, 1 - step), *parts[0], on_ring(row, 1)),
            copy_of(on_ring(block, step - 1), *parts[1], on_ring(row, -1)),
        )
        for copy in pair:
            when(present)(copy.start)
            sends.append((present, copy))
        return pair

    def start(copy):
        copy.start()
        sends.append((None, copy))
        return copy

    def land(copies):
        for present, copy in copies:
            pl.when(present)(copy.wait_recv)

    blocks = [(row, None)]
    stage = [1]
    low = depth // 2
    flight = line_go(1, 0, side * low, low)
    if early:
        first = [start(copy_of(me, side * low, low, on_ring(row, 1)))]
        begun()
        swapped()
        flight += line_go(1, 0, (1 - side) * low, low)
        first.append(start(copy_of(me, (1 - side) * low, low, on_ring(row, 1))))
        rings = [tuple(first)]
    else:
        begun()
        swapped()
        flight += line_go(1, 0, (1 - side) * low, low)
        rings = [ring_go(row, None, 1)]
    between(0)
    extra = []
    middle = (depth - early) // 2

    def advance(i):
        block, present = blocks[i]
        step = stage[i]
        stage[i] += 1
        for copy in rings[i]:
            when(present)(copy.wait_recv)
        if step < half:
            rings[i] = ring_go(block, present, step + 1)
        else:
            done(block, when(present))

    for step in range(1, major):
        land(flight)
        if step + 1 < major:
            flight = line_go(step + 1, 0, 0, depth)
        known = len(blocks)
        for way in (1, -1):
            block = lax.rem(row - way * step + major, major)
            blocks.append((block, has(-way * step)))
            stage.append(1)
            rings.append(ring_go(*blocks[-1], 1))
        if early:
            if step == 1:
                advance(0)
            land(extra)
            extra = line_go(step, 1, middle, early)
        between(step)
        for i in range(known):
            if stage[i] <= half:
                advance(i)
    land(extra)
    for _ in range(half):
        for i in range(len(blocks)):
            if stage[i] <= half:
                advance(i)
    last()
    return [(when(present), copy) for present, copy in sends]


def rows_of(ref, d, capacity):
    return ref.at[:, piece(d, capacity)]


def slot_marks(slots, first, amount):
    spot = lax.broadcasted_iota(jnp.int32, (amount, slots.shape[1]), 0) + first
    return (spot == slots).astype(jnp.float32).astype(jnp.bfloat16)


def gather_kernel(
    n, w_ref, facts_ref, table_ref, cot_ref, bytes_ref, gain_ref,
    arrived, wanted_ref, proj_ref,
    w_all, tell, table, looked, y_ref, cots, part, beside, own, away, across, half_ref,
    sums, chain, places, full, back_in, ws, wr, qs, qr, xs, xr, zs, zr, ts, ps, pr, cs, cr, gs, gr, ms, mr,
    ds, dr, es, er, ns, nr, local, still, kept,
):
    core = lax.axis_index("mp")
    other = 1 - core
    major, minor = factors(n)
    me = lax.axis_index("table")
    row, place = me // minor, lax.rem(me, minor)
    side = lax.rem(me, 2)
    mate = {"table": me + 1 - 2 * side}
    twin = {"mp": other}
    depth = w_ref.shape[0]
    ngram, rows, width = table_ref.shape
    tokens = cot_ref.shape[0]
    quarter = width // 2
    capacity = looked.shape[1] // n
    plane = minor * capacity
    lines, fast = factors(n // 2)
    each = lines // 2
    span = fast * 2 * depth
    tile = width // 4

    def has(shift):
        return jnp.logical_and(row + shift >= 0, row + shift < major)

    w_swap = remote(
        w_ref.at[:, piece(1 - side, quarter)], w_all.at[piece(me, depth)],
        ps.at[0], pr.at[0], mate,
    )
    c_swap = remote(
        cot_ref.at[:, piece(1 - side, quarter)], cots.at[piece(side, tokens)],
        ps.at[1], pr.at[1], mate,
    )
    keep = (
        pltpu.make_async_copy(
            w_ref.at[:, piece(side, quarter)], w_all.at[piece(me, depth)], local.at[0]
        ),
        pltpu.make_async_copy(
            cot_ref.at[:, piece(side, quarter)], cots.at[piece(side, tokens)], local.at[1]
        ),
    )
    loads = [
        pltpu.make_async_copy(table_ref.at[k], table.at[k], ts.at[k]) for k in range(ngram)
    ]
    questions = []
    for j in range(1, n):
        to = lax.rem(me + j, n)
        questions.append(remote(tell, places.at[me], qs.at[j], qr.at[j], {"table": to}))

    for copy in [keep[0]] + loads + [keep[1]]:
        copy.start()

    def find_slots():
        before_mask = lax.broadcasted_iota(jnp.int32, (tokens, tokens), 0) < lax.broadcasted_iota(
            jnp.int32, (tokens, tokens), 1
        )
        earlier = before_mask.astype(jnp.float32).astype(jnp.bfloat16)
        tell[...] = facts_ref[...]
        for k in range(ngram):
            owners = facts_ref[k : k + 1, :]
            named = (lax.broadcasted_iota(jnp.int32, (n, tokens), 0) == owners).astype(jnp.float32)
            before = jnp.dot(
                named.astype(jnp.bfloat16), earlier, preferred_element_type=jnp.float32
            )
            rank = jnp.sum(before * named, axis=0, keepdims=True).astype(jnp.int32)
            tell[k : k + 1, :] = owners * capacity + rank
        places[me] = tell[...]

    greet_all(n, find_slots)
    w_swap.start()
    for copy in questions:
        copy.start()
    c_swap.start()

    def plane_copies(d):
        copies = []
        for j in range(1, minor):
            to = lax.rem(place + j, minor)
            copies.append(
                remote(
                    rows_of(looked, d * minor + to, capacity),
                    rows_of(y_ref, d * minor + place, capacity),
                    xs.at[d * minor + j], xr.at[d * minor + j], {"table": row * minor + to},
                )
            )
        return copies

    def stay(d):
        return pltpu.make_async_copy(
            rows_of(looked, d * minor + place, capacity),
            rows_of(y_ref, d * minor + place, capacity),
            still.at[d],
        )

    ends = [(d, way) for d in range(major - 1, 0, -1) for way in (1, -1)]

    def target(d, way):
        return lax.rem(row + way * d + major, major)

    def plane_go(d):
        for copy in plane_copies(d) + [stay(d)]:
            copy.start()

    group = 128 // capacity

    def find_rows():
        for copy in questions:
            copy.wait_recv()
        ours = lax.broadcasted_iota(jnp.int32, (capacity, tokens), 0) + me * capacity
        spots = lax.broadcasted_iota(jnp.int32, (128, rows), 1).astype(jnp.float32) + 1.0
        down = lax.broadcasted_iota(jnp.int32, (128, 128), 0)
        same = down == lax.broadcasted_iota(jnp.int32, (128, 128), 1)
        for k in range(ngram):
            for q in range(n // group):
                wanted = []
                for d in range(q * group, (q + 1) * group):
                    offsets = places[d, ngram + k : ngram + k + 1, :].astype(jnp.float32) + 1.0
                    named = ours == places[d, k : k + 1, :]
                    wanted.append(
                        jnp.sum(jnp.where(named, offsets, 0.0), axis=1, keepdims=True)
                    )
                wanted = jnp.concatenate(wanted, axis=0)
                wanted_ref[k : k + 1, q * 128 : (q + 1) * 128] = jnp.sum(
                    jnp.where(same, wanted, 0.0), axis=0, keepdims=True
                )
                full[q * 128 : (q + 1) * 128, k * rows : (k + 1) * rows] = (
                    (spots == wanted).astype(jnp.float32).astype(jnp.bfloat16)
                )

    def look_up():
        for load in loads:
            load.wait()
        for k in range(ngram):
            @pl.loop(0, 8)
            def _(c):
                columns = piece(c, width // 8)
                looked[k, :, columns] = jnp.dot(
                    full[:, k * rows : (k + 1) * rows],
                    table[k, :, columns],
                    preferred_element_type=jnp.float32,
                ).astype(looked.dtype)

    def arrive(d):
        for copy in plane_copies(d):
            copy.wait_recv()
        stay(d).wait()

    def part_of(d, columns):
        total = None
        for k in range(ngram):
            mark = slot_marks(places[d * minor + place, k : k + 1, :], row * plane, plane)
            term = lax.dot_general(
                mark,
                y_ref[k, piece(d, plane), columns],
                (((0,), (0,)), ((), ())),
                preferred_element_type=jnp.float32,
            )
            total = term if total is None else total + term
        return total

    def chain_copy(d, way):
        to = lax.rem(row + way + major, major) * minor + place
        spot = (d - 1) * 2 + (0 if way == 1 else 1)
        land = major if d == 1 and way == -1 else target(d, way)
        return remote(
            chain.at[target(d, way)], chain.at[land], zs.at[spot], zr.at[spot], {"table": to}
        )

    def hop(d, way):
        @pl.when(has(way * d))
        def _():
            end = target(d, way)
            arrive(end)

            @pl.when(has(-way))
            def _():
                if d < major - 1:
                    chain_copy(d + 1, way).wait_recv()

            @pl.loop(0, 4)
            def _(c):
                columns = piece(c, tile)
                total = part_of(end, columns) + chain[end, :, columns].astype(jnp.float32)
                chain[end, :, columns] = total.astype(chain.dtype)

            chain_copy(d, way).start()

    def hand_out(d):
        if d == 0:
            plane_go(row)
        else:
            for way in (1, -1):
                pl.when(has(way * d))(functools.partial(plane_go, target(d, way)))

    def between(i):
        if i == 0:
            look_up()
            hand_out(major - 1)
            for way in (1, -1):
                @pl.when(jnp.logical_not(has(-way)))
                def _():
                    for d in range(0, major):
                        land = major if d == 0 and way == -1 else target(d, way)
                        chain[land] = jnp.zeros(chain.shape[1:], chain.dtype)

            c_swap.wait_recv()
            keep[1].wait()
        else:
            for way in (1, -1):
                hop(major - i, way)
            hand_out(major - 1 - i)

    totals = remote(sums.at[0], sums.at[1], ms.at[0], mr.at[0], twin)
    inners = remote(sums.at[2], sums.at[3], ms.at[1], mr.at[1], twin)

    def embed():
        arrive(row)
        for way in (1, -1):
            pl.when(has(-way))(chain_copy(1, way).wait_recv)
        sums[0] = jnp.zeros(sums.shape[1:], jnp.float32)
        picks = slot_marks(facts_ref[2 * ngram : 2 * ngram + 1, :], 0, bytes_ref.shape[0])

        @pl.loop(0, 4)
        def _(c):
            columns = piece(c, tile)
            total = lax.dot_general(
                picks,
                bytes_ref[:, columns],
                (((0,), (0,)), ((), ())),
                preferred_element_type=jnp.float32,
            )
            total = total + part_of(row, columns)
            total = total + chain[row, :, columns].astype(jnp.float32)
            total = total + chain[major, :, columns].astype(jnp.float32)
            rounded = total.astype(half_ref.dtype)
            half_ref[:, columns] = rounded
            values = rounded.astype(jnp.float32)
            sums[0] += jnp.broadcast_to(
                jnp.sum(values * values, axis=1, keepdims=True), sums.shape[1:]
            )

        totals.start()

    chunk = min(512, span)

    pieces = span // chunk

    def to_twin(block, c):
        spot = lax.rem(block, each)
        return remote(
            part.at[:, pl.ds(pl.multiple_of(block * span + c * chunk, chunk), chunk)],
            beside.at[:, pl.ds(pl.multiple_of(spot * span + c * chunk, chunk), chunk)],
            cs.at[spot * pieces + c],
            cr.at[spot * pieces + c],
            twin,
        )

    def to_mate(spot, c):
        at = pl.ds(pl.multiple_of(spot * span + c * chunk, chunk), chunk)
        i = spot * pieces + c
        return remote(away.at[:, at], across.at[:, at], gs.at[i], gr.at[i], mate)

    def finish(block):
        spot = lax.rem(block, each)
        theirs, ours = piece(1 - side, tokens), piece(side, tokens)

        @pl.when(block // each == core)
        def _():
            for c in range(pieces):
                to_twin(block, c).wait_recv()
                come = pl.ds(pl.multiple_of(block * span + c * chunk, chunk), chunk)
                go = pl.ds(pl.multiple_of(spot * span + c * chunk, chunk), chunk)
                away[:, go] = (part[theirs, come] + beside[theirs, go]).astype(away.dtype)
                to_mate(spot, c).start()
            for c in range(pieces):
                come = pl.ds(pl.multiple_of(block * span + c * chunk, chunk), chunk)
                go = pl.ds(pl.multiple_of(spot * span + c * chunk, chunk), chunk)
                own[:, go] = part[ours, come] + beside[ours, go]

    waiting = []

    def done(block, when):
        @when
        def _():
            for c in range(pieces):
                some = pl.ds(pl.multiple_of(block * span + c * chunk, chunk), chunk)
                part[:, some] = lax.dot_general(
                    cots[...],
                    w_all[some, :],
                    (((1,), (1,)), ((), ())),
                    preferred_element_type=jnp.float32,
                )
                pl.when(block // each == other)(to_twin(block, c).start)

        waiting.append((block, when))
        if len(waiting) > 1:
            settle()

    def settle():
        block, when = waiting.pop(0)
        when(functools.partial(finish, block))

    keep[0].wait()
    started = run_gather(
        n // 2, w_all, 2 * depth, ws, wr, find_rows, w_swap.wait_recv, between, done, embed
    )
    while waiting:
        settle()

    totals.wait_recv()
    full_width = 2 * width
    sums[4] = lax.rsqrt((sums[0] + sums[1]) / full_width + eps)

    def block_of(whose):
        return full.at[piece(whose, tokens), piece(core, width)]

    swap = remote(block_of(side), block_of(side), ns.at[0], nr.at[0], mate)
    lend = remote(block_of(side), block_of(side), ns.at[1], nr.at[1], twin)
    pass_on = remote(block_of(1 - side), block_of(1 - side), ns.at[2], nr.at[2], twin)
    back = remote(away.at[:, :quarter], back_in, ns.at[3], nr.at[3], mate)

    def gain_of(c):
        return gain_ref[:, pl.ds(pl.multiple_of(core * width + c * tile, tile), tile)]

    @pl.loop(0, 4)
    def _(c):
        values = half_ref[:, piece(c, tile)].astype(jnp.float32)
        there = pl.ds(pl.multiple_of(core * width + c * tile, tile), tile)
        full[piece(side, tokens), there] = (values * sums[4][:, :1] * gain_of(c)).astype(
            full.dtype
        )

    swap.start()
    lend.start()
    sums[2] = jnp.zeros(sums.shape[1:], jnp.float32)
    for spot in range(each):
        for c in range(pieces):
            to_mate(spot, c).wait_recv()

    @pl.loop(0, 4)
    def _(c):
        columns = piece(c, tile)
        scaled = (own[:, columns] + across[:, columns].astype(jnp.float32)) * gain_of(c)
        own[:, columns] = scaled
        values = half_ref[:, columns].astype(jnp.float32)
        sums[2] += jnp.broadcast_to(
            jnp.sum(values * scaled, axis=1, keepdims=True), sums.shape[1:]
        )

    inners.start()
    for d in range(major):
        for copy in plane_copies(d):
            copy.wait_send()
    inners.wait_recv()

    per = rows // tokens
    broad = width // 2

    def line_of(origin, h):
        return table.at[origin // per, piece(lax.rem(origin, per), tokens), piece(h, broad)]

    def line_copy(step, way, h):
        origin = lax.rem(row - way * (step - 1) + major, major)
        to = lax.rem(row + way + major, major) * minor + place
        spot = ((step - 1) * 2 + (0 if way == 1 else 1)) * 2 + h
        here = line_of(origin, h)
        return remote(here, here, ds.at[spot], dr.at[spot], {"table": to})

    def leaves(step, way):
        return jnp.logical_and(has(-way * (step - 1)), has(way))

    def give_copies(i, origin, h):
        copies = []
        for j in range(1, minor):
            to = lax.rem(place + j, minor)
            spot = (i * minor + j) * 2 + h
            copies.append(
                remote(
                    looked.at[:, piece(origin * minor + to, capacity), piece(h, broad)],
                    arrived.at[:, piece(origin * minor + place, capacity), piece(h, broad)],
                    es.at[spot], er.at[spot], {"table": row * minor + to},
                )
            )
        return copies

    def keep_own(origin, h):
        at = piece(origin * minor + place, capacity)
        return pltpu.make_async_copy(
            looked.at[:, at, piece(h, broad)],
            arrived.at[:, at, piece(h, broad)],
            kept.at[origin * 2 + h],
        )

    def give(i, origin, h):
        for k in range(ngram):
            mark = slot_marks(
                places[origin * minor + place, k : k + 1, :], row * plane, plane
            )
            looked[k, piece(origin, plane), h * broad : (h + 1) * broad] = jnp.dot(
                mark,
                table[
                    origin // per,
                    piece(lax.rem(origin, per), tokens),
                    h * broad : (h + 1) * broad,
                ],
                preferred_element_type=jnp.float32,
            ).astype(looked.dtype)
        for copy in give_copies(i, origin, h) + [keep_own(origin, h)]:
            copy.start()

    for h in range(2):
        @pl.loop(0, 2)
        def _(c):
            columns = pl.ds(pl.multiple_of(h * broad + c * tile, tile), tile)
            scale = sums[4][:, :1]
            inner = (sums[2][:, :1] + sums[3][:, :1]) / full_width
            values = half_ref[:, columns].astype(jnp.float32)
            table[row // per, piece(lax.rem(row, per), tokens), columns] = (
                scale * own[:, columns] - values * scale * scale * scale * inner
            ).astype(table.dtype)

        for way in (1, -1):
            pl.when(leaves(1, way))(line_copy(1, way, h).start)

    step_of = min(256, quarter)

    def project(whose, out):
        @pl.loop(0, quarter // step_of)
        def _(c):
            columns = piece(c, step_of)
            out(
                c,
                jnp.dot(
                    full[piece(whose, tokens), :],
                    w_all[:, columns],
                    preferred_element_type=jnp.float32,
                ),
            )

    def put_away(c, values):
        away[:, piece(c, step_of)] = values.astype(away.dtype)

    def put_own(c, values):
        there = pl.ds(pl.multiple_of(side * quarter + c * step_of, step_of), step_of)
        proj_ref[:, there] = values.astype(proj_ref.dtype)

    def project_away():
        lend.wait_recv()
        pass_on.wait_recv()
        for spot in range(each):
            for c in range(pieces):
                to_mate(spot, c).wait_send()
        project(1 - side, put_away)
        back.start()

    for h in range(2):
        give(0, row, h)
    swap.wait_recv()
    pass_on.start()
    blocks = [(0, row, None)]
    for s in range(1, major):
        new = []
        for way in (1, -1):
            new.append((len(blocks), lax.rem(row - way * s + major, major), has(-way * s)))
            blocks.append(new[-1])
        for h in range(2):
            for way in (1, -1):
                pl.when(has(-way * s))(line_copy(s, way, h).wait_recv)
                if s + 1 < major:
                    pl.when(leaves(s + 1, way))(line_copy(s + 1, way, h).start)
            for i, origin, present in new:
                pl.when(present)(functools.partial(give, i, origin, h))
        if s == 1:
            project_away()
        if s == min(2, major - 1):
            project(side, put_own)

    back.wait_recv()
    proj_ref[:, piece(1 - side, quarter)] = back_in[...]
    for i, origin, present in blocks:

        def end():
            for h in range(2):
                for copy in give_copies(i, origin, h):
                    copy.wait_recv()
                    copy.wait_send()
                keep_own(origin, h).wait()

        if present is None:
            end()
        else:
            pl.when(present)(end)
    for copy in questions + [w_swap, c_swap, totals, inners, swap, lend, pass_on, back]:
        copy.wait_send()
    for d, way in ends:
        pl.when(has(way * d))(chain_copy(d, way).wait_send)
    for spot in range(each):
        for c in range(pieces):
            to_twin(other * each + spot, c).wait_send()
    for when, copy in started:
        when(copy.wait_send)
    for s in range(1, major):
        for way in (1, -1):
            for h in range(2):
                pl.when(leaves(s, way))(line_copy(s, way, h).wait_send)


def gather_and_exchange(w, facts, table, cot, codes, gain, capacity, n):
    steps = gather_steps(n // 2)
    lines = factors(n // 2)[0]
    major, minor = factors(n)
    ngram, _, width = table.shape
    levels = -(-ngram // 8) * 8
    span = n * w.shape[0] // lines
    pieces = lines // 2 * (span // min(512, span))
    tokens = cot.shape[0]
    depth = w.shape[0]
    half = (tokens, width)
    f32, bf16 = jnp.float32, jnp.bfloat16
    dma = pltpu.SemaphoreType.DMA
    return pl.pallas_call(
        functools.partial(gather_kernel, n),
        out_shape=(
            jax.ShapeDtypeStruct((ngram, n * capacity, width), bf16),
            jax.ShapeDtypeStruct((levels, n * capacity), f32),
            jax.ShapeDtypeStruct(half, bf16),
        ),
        in_specs=[ANY, WHOLE, ANY, ANY, WHOLE, WHOLE],
        out_specs=(ANY, WHOLE, WHOLE),
        scratch_shapes=[
            pltpu.VMEM((n * depth, width // 2), w.dtype),
            pltpu.VMEM(facts.shape, facts.dtype),
            pltpu.VMEM(table.shape, table.dtype),
            pltpu.VMEM((ngram, n * capacity, width), table.dtype),
            pltpu.VMEM((ngram, n * capacity, width), table.dtype),
            pltpu.VMEM((2 * tokens, width // 2), cot.dtype),
            pltpu.VMEM((2 * tokens, n * depth), f32),
            pltpu.VMEM((2 * tokens, width), f32),
            pltpu.VMEM(half, f32),
            pltpu.VMEM(half, bf16),
            pltpu.VMEM(half, bf16),
            pltpu.VMEM(half, bf16),
            pltpu.VMEM((5, tokens, 128), f32),
            pltpu.VMEM((major + 1, *half), bf16),
            pltpu.VMEM((n, *facts.shape), facts.dtype),
            pltpu.VMEM((2 * tokens, 2 * width), bf16),
            pltpu.VMEM((tokens, width // 2), bf16),
            dma((steps,)),
            dma((steps,)),
            dma((n,)),
            dma((n,)),
            dma((n,)),
            dma((n,)),
            dma((2 * (major - 1),)),
            dma((2 * (major - 1),)),
            dma((ngram,)),
            dma((2,)),
            dma((2,)),
            dma((pieces,)),
            dma((pieces,)),
            dma((pieces,)),
            dma((pieces,)),
            dma((2,)),
            dma((2,)),
            dma((4 * (major - 1),)),
            dma((4 * (major - 1),)),
            dma((2 * (2 * major - 1) * minor,)),
            dma((2 * (2 * major - 1) * minor,)),
            dma((4,)),
            dma((4,)),
            dma((2,)),
            dma((major,)),
            dma((2 * major,)),
        ],
        compiler_params=pltpu.CompilerParams(
            collective_id=1, has_side_effects=True, vmem_limit_bytes=VMEM_LIMIT
        ),
    )(w, facts, table, cot, codes, gain)


def sum_kernel(wanted_ref, arrived_ref, out_ref, hits):
    k = pl.program_id(0)
    rows, slots = hits.shape

    @pl.when(pl.program_id(1) == 0)
    def _():
        spots = lax.broadcasted_iota(jnp.int32, (rows, slots), 0).astype(jnp.float32) + 1.0
        wanted = wanted_ref[pl.ds(k, 1), :]
        hits[...] = (spots == wanted).astype(jnp.float32).astype(hits.dtype)

    out_ref[0] = jnp.dot(
        hits[...], arrived_ref[0], preferred_element_type=jnp.float32
    ).astype(out_ref.dtype)


def sum_rows(wanted, arrived, rows):
    ngram, slots, width = arrived.shape
    tile = min(1024, width)
    return pl.pallas_call(
        sum_kernel,
        grid=(ngram, width // tile),
        out_shape=jax.ShapeDtypeStruct((ngram, rows, width), arrived.dtype),
        in_specs=[
            pl.BlockSpec(wanted.shape, lambda k, c: (0, 0)),
            pl.BlockSpec((1, slots, tile), lambda k, c: (k, 0, c)),
        ],
        out_specs=pl.BlockSpec((1, rows, tile), lambda k, c: (k, 0, c)),
        scratch_shapes=[pltpu.VMEM((rows, slots), jnp.bfloat16)],
        compiler_params=pltpu.CompilerParams(vmem_limit_bytes=VMEM_LIMIT),
    )(wanted, arrived)


def on_device(
    hash_tables, byte_table, byte_ids, hash_owner, hash_offset, gain, proj_weight, cotangent
):
    groups = lax.axis_size("table")
    ngram, rows_dev, _ = hash_tables.shape
    tokens = byte_ids.shape[0]
    capacity = 2 * tokens // groups
    facts = jnp.concatenate([hash_owner[:, :, 0], hash_offset, byte_ids[None, :]], axis=0)
    levels = -(-facts.shape[0] // 8) * 8
    facts = jnp.pad(facts, ((0, levels - facts.shape[0]), (0, 0)))
    arrived, wanted, projected = gather_and_exchange(
        proj_weight, facts, hash_tables, cotangent, byte_table, gain[None, :], capacity, groups
    )
    return (projected, sum_rows(wanted, arrived, rows_dev))


def solution(mesh):
    return jax.shard_map(
        on_device,
        mesh=mesh,
        in_specs=(
            P(None, "table", "mp"),
            P(None, "mp"),
            P("table"),
            P(None, "table", None),
            P(None, "table"),
            P(),
            P("table", "mp"),
            P("table", "mp"),
        ),
        out_specs=(P("table", "mp"), P(None, "table", "mp")),
        check_vma=False,
    )
```

```python
import functools

import jax
import jax.numpy as jnp
from jax import lax
from jax.experimental import pallas as pl
from jax.experimental.pallas import tpu as pltpu
from jax.sharding import PartitionSpec as P

eps = 1e-05
MESH = pl.DeviceIdType.MESH
ANY = pl.BlockSpec(memory_space=pl.ANY)
WHOLE = pl.BlockSpec(memory_space=pltpu.VMEM)
VMEM_LIMIT = 61 * 2**20
EARLY = 6
CUTS = 2


def piece(i, size):
    return pl.ds(pl.multiple_of(i * size, size), size)


def greet_all(n, meanwhile=None):
    me = lax.axis_index("table")
    other = 1 - lax.axis_index("mp")
    barrier = pltpu.get_barrier_semaphore()
    for j in range(1, n):
        pl.semaphore_signal(
            barrier, inc=1, device_id={"table": lax.rem(me + j, n)}, device_id_type=MESH
        )
    pl.semaphore_signal(barrier, inc=1, device_id={"mp": other}, device_id_type=MESH)
    if meanwhile is not None:
        meanwhile()
    pl.semaphore_wait(barrier, n)
    return other


def remote(src, dst, send, recv, to):
    return pltpu.make_async_remote_copy(
        src_ref=src,
        dst_ref=dst,
        send_sem=send,
        recv_sem=recv,
        device_id=to,
        device_id_type=MESH,
    )


def factors(n):
    major = 1
    while major * major < n:
        major *= 2
    return major, n // major


def snake(i):
    return (i // 2) * 2 + (i % 2 + i // 2) % 2


def gather_steps(n):
    major, minor = factors(n)
    return 4 * major + 2 + (2 * major - 1) * 2 * (minor // 2)


def early_rows(depth, minor):
    return depth * EARLY // 32 * 2 if minor == 2 else 0


def run_gather(n, out_ref, depth, send, recv, begun, swapped, between, done, last):
    major, minor = factors(n)
    half = minor // 2
    early = early_rows(depth, minor)
    side = lax.rem(lax.axis_index("table"), 2)
    me = lax.axis_index("table") // 2
    row, place = me // minor, snake(me % minor)
    spot = [0]
    sends = []

    def always(body):
        body()

    def when(condition):
        return always if condition is None else pl.when(condition)

    def on_ring(r, shift):
        return r * minor + snake(lax.rem(place + shift + minor, minor))

    def copy_of(origin, offset, size, to):
        at = pl.ds(pl.multiple_of(origin * depth + offset, 16), size)
        copy = remote(
            out_ref.at[at],
            out_ref.at[at],
            send.at[spot[0]],
            recv.at[spot[0]],
            {"table": to * 2 + side},
        )
        spot[0] += 1
        return copy

    def has(shift):
        return jnp.logical_and(row + shift >= 0, row + shift < major)

    def line_go(step, over, offset, size):
        copies = []
        for way in (1, -1):
            origin = lax.rem(row - way * (step - 1) + major, major)
            to = lax.rem(row + way + major, major)
            column = me % minor if over == 0 else minor - 1 - me % minor
            copy = copy_of(origin * minor + column, offset, size, to * minor + me % minor)
            leaves = jnp.logical_and(has(-way * (step - 1)), has(way))
            pl.when(leaves)(copy.start)
            sends.append((leaves, copy))
            copies.append((has(-way * step), copy))
        return copies

    def ring_go(block, present, step, parts=None):
        if parts is None and step < half:
            parts = ((0, depth), (0, depth))
        elif parts is None:
            size = (depth - early) // 2
            parts = ((0, size), (depth - size, size))
        pair = (
            copy_of(on_ring(block, 1 - step), *parts[0], on_ring(row, 1)),
            copy_of(on_ring(block, step - 1), *parts[1], on_ring(row, -1)),
        )
        for copy in pair:
            when(present)(copy.start)
            sends.append((present, copy))
        return pair

    def start(copy):
        copy.start()
        sends.append((None, copy))
        return copy

    def land(copies):
        for present, copy in copies:
            pl.when(present)(copy.wait_recv)

    blocks = [(row, None)]
    stage = [1]
    low = depth // 2
    flight = line_go(1, 0, side * low, low)
    if early:
        first = [start(copy_of(me, side * low, low, on_ring(row, 1)))]
        begun()
        swapped()
        flight += line_go(1, 0, (1 - side) * low, low)
        first.append(start(copy_of(me, (1 - side) * low, low, on_ring(row, 1))))
        rings = [tuple(first)]
    else:
        begun()
        swapped()
        flight += line_go(1, 0, (1 - side) * low, low)
        rings = [ring_go(row, None, 1)]
    between(0)
    extra = []
    middle = (depth - early) // 2

    def advance(i):
        block, present = blocks[i]
        step = stage[i]
        stage[i] += 1
        for copy in rings[i]:
            when(present)(copy.wait_recv)
        if step < half:
            rings[i] = ring_go(block, present, step + 1)
        else:
            done(block, when(present))

    for step in range(1, major):
        land(flight)
        if step + 1 < major:
            flight = line_go(step + 1, 0, 0, depth)
        known = len(blocks)
        for way in (1, -1):
            block = lax.rem(row - way * step + major, major)
            blocks.append((block, has(-way * step)))
            stage.append(1)
            rings.append(ring_go(*blocks[-1], 1))
        if early:
            if step == 1:
                advance(0)
            land(extra)
            extra = line_go(step, 1, middle, early)
        between(step)
        for i in range(known):
            if stage[i] <= half:
                advance(i)
    land(extra)
    for _ in range(half):
        for i in range(len(blocks)):
            if stage[i] <= half:
                advance(i)
    last()
    return [(when(present), copy) for present, copy in sends]


def rows_of(ref, d, capacity):
    return ref.at[:, piece(d, capacity)]


def slot_marks(slots, first, amount):
    spot = lax.broadcasted_iota(jnp.int32, (amount, slots.shape[1]), 0) + first
    return (spot == slots).astype(jnp.float32).astype(jnp.bfloat16)


def gather_kernel(
    n, w_ref, facts_ref, table_ref, cot_ref, bytes_ref, gain_ref,
    arrived, wanted_ref, proj_ref,
    w_all, tell, table, looked, y_ref, cots, part, beside, own, away, across, half_ref,
    sums, chain, places, full, back_in, ws, wr, qs, qr, xs, xr, zs, zr, ts, ps, pr, cs, cr, gs, gr, ms, mr,
    ds, dr, es, er, ns, nr, local, still, kept,
):
    core = lax.axis_index("mp")
    other = 1 - core
    major, minor = factors(n)
    me = lax.axis_index("table")
    row, place = me // minor, lax.rem(me, minor)
    side = lax.rem(me, 2)
    mate = {"table": me + 1 - 2 * side}
    twin = {"mp": other}
    depth = w_ref.shape[0]
    ngram, rows, width = table_ref.shape
    tokens = cot_ref.shape[0]
    quarter = width // 2
    capacity = looked.shape[1] // n
    plane = minor * capacity
    lines, fast = factors(n // 2)
    each = lines // 2
    span = fast * 2 * depth
    tile = width // 4

    def has(shift):
        return jnp.logical_and(row + shift >= 0, row + shift < major)

    w_swap = remote(
        w_ref.at[:, piece(1 - side, quarter)], w_all.at[piece(me, depth)],
        ps.at[0], pr.at[0], mate,
    )
    c_swap = remote(
        cot_ref.at[:, piece(1 - side, quarter)], cots.at[piece(side, tokens)],
        ps.at[1], pr.at[1], mate,
    )
    keep = (
        pltpu.make_async_copy(
            w_ref.at[:, piece(side, quarter)], w_all.at[piece(me, depth)], local.at[0]
        ),
        pltpu.make_async_copy(
            cot_ref.at[:, piece(side, quarter)], cots.at[piece(side, tokens)], local.at[1]
        ),
    )
    loads = [
        pltpu.make_async_copy(table_ref.at[k], table.at[k], ts.at[k]) for k in range(ngram)
    ]
    questions = []
    for j in range(1, n):
        to = lax.rem(me + j, n)
        questions.append(remote(tell, places.at[me], qs.at[j], qr.at[j], {"table": to}))

    for copy in [keep[0]] + loads + [keep[1]]:
        copy.start()

    def find_slots():
        before_mask = lax.broadcasted_iota(jnp.int32, (tokens, tokens), 0) < lax.broadcasted_iota(
            jnp.int32, (tokens, tokens), 1
        )
        earlier = before_mask.astype(jnp.float32).astype(jnp.bfloat16)
        tell[...] = facts_ref[...]
        for k in range(ngram):
            owners = facts_ref[k : k + 1, :]
            named = (lax.broadcasted_iota(jnp.int32, (n, tokens), 0) == owners).astype(jnp.float32)
            before = jnp.dot(
                named.astype(jnp.bfloat16), earlier, preferred_element_type=jnp.float32
            )
            rank = jnp.sum(before * named, axis=0, keepdims=True).astype(jnp.int32)
            tell[k : k + 1, :] = owners * capacity + rank
        places[me] = tell[...]

    greet_all(n, find_slots)
    w_swap.start()
    for copy in questions:
        copy.start()
    c_swap.start()

    def plane_copies(d):
        copies = []
        for j in range(1, minor):
            to = lax.rem(place + j, minor)
            copies.append(
                remote(
                    rows_of(looked, d * minor + to, capacity),
                    rows_of(y_ref, d * minor + place, capacity),
                    xs.at[d * minor + j], xr.at[d * minor + j], {"table": row * minor + to},
                )
            )
        return copies

    def stay(d):
        return pltpu.make_async_copy(
            rows_of(looked, d * minor + place, capacity),
            rows_of(y_ref, d * minor + place, capacity),
            still.at[d],
        )

    ends = [(d, way) for d in range(major - 1, 0, -1) for way in (1, -1)]

    def target(d, way):
        return lax.rem(row + way * d + major, major)

    def plane_go(d):
        for copy in plane_copies(d) + [stay(d)]:
            copy.start()

    group = 128 // capacity

    def find_rows():
        for copy in questions:
            copy.wait_recv()
        ours = lax.broadcasted_iota(jnp.int32, (capacity, tokens), 0) + me * capacity
        spots = lax.broadcasted_iota(jnp.int32, (128, rows), 1).astype(jnp.float32) + 1.0
        down = lax.broadcasted_iota(jnp.int32, (128, 128), 0)
        same = down == lax.broadcasted_iota(jnp.int32, (128, 128), 1)
        for k in range(ngram):
            for q in range(n // group):
                wanted = []
                for d in range(q * group, (q + 1) * group):
                    offsets = places[d, ngram + k : ngram + k + 1, :].astype(jnp.float32) + 1.0
                    named = ours == places[d, k : k + 1, :]
                    wanted.append(
                        jnp.sum(jnp.where(named, offsets, 0.0), axis=1, keepdims=True)
                    )
                wanted = jnp.concatenate(wanted, axis=0)
                wanted_ref[k : k + 1, q * 128 : (q + 1) * 128] = jnp.sum(
                    jnp.where(same, wanted, 0.0), axis=0, keepdims=True
                )
                full[q * 128 : (q + 1) * 128, k * rows : (k + 1) * rows] = (
                    (spots == wanted).astype(jnp.float32).astype(jnp.bfloat16)
                )

    def look_up():
        for load in loads:
            load.wait()
        for k in range(ngram):
            @pl.loop(0, 8)
            def _(c):
                columns = piece(c, width // 8)
                looked[k, :, columns] = jnp.dot(
                    full[:, k * rows : (k + 1) * rows],
                    table[k, :, columns],
                    preferred_element_type=jnp.float32,
                ).astype(looked.dtype)

    def arrive(d):
        for copy in plane_copies(d):
            copy.wait_recv()
        stay(d).wait()

    def part_of(d, columns):
        total = None
        for k in range(ngram):
            mark = slot_marks(places[d * minor + place, k : k + 1, :], row * plane, plane)
            term = lax.dot_general(
                mark,
                y_ref[k, piece(d, plane), columns],
                (((0,), (0,)), ((), ())),
                preferred_element_type=jnp.float32,
            )
            total = term if total is None else total + term
        return total

    def chain_copy(d, way, h):
        to = lax.rem(row + way + major, major) * minor + place
        spot = ((d - 1) * 2 + (0 if way == 1 else 1)) * CUTS + h
        land = major if d == 1 and way == -1 else target(d, way)
        columns = piece(h, width // CUTS)
        return remote(
            chain.at[target(d, way), :, columns], chain.at[land, :, columns],
            zs.at[spot], zr.at[spot], {"table": to},
        )

    def hop(d, way, among=None):
        goes = has(way * d)

        @pl.when(goes if among is None else jnp.logical_and(goes, among))
        def _():
            end = target(d, way)
            arrive(end)

            for h in range(CUTS):
                if d < major - 1:
                    pl.when(has(-way))(chain_copy(d + 1, way, h).wait_recv)

                @pl.loop(h * 4 // CUTS, (h + 1) * 4 // CUTS)
                def _(c):
                    columns = piece(c, tile)
                    total = part_of(end, columns) + chain[end, :, columns].astype(jnp.float32)
                    chain[end, :, columns] = total.astype(chain.dtype)

                chain_copy(d, way, h).start()

    def hand_out(d):
        if d == 0:
            plane_go(row)
        else:
            for way in (1, -1):
                pl.when(has(way * d))(functools.partial(plane_go, target(d, way)))

    def between(i):
        if i == 0:
            look_up()
            hand_out(major - 1)
            hand_out(major - 2)
            for way in (1, -1):
                @pl.when(jnp.logical_not(has(-way)))
                def _():
                    for d in range(0, major):
                        land = major if d == 0 and way == -1 else target(d, way)
                        chain[land] = jnp.zeros(chain.shape[1:], chain.dtype)

            c_swap.wait_recv()
            keep[1].wait()
        else:
            for way in (1, -1):
                head = jnp.logical_not(has(-way))
                if i == 1:
                    hop(major - 1, way)
                else:
                    hop(major - i, way, has(-way))
                if i < major - 1:
                    hop(major - 1 - i, way, head)
            if i < major - 1:
                hand_out(major - 2 - i)

    totals = remote(sums.at[0], sums.at[1], ms.at[0], mr.at[0], twin)
    inners = remote(sums.at[2], sums.at[3], ms.at[1], mr.at[1], twin)

    def embed():
        arrive(row)
        sums[0] = jnp.zeros(sums.shape[1:], jnp.float32)
        picks = slot_marks(facts_ref[2 * ngram : 2 * ngram + 1, :], 0, bytes_ref.shape[0])
        for h in range(CUTS):
            for way in (1, -1):
                pl.when(has(-way))(chain_copy(1, way, h).wait_recv)

            @pl.loop(h * 4 // CUTS, (h + 1) * 4 // CUTS)
            def _(c):
                columns = piece(c, tile)
                total = lax.dot_general(
                    picks,
                    bytes_ref[:, columns],
                    (((0,), (0,)), ((), ())),
                    preferred_element_type=jnp.float32,
                )
                total = total + part_of(row, columns)
                total = total + chain[row, :, columns].astype(jnp.float32)
                total = total + chain[major, :, columns].astype(jnp.float32)
                rounded = total.astype(half_ref.dtype)
                half_ref[:, columns] = rounded
                values = rounded.astype(jnp.float32)
                sums[0] += jnp.broadcast_to(
                    jnp.sum(values * values, axis=1, keepdims=True), sums.shape[1:]
                )

        totals.start()

    chunk = min(512, span)

    pieces = span // chunk

    def to_twin(block, c):
        spot = lax.rem(block, each)
        return remote(
            part.at[:, pl.ds(pl.multiple_of(block * span + c * chunk, chunk), chunk)],
            beside.at[:, pl.ds(pl.multiple_of(spot * span + c * chunk, chunk), chunk)],
            cs.at[spot * pieces + c],
            cr.at[spot * pieces + c],
            twin,
        )

    def to_mate(spot, c):
        at = pl.ds(pl.multiple_of(spot * span + c * chunk, chunk), chunk)
        i = spot * pieces + c
        return remote(away.at[:, at], across.at[:, at], gs.at[i], gr.at[i], mate)

    def finish(block):
        spot = lax.rem(block, each)
        theirs, ours = piece(1 - side, tokens), piece(side, tokens)

        @pl.when(block // each == core)
        def _():
            for c in range(pieces):
                to_twin(block, c).wait_recv()
                come = pl.ds(pl.multiple_of(block * span + c * chunk, chunk), chunk)
                go = pl.ds(pl.multiple_of(spot * span + c * chunk, chunk), chunk)
                away[:, go] = (part[theirs, come] + beside[theirs, go]).astype(away.dtype)
                to_mate(spot, c).start()
            for c in range(pieces):
                come = pl.ds(pl.multiple_of(block * span + c * chunk, chunk), chunk)
                go = pl.ds(pl.multiple_of(spot * span + c * chunk, chunk), chunk)
                own[:, go] = part[ours, come] + beside[ours, go]

    waiting = []

    def done(block, when):
        @when
        def _():
            for c in range(pieces):
                some = pl.ds(pl.multiple_of(block * span + c * chunk, chunk), chunk)
                part[:, some] = lax.dot_general(
                    cots[...],
                    w_all[some, :],
                    (((1,), (1,)), ((), ())),
                    preferred_element_type=jnp.float32,
                )
                pl.when(block // each == other)(to_twin(block, c).start)

        waiting.append((block, when))
        if len(waiting) > 1:
            settle()

    def settle():
        block, when = waiting.pop(0)
        when(functools.partial(finish, block))

    keep[0].wait()
    started = run_gather(
        n // 2, w_all, 2 * depth, ws, wr, find_rows, w_swap.wait_recv, between, done, embed
    )
    while waiting:
        settle()

    totals.wait_recv()
    full_width = 2 * width
    sums[4] = lax.rsqrt((sums[0] + sums[1]) / full_width + eps)

    def block_of(whose):
        return full.at[piece(whose, tokens), piece(core, width)]

    swap = remote(block_of(side), block_of(side), ns.at[0], nr.at[0], mate)
    lend = remote(block_of(side), block_of(side), ns.at[1], nr.at[1], twin)
    pass_on = remote(block_of(1 - side), block_of(1 - side), ns.at[2], nr.at[2], twin)
    back = remote(away.at[:, :quarter], back_in, ns.at[3], nr.at[3], mate)

    def gain_of(c):
        return gain_ref[:, pl.ds(pl.multiple_of(core * width + c * tile, tile), tile)]

    @pl.loop(0, 4)
    def _(c):
        values = half_ref[:, piece(c, tile)].astype(jnp.float32)
        there = pl.ds(pl.multiple_of(core * width + c * tile, tile), tile)
        full[piece(side, tokens), there] = (values * sums[4][:, :1] * gain_of(c)).astype(
            full.dtype
        )

    swap.start()
    lend.start()
    sums[2] = jnp.zeros(sums.shape[1:], jnp.float32)
    for spot in range(each):
        for c in range(pieces):
            to_mate(spot, c).wait_recv()

    @pl.loop(0, 4)
    def _(c):
        columns = piece(c, tile)
        scaled = (own[:, columns] + across[:, columns].astype(jnp.float32)) * gain_of(c)
        own[:, columns] = scaled
        values = half_ref[:, columns].astype(jnp.float32)
        sums[2] += jnp.broadcast_to(
            jnp.sum(values * scaled, axis=1, keepdims=True), sums.shape[1:]
        )

    inners.start()
    for d in range(major):
        for copy in plane_copies(d):
            copy.wait_send()
    inners.wait_recv()

    per = rows // tokens
    broad = width // 2

    def line_of(origin, h):
        return table.at[origin // per, piece(lax.rem(origin, per), tokens), piece(h, broad)]

    def line_copy(step, way, h):
        origin = lax.rem(row - way * (step - 1) + major, major)
        to = lax.rem(row + way + major, major) * minor + place
        spot = ((step - 1) * 2 + (0 if way == 1 else 1)) * 2 + h
        here = line_of(origin, h)
        return remote(here, here, ds.at[spot], dr.at[spot], {"table": to})

    def leaves(step, way):
        return jnp.logical_and(has(-way * (step - 1)), has(way))

    def give_copies(i, origin, h):
        copies = []
        for j in range(1, minor):
            to = lax.rem(place + j, minor)
            spot = (i * minor + j) * 2 + h
            copies.append(
                remote(
                    looked.at[:, piece(origin * minor + to, capacity), piece(h, broad)],
                    arrived.at[:, piece(origin * minor + place, capacity), piece(h, broad)],
                    es.at[spot], er.at[spot], {"table": row * minor + to},
                )
            )
        return copies

    def keep_own(origin, h):
        at = piece(origin * minor + place, capacity)
        return pltpu.make_async_copy(
            looked.at[:, at, piece(h, broad)],
            arrived.at[:, at, piece(h, broad)],
            kept.at[origin * 2 + h],
        )

    def give(i, origin, h):
        for k in range(ngram):
            mark = slot_marks(
                places[origin * minor + place, k : k + 1, :], row * plane, plane
            )
            looked[k, piece(origin, plane), h * broad : (h + 1) * broad] = jnp.dot(
                mark,
                table[
                    origin // per,
                    piece(lax.rem(origin, per), tokens),
                    h * broad : (h + 1) * broad,
                ],
                preferred_element_type=jnp.float32,
            ).astype(looked.dtype)
        for copy in give_copies(i, origin, h) + [keep_own(origin, h)]:
            copy.start()

    for h in range(2):
        @pl.loop(0, 2)
        def _(c):
            columns = pl.ds(pl.multiple_of(h * broad + c * tile, tile), tile)
            scale = sums[4][:, :1]
            inner = (sums[2][:, :1] + sums[3][:, :1]) / full_width
            values = half_ref[:, columns].astype(jnp.float32)
            table[row // per, piece(lax.rem(row, per), tokens), columns] = (
                scale * own[:, columns] - values * scale * scale * scale * inner
            ).astype(table.dtype)

        for way in (1, -1):
            pl.when(leaves(1, way))(line_copy(1, way, h).start)

    step_of = min(256, quarter)

    def project(whose, out):
        @pl.loop(0, quarter // step_of)
        def _(c):
            columns = piece(c, step_of)
            out(
                c,
                jnp.dot(
                    full[piece(whose, tokens), :],
                    w_all[:, columns],
                    preferred_element_type=jnp.float32,
                ),
            )

    def put_away(c, values):
        away[:, piece(c, step_of)] = values.astype(away.dtype)

    def put_own(c, values):
        there = pl.ds(pl.multiple_of(side * quarter + c * step_of, step_of), step_of)
        proj_ref[:, there] = values.astype(proj_ref.dtype)

    def project_away():
        lend.wait_recv()
        pass_on.wait_recv()
        for spot in range(each):
            for c in range(pieces):
                to_mate(spot, c).wait_send()
        project(1 - side, put_away)
        back.start()

    for h in range(2):
        give(0, row, h)
    swap.wait_recv()
    pass_on.start()
    blocks = [(0, row, None)]
    for s in range(1, major):
        new = []
        for way in (1, -1):
            new.append((len(blocks), lax.rem(row - way * s + major, major), has(-way * s)))
            blocks.append(new[-1])
        for h in range(2):
            for way in (1, -1):
                pl.when(has(-way * s))(line_copy(s, way, h).wait_recv)
                if s + 1 < major:
                    pl.when(leaves(s + 1, way))(line_copy(s + 1, way, h).start)
            for i, origin, present in new:
                pl.when(present)(functools.partial(give, i, origin, h))
        if s == 1:
            project_away()
        if s == min(2, major - 1):
            project(side, put_own)

    back.wait_recv()
    proj_ref[:, piece(1 - side, quarter)] = back_in[...]
    for i, origin, present in blocks:

        def end():
            for h in range(2):
                for copy in give_copies(i, origin, h):
                    copy.wait_recv()
                    copy.wait_send()
                keep_own(origin, h).wait()

        if present is None:
            end()
        else:
            pl.when(present)(end)
    for copy in questions + [w_swap, c_swap, totals, inners, swap, lend, pass_on, back]:
        copy.wait_send()
    for d, way in ends:
        for h in range(CUTS):
            pl.when(has(way * d))(chain_copy(d, way, h).wait_send)
    for spot in range(each):
        for c in range(pieces):
            to_twin(other * each + spot, c).wait_send()
    for when, copy in started:
        when(copy.wait_send)
    for s in range(1, major):
        for way in (1, -1):
            for h in range(2):
                pl.when(leaves(s, way))(line_copy(s, way, h).wait_send)


def gather_and_exchange(w, facts, table, cot, codes, gain, capacity, n):
    steps = gather_steps(n // 2)
    lines = factors(n // 2)[0]
    major, minor = factors(n)
    ngram, _, width = table.shape
    levels = -(-ngram // 8) * 8
    span = n * w.shape[0] // lines
    pieces = lines // 2 * (span // min(512, span))
    tokens = cot.shape[0]
    depth = w.shape[0]
    half = (tokens, width)
    f32, bf16 = jnp.float32, jnp.bfloat16
    dma = pltpu.SemaphoreType.DMA
    return pl.pallas_call(
        functools.partial(gather_kernel, n),
        out_shape=(
            jax.ShapeDtypeStruct((ngram, n * capacity, width), bf16),
            jax.ShapeDtypeStruct((levels, n * capacity), f32),
            jax.ShapeDtypeStruct(half, bf16),
        ),
        in_specs=[ANY, WHOLE, ANY, ANY, WHOLE, WHOLE],
        out_specs=(ANY, WHOLE, WHOLE),
        scratch_shapes=[
            pltpu.VMEM((n * depth, width // 2), w.dtype),
            pltpu.VMEM(facts.shape, facts.dtype),
            pltpu.VMEM(table.shape, table.dtype),
            pltpu.VMEM((ngram, n * capacity, width), table.dtype),
            pltpu.VMEM((ngram, n * capacity, width), table.dtype),
            pltpu.VMEM((2 * tokens, width // 2), cot.dtype),
            pltpu.VMEM((2 * tokens, n * depth), f32),
            pltpu.VMEM((2 * tokens, width), f32),
            pltpu.VMEM(half, f32),
            pltpu.VMEM(half, bf16),
            pltpu.VMEM(half, bf16),
            pltpu.VMEM(half, bf16),
            pltpu.VMEM((5, tokens, 128), f32),
            pltpu.VMEM((major + 1, *half), bf16),
            pltpu.VMEM((n, *facts.shape), facts.dtype),
            pltpu.VMEM((2 * tokens, 2 * width), bf16),
            pltpu.VMEM((tokens, width // 2), bf16),
            dma((steps,)),
            dma((steps,)),
            dma((n,)),
            dma((n,)),
            dma((n,)),
            dma((n,)),
            dma((2 * (major - 1) * CUTS,)),
            dma((2 * (major - 1) * CUTS,)),
            dma((ngram,)),
            dma((2,)),
            dma((2,)),
            dma((pieces,)),
            dma((pieces,)),
            dma((pieces,)),
            dma((pieces,)),
            dma((2,)),
            dma((2,)),
            dma((4 * (major - 1),)),
            dma((4 * (major - 1),)),
            dma((2 * (2 * major - 1) * minor,)),
            dma((2 * (2 * major - 1) * minor,)),
            dma((4,)),
            dma((4,)),
            dma((2,)),
            dma((major,)),
            dma((2 * major,)),
        ],
        compiler_params=pltpu.CompilerParams(
            collective_id=1, has_side_effects=True, vmem_limit_bytes=VMEM_LIMIT
        ),
    )(w, facts, table, cot, codes, gain)


def sum_kernel(wanted_ref, arrived_ref, out_ref, hits):
    k = pl.program_id(0)
    rows, slots = hits.shape

    @pl.when(pl.program_id(1) == 0)
    def _():
        spots = lax.broadcasted_iota(jnp.int32, (rows, slots), 0).astype(jnp.float32) + 1.0
        wanted = wanted_ref[pl.ds(k, 1), :]
        hits[...] = (spots == wanted).astype(jnp.float32).astype(hits.dtype)

    out_ref[0] = jnp.dot(
        hits[...], arrived_ref[0], preferred_element_type=jnp.float32
    ).astype(out_ref.dtype)


def sum_rows(wanted, arrived, rows):
    ngram, slots, width = arrived.shape
    tile = min(1024, width)
    return pl.pallas_call(
        sum_kernel,
        grid=(ngram, width // tile),
        out_shape=jax.ShapeDtypeStruct((ngram, rows, width), arrived.dtype),
        in_specs=[
            pl.BlockSpec(wanted.shape, lambda k, c: (0, 0)),
            pl.BlockSpec((1, slots, tile), lambda k, c: (k, 0, c)),
        ],
        out_specs=pl.BlockSpec((1, rows, tile), lambda k, c: (k, 0, c)),
        scratch_shapes=[pltpu.VMEM((rows, slots), jnp.bfloat16)],
        compiler_params=pltpu.CompilerParams(vmem_limit_bytes=VMEM_LIMIT),
    )(wanted, arrived)


def on_device(
    hash_tables, byte_table, byte_ids, hash_owner, hash_offset, gain, proj_weight, cotangent
):
    groups = lax.axis_size("table")
    ngram, rows_dev, _ = hash_tables.shape
    tokens = byte_ids.shape[0]
    capacity = 2 * tokens // groups
    facts = jnp.concatenate([hash_owner[:, :, 0], hash_offset, byte_ids[None, :]], axis=0)
    levels = -(-facts.shape[0] // 8) * 8
    facts = jnp.pad(facts, ((0, levels - facts.shape[0]), (0, 0)))
    arrived, wanted, projected = gather_and_exchange(
        proj_weight, facts, hash_tables, cotangent, byte_table, gain[None, :], capacity, groups
    )
    return (projected, sum_rows(wanted, arrived, rows_dev))


def solution(mesh):
    return jax.shard_map(
        on_device,
        mesh=mesh,
        in_specs=(
            P(None, "table", "mp"),
            P(None, "mp"),
            P("table"),
            P(None, "table", None),
            P(None, "table"),
            P(),
            P("table", "mp"),
            P("table", "mp"),
        ),
        out_specs=(P("table", "mp"), P(None, "table", "mp")),
        check_vma=False,
    )
```

```python
import functools

import jax
import jax.numpy as jnp
from jax import lax
from jax.experimental import pallas as pl
from jax.experimental.pallas import tpu as pltpu
from jax.sharding import PartitionSpec as P

eps = 1e-05
MESH = pl.DeviceIdType.MESH
ANY = pl.BlockSpec(memory_space=pl.ANY)
WHOLE = pl.BlockSpec(memory_space=pltpu.VMEM)
VMEM_LIMIT = 61 * 2**20
EARLY = 6
CUTS = 2


def piece(i, size):
    return pl.ds(pl.multiple_of(i * size, size), size)


def greet_all(n, meanwhile=None):
    me = lax.axis_index("table")
    other = 1 - lax.axis_index("mp")
    barrier = pltpu.get_barrier_semaphore()
    for j in range(1, n):
        pl.semaphore_signal(
            barrier, inc=1, device_id={"table": lax.rem(me + j, n)}, device_id_type=MESH
        )
    pl.semaphore_signal(barrier, inc=1, device_id={"mp": other}, device_id_type=MESH)
    if meanwhile is not None:
        meanwhile()
    pl.semaphore_wait(barrier, n)
    return other


def remote(src, dst, send, recv, to):
    return pltpu.make_async_remote_copy(
        src_ref=src,
        dst_ref=dst,
        send_sem=send,
        recv_sem=recv,
        device_id=to,
        device_id_type=MESH,
    )


def factors(n):
    major = 1
    while major * major < n:
        major *= 2
    return major, n // major


def snake(i):
    return (i // 2) * 2 + (i % 2 + i // 2) % 2


def gather_steps(n):
    major, minor = factors(n)
    return 6 * major + 2 + (2 * major - 1) * 2 * (minor // 2)


def early_rows(depth, minor):
    return depth * EARLY // 32 * 2 if minor == 2 else 0


def run_gather(n, out_ref, depth, send, recv, begun, swapped, between, done, last):
    major, minor = factors(n)
    half = minor // 2
    early = early_rows(depth, minor)
    side = lax.rem(lax.axis_index("table"), 2)
    me = lax.axis_index("table") // 2
    row, place = me // minor, snake(me % minor)
    spot = [0]
    sends = []

    def always(body):
        body()

    def when(condition):
        return always if condition is None else pl.when(condition)

    def on_ring(r, shift):
        return r * minor + snake(lax.rem(place + shift + minor, minor))

    def copy_of(origin, offset, size, to):
        at = pl.ds(pl.multiple_of(origin * depth + offset, 16), size)
        copy = remote(
            out_ref.at[at],
            out_ref.at[at],
            send.at[spot[0]],
            recv.at[spot[0]],
            {"table": to * 2 + side},
        )
        spot[0] += 1
        return copy

    def has(shift):
        return jnp.logical_and(row + shift >= 0, row + shift < major)

    def line_go(step, over, offset, size):
        copies = []
        for way in (1, -1):
            origin = lax.rem(row - way * (step - 1) + major, major)
            to = lax.rem(row + way + major, major)
            column = me % minor if over == 0 else minor - 1 - me % minor
            copy = copy_of(origin * minor + column, offset, size, to * minor + me % minor)
            leaves = jnp.logical_and(has(-way * (step - 1)), has(way))
            pl.when(leaves)(copy.start)
            sends.append((leaves, copy))
            copies.append((has(-way * step), copy))
        return copies

    def ring_go(block, present, step, parts=None):
        if parts is None and step < half:
            parts = ((0, depth), (0, depth))
        elif parts is None:
            size = (depth - early) // 2
            parts = ((0, size), (depth - size, size))
        pair = (
            copy_of(on_ring(block, 1 - step), *parts[0], on_ring(row, 1)),
            copy_of(on_ring(block, step - 1), *parts[1], on_ring(row, -1)),
        )
        for copy in pair:
            when(present)(copy.start)
            sends.append((present, copy))
        return pair

    def start(copy):
        copy.start()
        sends.append((None, copy))
        return copy

    def land(copies):
        for present, copy in copies:
            pl.when(present)(copy.wait_recv)

    blocks = [(row, None)]
    stage = [1]
    low = depth // 2
    flight = [line_go(1, 0, side * low, low)]
    if early:
        first = [start(copy_of(me, side * low, low, on_ring(row, 1)))]
        begun()
        swapped()
        flight.append(line_go(1, 0, (1 - side) * low, low))
        first.append(start(copy_of(me, (1 - side) * low, low, on_ring(row, 1))))
        rings = [tuple(first)]
    else:
        begun()
        swapped()
        flight.append(line_go(1, 0, (1 - side) * low, low))
        rings = [ring_go(row, None, 1)]
    between(0)
    extra = []
    middle = (depth - early) // 2

    def advance(i):
        block, present = blocks[i]
        step = stage[i]
        stage[i] += 1
        for copy in rings[i]:
            when(present)(copy.wait_recv)
        if step < half:
            rings[i] = ring_go(block, present, step + 1)
        else:
            done(block, when(present))

    for step in range(1, major):
        known = len(blocks)
        for way in (1, -1):
            block = lax.rem(row - way * step + major, major)
            blocks.append((block, has(-way * step)))
            stage.append(1)
            rings.append(())
        onward = []
        for copies, q in zip(flight, (side, 1 - side)):
            land(copies)
            if step + 1 < major:
                onward.append(line_go(step + 1, 0, q * low, low))
            if early:
                for i in range(known, len(blocks)):
                    block, present = blocks[i]
                    copy = copy_of(
                        on_ring(block, 0), q * (depth - middle), middle, on_ring(row, 1)
                    )
                    pl.when(present)(copy.start)
                    sends.append((present, copy))
                    rings[i] += (copy,)
        flight = onward
        if not early:
            for i in range(known, len(blocks)):
                rings[i] = ring_go(*blocks[i], 1)
        if early:
            if step == 1:
                advance(0)
            land(extra)
            extra = line_go(step, 1, middle, early)
        between(step)
        for i in range(known):
            if stage[i] <= half:
                advance(i)
    land(extra)
    for _ in range(half):
        for i in range(len(blocks)):
            if stage[i] <= half:
                advance(i)
    last()
    return [(when(present), copy) for present, copy in sends]


def rows_of(ref, d, capacity):
    return ref.at[:, piece(d, capacity)]


def slot_marks(slots, first, amount):
    spot = lax.broadcasted_iota(jnp.int32, (amount, slots.shape[1]), 0) + first
    return (spot == slots).astype(jnp.float32).astype(jnp.bfloat16)


def gather_kernel(
    n, w_ref, owner_ref, offset_ref, ids_ref, table_ref, cot_ref, bytes_ref, gain_ref,
    arrived, wanted_ref, proj_ref,
    w_all, tell, owner, offset, ids, table, looked, y_ref, cots, part, beside, own, away, across, half_ref,
    sums, chain, places, full, back_in, ws, wr, qs, qr, xs, xr, zs, zr, ts, ps, pr, cs, cr, gs, gr, ms, mr,
    ds, dr, es, er, ns, nr, local, still, kept, fs,
):
    core = lax.axis_index("mp")
    other = 1 - core
    major, minor = factors(n)
    me = lax.axis_index("table")
    row, place = me // minor, lax.rem(me, minor)
    side = lax.rem(me, 2)
    mate = {"table": me + 1 - 2 * side}
    twin = {"mp": other}
    depth = w_ref.shape[0]
    ngram, rows, width = table_ref.shape
    tokens = cot_ref.shape[0]
    quarter = width // 2
    capacity = looked.shape[1] // n
    plane = minor * capacity
    lines, fast = factors(n // 2)
    each = lines // 2
    span = fast * 2 * depth
    tile = width // 4

    def has(shift):
        return jnp.logical_and(row + shift >= 0, row + shift < major)

    w_swap = remote(
        w_ref.at[:, piece(1 - side, quarter)], w_all.at[piece(me, depth)],
        ps.at[0], pr.at[0], mate,
    )
    c_swap = remote(
        cot_ref.at[:, piece(1 - side, quarter)], cots.at[piece(side, tokens)],
        ps.at[1], pr.at[1], mate,
    )
    keep = (
        pltpu.make_async_copy(
            w_ref.at[:, piece(side, quarter)], w_all.at[piece(me, depth)], local.at[0]
        ),
        pltpu.make_async_copy(
            cot_ref.at[:, piece(side, quarter)], cots.at[piece(side, tokens)], local.at[1]
        ),
    )
    loads = [
        pltpu.make_async_copy(table_ref.at[k], table.at[k], ts.at[k]) for k in range(ngram)
    ]
    questions = []
    for j in range(1, n):
        to = lax.rem(me + j, n)
        questions.append(remote(tell, places.at[me], qs.at[j], qr.at[j], {"table": to}))

    facts = [
        pltpu.make_async_copy(src, dst, fs.at[i])
        for i, (src, dst) in enumerate(
            ((owner_ref, owner), (offset_ref, offset), (ids_ref, ids))
        )
    ]
    for copy in facts + [keep[0]] + loads + [keep[1]]:
        copy.start()

    def find_slots():
        before_mask = lax.broadcasted_iota(jnp.int32, (tokens, tokens), 0) < lax.broadcasted_iota(
            jnp.int32, (tokens, tokens), 1
        )
        earlier = before_mask.astype(jnp.float32).astype(jnp.bfloat16)
        for copy in facts:
            copy.wait()
        tell[...] = jnp.zeros(tell.shape, tell.dtype)
        tell[ngram : 2 * ngram, :] = offset[...]
        for k in range(ngram):
            owners = owner[k : k + 1, :]
            named = (lax.broadcasted_iota(jnp.int32, (n, tokens), 0) == owners).astype(jnp.float32)
            before = jnp.dot(
                named.astype(jnp.bfloat16), earlier, preferred_element_type=jnp.float32
            )
            rank = jnp.sum(before * named, axis=0, keepdims=True).astype(jnp.int32)
            tell[k : k + 1, :] = owners * capacity + rank
        places[me] = tell[...]

    greet_all(n, find_slots)
    w_swap.start()
    for copy in questions:
        copy.start()
    c_swap.start()

    def plane_copies(d):
        copies = []
        for j in range(1, minor):
            to = lax.rem(place + j, minor)
            copies.append(
                remote(
                    rows_of(looked, d * minor + to, capacity),
                    rows_of(y_ref, d * minor + place, capacity),
                    xs.at[d * minor + j], xr.at[d * minor + j], {"table": row * minor + to},
                )
            )
        return copies

    def stay(d):
        return pltpu.make_async_copy(
            rows_of(looked, d * minor + place, capacity),
            rows_of(y_ref, d * minor + place, capacity),
            still.at[d],
        )

    ends = [(d, way) for d in range(major - 1, 0, -1) for way in (1, -1)]

    def target(d, way):
        return lax.rem(row + way * d + major, major)

    def plane_go(d):
        for copy in plane_copies(d) + [stay(d)]:
            copy.start()

    group = 128 // capacity

    def find_rows():
        for copy in questions:
            copy.wait_recv()
        ours = lax.broadcasted_iota(jnp.int32, (capacity, tokens), 0) + me * capacity
        spots = lax.broadcasted_iota(jnp.int32, (128, rows), 1).astype(jnp.float32) + 1.0
        down = lax.broadcasted_iota(jnp.int32, (128, 128), 0)
        same = down == lax.broadcasted_iota(jnp.int32, (128, 128), 1)
        for k in range(ngram):
            for q in range(n // group):
                wanted = []
                for d in range(q * group, (q + 1) * group):
                    offsets = places[d, ngram + k : ngram + k + 1, :].astype(jnp.float32) + 1.0
                    named = ours == places[d, k : k + 1, :]
                    wanted.append(
                        jnp.sum(jnp.where(named, offsets, 0.0), axis=1, keepdims=True)
                    )
                wanted = jnp.concatenate(wanted, axis=0)
                wanted_ref[k : k + 1, q * 128 : (q + 1) * 128] = jnp.sum(
                    jnp.where(same, wanted, 0.0), axis=0, keepdims=True
                )
                full[q * 128 : (q + 1) * 128, k * rows : (k + 1) * rows] = (
                    (spots == wanted).astype(jnp.float32).astype(jnp.bfloat16)
                )

    def look_up():
        for load in loads:
            load.wait()
        for k in range(ngram):
            @pl.loop(0, 8)
            def _(c):
                columns = piece(c, width // 8)
                looked[k, :, columns] = jnp.dot(
                    full[:, k * rows : (k + 1) * rows],
                    table[k, :, columns],
                    preferred_element_type=jnp.float32,
                ).astype(looked.dtype)

    def arrive(d):
        for copy in plane_copies(d):
            copy.wait_recv()
        stay(d).wait()

    def part_of(d, columns):
        total = None
        for k in range(ngram):
            mark = slot_marks(places[d * minor + place, k : k + 1, :], row * plane, plane)
            term = lax.dot_general(
                mark,
                y_ref[k, piece(d, plane), columns],
                (((0,), (0,)), ((), ())),
                preferred_element_type=jnp.float32,
            )
            total = term if total is None else total + term
        return total

    def chain_copy(d, way, h):
        to = lax.rem(row + way + major, major) * minor + place
        spot = ((d - 1) * 2 + (0 if way == 1 else 1)) * CUTS + h
        land = major if d == 1 and way == -1 else target(d, way)
        columns = piece(h, width // CUTS)
        return remote(
            chain.at[target(d, way), :, columns], chain.at[land, :, columns],
            zs.at[spot], zr.at[spot], {"table": to},
        )

    def hop(d, way, among=None):
        goes = has(way * d)

        @pl.when(goes if among is None else jnp.logical_and(goes, among))
        def _():
            end = target(d, way)
            arrive(end)

            for h in range(CUTS):
                if d < major - 1:
                    pl.when(has(-way))(chain_copy(d + 1, way, h).wait_recv)

                @pl.loop(h * 4 // CUTS, (h + 1) * 4 // CUTS)
                def _(c):
                    columns = piece(c, tile)
                    total = part_of(end, columns) + chain[end, :, columns].astype(jnp.float32)
                    chain[end, :, columns] = total.astype(chain.dtype)

                chain_copy(d, way, h).start()

    def hand_out(d):
        if d == 0:
            plane_go(row)
        else:
            for way in (1, -1):
                pl.when(has(way * d))(functools.partial(plane_go, target(d, way)))

    def between(i):
        if i == 0:
            look_up()
            hand_out(major - 1)
            hand_out(major - 2)
            for way in (1, -1):
                @pl.when(jnp.logical_not(has(-way)))
                def _():
                    for d in range(0, major):
                        land = major if d == 0 and way == -1 else target(d, way)
                        chain[land] = jnp.zeros(chain.shape[1:], chain.dtype)

            c_swap.wait_recv()
            keep[1].wait()
        else:
            for way in (1, -1):
                head = jnp.logical_not(has(-way))
                if i == 1:
                    hop(major - 1, way)
                else:
                    hop(major - i, way, has(-way))
                if i < major - 1:
                    hop(major - 1 - i, way, head)
            if i < major - 1:
                hand_out(major - 2 - i)

    totals = remote(sums.at[0], sums.at[1], ms.at[0], mr.at[0], twin)
    inners = remote(sums.at[2], sums.at[3], ms.at[1], mr.at[1], twin)

    def embed():
        arrive(row)
        sums[0] = jnp.zeros(sums.shape[1:], jnp.float32)
        picks = slot_marks(ids[...], 0, bytes_ref.shape[0])
        for h in range(CUTS):
            for way in (1, -1):
                pl.when(has(-way))(chain_copy(1, way, h).wait_recv)

            @pl.loop(h * 4 // CUTS, (h + 1) * 4 // CUTS)
            def _(c):
                columns = piece(c, tile)
                total = lax.dot_general(
                    picks,
                    bytes_ref[:, columns],
                    (((0,), (0,)), ((), ())),
                    preferred_element_type=jnp.float32,
                )
                total = total + part_of(row, columns)
                total = total + chain[row, :, columns].astype(jnp.float32)
                total = total + chain[major, :, columns].astype(jnp.float32)
                rounded = total.astype(half_ref.dtype)
                half_ref[:, columns] = rounded
                values = rounded.astype(jnp.float32)
                sums[0] += jnp.broadcast_to(
                    jnp.sum(values * values, axis=1, keepdims=True), sums.shape[1:]
                )

        totals.start()

    chunk = min(512, span)

    pieces = span // chunk

    def to_twin(block, c):
        spot = lax.rem(block, each)
        return remote(
            part.at[:, pl.ds(pl.multiple_of(block * span + c * chunk, chunk), chunk)],
            beside.at[:, pl.ds(pl.multiple_of(spot * span + c * chunk, chunk), chunk)],
            cs.at[spot * pieces + c],
            cr.at[spot * pieces + c],
            twin,
        )

    def to_mate(spot, c):
        at = pl.ds(pl.multiple_of(spot * span + c * chunk, chunk), chunk)
        i = spot * pieces + c
        return remote(away.at[:, at], across.at[:, at], gs.at[i], gr.at[i], mate)

    def finish(block):
        spot = lax.rem(block, each)
        theirs, ours = piece(1 - side, tokens), piece(side, tokens)

        @pl.when(block // each == core)
        def _():
            for c in range(pieces):
                to_twin(block, c).wait_recv()
                come = pl.ds(pl.multiple_of(block * span + c * chunk, chunk), chunk)
                go = pl.ds(pl.multiple_of(spot * span + c * chunk, chunk), chunk)
                away[:, go] = (part[theirs, come] + beside[theirs, go]).astype(away.dtype)
                to_mate(spot, c).start()
            for c in range(pieces):
                come = pl.ds(pl.multiple_of(block * span + c * chunk, chunk), chunk)
                go = pl.ds(pl.multiple_of(spot * span + c * chunk, chunk), chunk)
                own[:, go] = part[ours, come] + beside[ours, go]

    waiting = []

    def done(block, when):
        @when
        def _():
            for c in range(pieces):
                some = pl.ds(pl.multiple_of(block * span + c * chunk, chunk), chunk)
                part[:, some] = lax.dot_general(
                    cots[...],
                    w_all[some, :],
                    (((1,), (1,)), ((), ())),
                    preferred_element_type=jnp.float32,
                )
                pl.when(block // each == other)(to_twin(block, c).start)

        waiting.append((block, when))
        if len(waiting) > 1:
            settle()

    def settle():
        block, when = waiting.pop(0)
        when(functools.partial(finish, block))

    keep[0].wait()
    started = run_gather(
        n // 2, w_all, 2 * depth, ws, wr, find_rows, w_swap.wait_recv, between, done, embed
    )
    while waiting:
        settle()

    totals.wait_recv()
    full_width = 2 * width
    sums[4] = lax.rsqrt((sums[0] + sums[1]) / full_width + eps)

    def block_of(whose):
        return full.at[piece(whose, tokens), piece(core, width)]

    swap = remote(block_of(side), block_of(side), ns.at[0], nr.at[0], mate)
    lend = remote(block_of(side), block_of(side), ns.at[1], nr.at[1], twin)
    pass_on = remote(block_of(1 - side), block_of(1 - side), ns.at[2], nr.at[2], twin)
    back = remote(away.at[:, :quarter], back_in, ns.at[3], nr.at[3], mate)

    def gain_of(c):
        return gain_ref[:, pl.ds(pl.multiple_of(core * width + c * tile, tile), tile)]

    @pl.loop(0, 4)
    def _(c):
        values = half_ref[:, piece(c, tile)].astype(jnp.float32)
        there = pl.ds(pl.multiple_of(core * width + c * tile, tile), tile)
        full[piece(side, tokens), there] = (values * sums[4][:, :1] * gain_of(c)).astype(
            full.dtype
        )

    swap.start()
    lend.start()
    sums[2] = jnp.zeros(sums.shape[1:], jnp.float32)
    for spot in range(each):
        for c in range(pieces):
            to_mate(spot, c).wait_recv()

    @pl.loop(0, 4)
    def _(c):
        columns = piece(c, tile)
        scaled = (own[:, columns] + across[:, columns].astype(jnp.float32)) * gain_of(c)
        own[:, columns] = scaled
        values = half_ref[:, columns].astype(jnp.float32)
        sums[2] += jnp.broadcast_to(
            jnp.sum(values * scaled, axis=1, keepdims=True), sums.shape[1:]
        )

    inners.start()
    for d in range(major):
        for copy in plane_copies(d):
            copy.wait_send()
    inners.wait_recv()

    per = rows // tokens
    broad = width // 2

    def line_of(origin, h):
        return table.at[origin // per, piece(lax.rem(origin, per), tokens), piece(h, broad)]

    def line_copy(step, way, h):
        origin = lax.rem(row - way * (step - 1) + major, major)
        to = lax.rem(row + way + major, major) * minor + place
        spot = ((step - 1) * 2 + (0 if way == 1 else 1)) * 2 + h
        here = line_of(origin, h)
        return remote(here, here, ds.at[spot], dr.at[spot], {"table": to})

    def leaves(step, way):
        return jnp.logical_and(has(-way * (step - 1)), has(way))

    def give_copies(i, origin, h):
        copies = []
        for j in range(1, minor):
            to = lax.rem(place + j, minor)
            spot = (i * minor + j) * 2 + h
            copies.append(
                remote(
                    looked.at[:, piece(origin * minor + to, capacity), piece(h, broad)],
                    arrived.at[:, piece(origin * minor + place, capacity), piece(h, broad)],
                    es.at[spot], er.at[spot], {"table": row * minor + to},
                )
            )
        return copies

    def keep_own(origin, h):
        at = piece(origin * minor + place, capacity)
        return pltpu.make_async_copy(
            looked.at[:, at, piece(h, broad)],
            arrived.at[:, at, piece(h, broad)],
            kept.at[origin * 2 + h],
        )

    def give(i, origin, h):
        for k in range(ngram):
            mark = slot_marks(
                places[origin * minor + place, k : k + 1, :], row * plane, plane
            )
            looked[k, piece(origin, plane), h * broad : (h + 1) * broad] = jnp.dot(
                mark,
                table[
                    origin // per,
                    piece(lax.rem(origin, per), tokens),
                    h * broad : (h + 1) * broad,
                ],
                preferred_element_type=jnp.float32,
            ).astype(looked.dtype)
        for copy in give_copies(i, origin, h) + [keep_own(origin, h)]:
            copy.start()

    for h in range(2):
        @pl.loop(0, 2)
        def _(c):
            columns = pl.ds(pl.multiple_of(h * broad + c * tile, tile), tile)
            scale = sums[4][:, :1]
            inner = (sums[2][:, :1] + sums[3][:, :1]) / full_width
            values = half_ref[:, columns].astype(jnp.float32)
            table[row // per, piece(lax.rem(row, per), tokens), columns] = (
                scale * own[:, columns] - values * scale * scale * scale * inner
            ).astype(table.dtype)

        for way in (1, -1):
            pl.when(leaves(1, way))(line_copy(1, way, h).start)

    step_of = min(256, quarter)

    def project(whose, out):
        @pl.loop(0, quarter // step_of)
        def _(c):
            columns = piece(c, step_of)
            out(
                c,
                jnp.dot(
                    full[piece(whose, tokens), :],
                    w_all[:, columns],
                    preferred_element_type=jnp.float32,
                ),
            )

    def put_away(c, values):
        away[:, piece(c, step_of)] = values.astype(away.dtype)

    def put_own(c, values):
        there = pl.ds(pl.multiple_of(side * quarter + c * step_of, step_of), step_of)
        proj_ref[:, there] = values.astype(proj_ref.dtype)

    def project_away():
        lend.wait_recv()
        pass_on.wait_recv()
        for spot in range(each):
            for c in range(pieces):
                to_mate(spot, c).wait_send()
        project(1 - side, put_away)
        back.start()

    for h in range(2):
        give(0, row, h)
    swap.wait_recv()
    pass_on.start()
    blocks = [(0, row, None)]
    for s in range(1, major):
        new = []
        for way in (1, -1):
            new.append((len(blocks), lax.rem(row - way * s + major, major), has(-way * s)))
            blocks.append(new[-1])
        for h in range(2):
            for way in (1, -1):
                pl.when(has(-way * s))(line_copy(s, way, h).wait_recv)
                if s + 1 < major:
                    pl.when(leaves(s + 1, way))(line_copy(s + 1, way, h).start)
            for i, origin, present in new:
                pl.when(present)(functools.partial(give, i, origin, h))
        if s == 1:
            project_away()
        if s == min(2, major - 1):
            project(side, put_own)

    back.wait_recv()
    proj_ref[:, piece(1 - side, quarter)] = back_in[...]
    for i, origin, present in blocks:

        def end():
            for h in range(2):
                for copy in give_copies(i, origin, h):
                    copy.wait_recv()
                    copy.wait_send()
                keep_own(origin, h).wait()

        if present is None:
            end()
        else:
            pl.when(present)(end)
    for copy in questions + [w_swap, c_swap, totals, inners, swap, lend, pass_on, back]:
        copy.wait_send()
    for d, way in ends:
        for h in range(CUTS):
            pl.when(has(way * d))(chain_copy(d, way, h).wait_send)
    for spot in range(each):
        for c in range(pieces):
            to_twin(other * each + spot, c).wait_send()
    for when, copy in started:
        when(copy.wait_send)
    for s in range(1, major):
        for way in (1, -1):
            for h in range(2):
                pl.when(leaves(s, way))(line_copy(s, way, h).wait_send)


def gather_and_exchange(w, owners, offsets, ids, table, cot, codes, gain, capacity, n):
    steps = gather_steps(n // 2)
    lines = factors(n // 2)[0]
    major, minor = factors(n)
    ngram, _, width = table.shape
    levels = -(-ngram // 8) * 8
    span = n * w.shape[0] // lines
    pieces = lines // 2 * (span // min(512, span))
    tokens = cot.shape[0]
    depth = w.shape[0]
    half = (tokens, width)
    told = (-(-2 * ngram // 8) * 8, tokens)
    f32, bf16 = jnp.float32, jnp.bfloat16
    dma = pltpu.SemaphoreType.DMA
    return pl.pallas_call(
        functools.partial(gather_kernel, n),
        out_shape=(
            jax.ShapeDtypeStruct((ngram, n * capacity, width), bf16),
            jax.ShapeDtypeStruct((levels, n * capacity), f32),
            jax.ShapeDtypeStruct(half, bf16),
        ),
        in_specs=[ANY, ANY, ANY, ANY, ANY, ANY, WHOLE, WHOLE],
        out_specs=(ANY, WHOLE, WHOLE),
        scratch_shapes=[
            pltpu.VMEM((n * depth, width // 2), w.dtype),
            pltpu.VMEM(told, owners.dtype),
            pltpu.VMEM(owners.shape, owners.dtype),
            pltpu.VMEM(offsets.shape, offsets.dtype),
            pltpu.VMEM(ids.shape, ids.dtype),
            pltpu.VMEM(table.shape, table.dtype),
            pltpu.VMEM((ngram, n * capacity, width), table.dtype),
            pltpu.VMEM((ngram, n * capacity, width), table.dtype),
            pltpu.VMEM((2 * tokens, width // 2), cot.dtype),
            pltpu.VMEM((2 * tokens, n * depth), f32),
            pltpu.VMEM((2 * tokens, width), f32),
            pltpu.VMEM(half, f32),
            pltpu.VMEM(half, bf16),
            pltpu.VMEM(half, bf16),
            pltpu.VMEM(half, bf16),
            pltpu.VMEM((5, tokens, 128), f32),
            pltpu.VMEM((major + 1, *half), bf16),
            pltpu.VMEM((n, *told), owners.dtype),
            pltpu.VMEM((2 * tokens, 2 * width), bf16),
            pltpu.VMEM((tokens, width // 2), bf16),
            dma((steps,)),
            dma((steps,)),
            dma((n,)),
            dma((n,)),
            dma((n,)),
            dma((n,)),
            dma((2 * (major - 1) * CUTS,)),
            dma((2 * (major - 1) * CUTS,)),
            dma((ngram,)),
            dma((2,)),
            dma((2,)),
            dma((pieces,)),
            dma((pieces,)),
            dma((pieces,)),
            dma((pieces,)),
            dma((2,)),
            dma((2,)),
            dma((4 * (major - 1),)),
            dma((4 * (major - 1),)),
            dma((2 * (2 * major - 1) * minor,)),
            dma((2 * (2 * major - 1) * minor,)),
            dma((4,)),
            dma((4,)),
            dma((2,)),
            dma((major,)),
            dma((2 * major,)),
            dma((3,)),
        ],
        compiler_params=pltpu.CompilerParams(
            collective_id=1, has_side_effects=True, vmem_limit_bytes=VMEM_LIMIT
        ),
    )(w, owners, offsets, ids, table, cot, codes, gain)


def sum_kernel(wanted_ref, arrived_ref, proj_ref, out_ref, proj_out, hits):
    k = pl.program_id(0)
    rows, slots = hits.shape
    proj_out[...] = proj_ref[...]

    @pl.when(pl.program_id(1) == 0)
    def _():
        spots = lax.broadcasted_iota(jnp.int32, (rows, slots), 0).astype(jnp.float32) + 1.0
        wanted = wanted_ref[pl.ds(k, 1), :]
        hits[...] = (spots == wanted).astype(jnp.float32).astype(hits.dtype)

    out_ref[0] = jnp.dot(
        hits[...], arrived_ref[0], preferred_element_type=jnp.float32
    ).astype(out_ref.dtype)


def sum_rows(wanted, arrived, projected, rows):
    ngram, slots, width = arrived.shape
    tile = min(1024, width)
    across = width // tile
    some = pl.BlockSpec(
        (projected.shape[0] // (ngram * across), width), lambda k, c: (k * across + c, 0)
    )
    return pl.pallas_call(
        sum_kernel,
        grid=(ngram, width // tile),
        out_shape=(
            jax.ShapeDtypeStruct((ngram, rows, width), arrived.dtype),
            jax.ShapeDtypeStruct(projected.shape, projected.dtype),
        ),
        in_specs=[
            pl.BlockSpec(wanted.shape, lambda k, c: (0, 0)),
            pl.BlockSpec((1, slots, tile), lambda k, c: (k, 0, c)),
            some,
        ],
        out_specs=(pl.BlockSpec((1, rows, tile), lambda k, c: (k, 0, c)), some),
        scratch_shapes=[pltpu.VMEM((rows, slots), jnp.bfloat16)],
        compiler_params=pltpu.CompilerParams(vmem_limit_bytes=VMEM_LIMIT),
    )(wanted, arrived, projected)


def on_device(
    hash_tables, byte_table, byte_ids, hash_owner, hash_offset, gain, proj_weight, cotangent
):
    groups = lax.axis_size("table")
    ngram, rows_dev, _ = hash_tables.shape
    tokens = byte_ids.shape[0]
    capacity = 2 * tokens // groups
    arrived, wanted, projected = gather_and_exchange(
        proj_weight, hash_owner[:, :, 0], hash_offset, byte_ids[None, :], hash_tables, cotangent,
        byte_table, gain[None, :], capacity, groups,
    )
    grads, projected = sum_rows(wanted, arrived, projected, rows_dev)
    return (projected, grads)


def solution(mesh):
    return jax.shard_map(
        on_device,
        mesh=mesh,
        in_specs=(
            P(None, "table", "mp"),
            P(None, "mp"),
            P("table"),
            P(None, "table", None),
            P(None, "table"),
            P(),
            P("table", "mp"),
            P("table", "mp"),
        ),
        out_specs=(P("table", "mp"), P(None, "table", "mp")),
        check_vma=False,
    )
```

```python
import functools

import jax
import jax.numpy as jnp
from jax import lax
from jax.experimental import pallas as pl
from jax.experimental.pallas import tpu as pltpu
from jax.sharding import PartitionSpec as P

eps = 1e-05
MESH = pl.DeviceIdType.MESH
ANY = pl.BlockSpec(memory_space=pl.ANY)
WHOLE = pl.BlockSpec(memory_space=pltpu.VMEM)
VMEM_LIMIT = 61 * 2**20
EARLY = 6
CUTS = 2


def piece(i, size):
    return pl.ds(pl.multiple_of(i * size, size), size)


def greet_all(n, meanwhile=None):
    me = lax.axis_index("table")
    other = 1 - lax.axis_index("mp")
    barrier = pltpu.get_barrier_semaphore()
    for j in range(1, n):
        pl.semaphore_signal(
            barrier, inc=1, device_id={"table": lax.rem(me + j, n)}, device_id_type=MESH
        )
    pl.semaphore_signal(barrier, inc=1, device_id={"mp": other}, device_id_type=MESH)
    if meanwhile is not None:
        meanwhile()
    pl.semaphore_wait(barrier, n)
    return other


def remote(src, dst, send, recv, to):
    return pltpu.make_async_remote_copy(
        src_ref=src,
        dst_ref=dst,
        send_sem=send,
        recv_sem=recv,
        device_id=to,
        device_id_type=MESH,
    )


def factors(n):
    major = 1
    while major * major < n:
        major *= 2
    return major, n // major


def snake(i):
    return (i // 2) * 2 + (i % 2 + i // 2) % 2


def gather_steps(n):
    major, minor = factors(n)
    return 6 * major + 2 + (2 * major - 1) * 2 * (minor // 2)


def early_rows(depth, minor):
    return depth * EARLY // 32 * 2 if minor == 2 else 0


def run_gather(n, out_ref, depth, send, recv, begun, swapped, between, done, last):
    major, minor = factors(n)
    half = minor // 2
    early = early_rows(depth, minor)
    side = lax.rem(lax.axis_index("table"), 2)
    me = lax.axis_index("table") // 2
    row, place = me // minor, snake(me % minor)
    spot = [0]
    sends = []

    def always(body):
        body()

    def when(condition):
        return always if condition is None else pl.when(condition)

    def on_ring(r, shift):
        return r * minor + snake(lax.rem(place + shift + minor, minor))

    def copy_of(origin, offset, size, to):
        at = pl.ds(pl.multiple_of(origin * depth + offset, 16), size)
        copy = remote(
            out_ref.at[at],
            out_ref.at[at],
            send.at[spot[0]],
            recv.at[spot[0]],
            {"table": to * 2 + side},
        )
        spot[0] += 1
        return copy

    def has(shift):
        return jnp.logical_and(row + shift >= 0, row + shift < major)

    def line_go(step, over, offset, size):
        copies = []
        for way in (1, -1):
            origin = lax.rem(row - way * (step - 1) + major, major)
            to = lax.rem(row + way + major, major)
            column = me % minor if over == 0 else minor - 1 - me % minor
            copy = copy_of(origin * minor + column, offset, size, to * minor + me % minor)
            leaves = jnp.logical_and(has(-way * (step - 1)), has(way))
            pl.when(leaves)(copy.start)
            sends.append((leaves, copy))
            copies.append((has(-way * step), copy))
        return copies

    def ring_go(block, present, step, parts=None):
        if parts is None and step < half:
            parts = ((0, depth), (0, depth))
        elif parts is None:
            size = (depth - early) // 2
            parts = ((0, size), (depth - size, size))
        pair = (
            copy_of(on_ring(block, 1 - step), *parts[0], on_ring(row, 1)),
            copy_of(on_ring(block, step - 1), *parts[1], on_ring(row, -1)),
        )
        for copy in pair:
            when(present)(copy.start)
            sends.append((present, copy))
        return pair

    def start(copy):
        copy.start()
        sends.append((None, copy))
        return copy

    def land(copies):
        for present, copy in copies:
            pl.when(present)(copy.wait_recv)

    blocks = [(row, None)]
    stage = [1]
    low = depth // 2
    flight = [line_go(1, 0, side * low, low)]
    if early:
        first = [start(copy_of(me, side * low, low, on_ring(row, 1)))]
        begun()
        swapped()
        flight.append(line_go(1, 0, (1 - side) * low, low))
        first.append(start(copy_of(me, (1 - side) * low, low, on_ring(row, 1))))
        rings = [tuple(first)]
    else:
        begun()
        swapped()
        flight.append(line_go(1, 0, (1 - side) * low, low))
        rings = [ring_go(row, None, 1)]
    between(0)
    extra = []
    middle = (depth - early) // 2

    def advance(i):
        block, present = blocks[i]
        step = stage[i]
        stage[i] += 1
        for copy in rings[i]:
            when(present)(copy.wait_recv)
        if step < half:
            rings[i] = ring_go(block, present, step + 1)
        else:
            done(block, when(present))

    for step in range(1, major):
        known = len(blocks)
        for way in (1, -1):
            block = lax.rem(row - way * step + major, major)
            blocks.append((block, has(-way * step)))
            stage.append(1)
            rings.append(())
        onward = []
        for copies, q in zip(flight, (side, 1 - side)):
            land(copies)
            if step + 1 < major:
                onward.append(line_go(step + 1, 0, q * low, low))
            if early:
                for i in range(known, len(blocks)):
                    block, present = blocks[i]
                    copy = copy_of(
                        on_ring(block, 0), q * (depth - middle), middle, on_ring(row, 1)
                    )
                    pl.when(present)(copy.start)
                    sends.append((present, copy))
                    rings[i] += (copy,)
        flight = onward
        if not early:
            for i in range(known, len(blocks)):
                rings[i] = ring_go(*blocks[i], 1)
        if early:
            if step == 1:
                advance(0)
            land(extra)
            extra = line_go(step, 1, middle, early)
        between(step)
        for i in range(known):
            if stage[i] <= half:
                advance(i)
    land(extra)
    for _ in range(half):
        for i in range(len(blocks)):
            if stage[i] <= half:
                advance(i)
    last()
    return [(when(present), copy) for present, copy in sends]


def rows_of(ref, d, capacity):
    return ref.at[:, piece(d, capacity)]


def slot_marks(slots, first, amount):
    spot = lax.broadcasted_iota(jnp.int32, (amount, slots.shape[1]), 0) + first
    return (spot == slots).astype(jnp.float32).astype(jnp.bfloat16)


def gather_kernel(
    n, w_ref, owner_ref, offset_ref, ids_ref, table_ref, cot_ref, bytes_ref, gain_ref,
    arrived, wanted_ref, proj_ref,
    w_all, tell, owner, offset, ids, table, looked, y_ref, cots, part, beside, own, away, across, half_ref,
    sums, chain, places, full, back_in, ws, wr, qs, qr, xs, xr, zs, zr, ts, ps, pr, cs, cr, gs, gr, ms, mr,
    ds, dr, es, er, ns, nr, local, still, kept, fs,
):
    core = lax.axis_index("mp")
    other = 1 - core
    major, minor = factors(n)
    me = lax.axis_index("table")
    row, place = me // minor, lax.rem(me, minor)
    side = lax.rem(me, 2)
    mate = {"table": me + 1 - 2 * side}
    twin = {"mp": other}
    depth = w_ref.shape[0]
    ngram, rows, width = table_ref.shape
    tokens = cot_ref.shape[0]
    quarter = width // 2
    capacity = looked.shape[1] // n
    plane = minor * capacity
    lines, fast = factors(n // 2)
    each = lines // 2
    span = fast * 2 * depth
    tile = width // 4

    def has(shift):
        return jnp.logical_and(row + shift >= 0, row + shift < major)

    w_swap = remote(
        w_ref.at[:, piece(1 - side, quarter)], w_all.at[piece(me, depth)],
        ps.at[0], pr.at[0], mate,
    )
    c_swap = remote(
        cot_ref.at[:, piece(1 - side, quarter)], cots.at[piece(side, tokens)],
        ps.at[1], pr.at[1], mate,
    )
    keep = (
        pltpu.make_async_copy(
            w_ref.at[:, piece(side, quarter)], w_all.at[piece(me, depth)], local.at[0]
        ),
        pltpu.make_async_copy(
            cot_ref.at[:, piece(side, quarter)], cots.at[piece(side, tokens)], local.at[1]
        ),
    )
    loads = [
        pltpu.make_async_copy(table_ref.at[k], table.at[k], ts.at[k]) for k in range(ngram)
    ]
    questions = []
    for j in range(1, n):
        to = lax.rem(me + j, n)
        questions.append(remote(tell, places.at[me], qs.at[j], qr.at[j], {"table": to}))

    facts = [
        pltpu.make_async_copy(src, dst, fs.at[i])
        for i, (src, dst) in enumerate(
            ((owner_ref, owner), (offset_ref, offset), (ids_ref, ids))
        )
    ]
    for copy in facts + [keep[0]] + loads + [keep[1]]:
        copy.start()

    def find_slots():
        before_mask = lax.broadcasted_iota(jnp.int32, (tokens, tokens), 0) < lax.broadcasted_iota(
            jnp.int32, (tokens, tokens), 1
        )
        earlier = before_mask.astype(jnp.float32).astype(jnp.bfloat16)
        for copy in facts:
            copy.wait()
        tell[...] = jnp.zeros(tell.shape, tell.dtype)
        tell[ngram : 2 * ngram, :] = offset[...]
        for k in range(ngram):
            owners = owner[k : k + 1, :]
            named = (lax.broadcasted_iota(jnp.int32, (n, tokens), 0) == owners).astype(jnp.float32)
            before = jnp.dot(
                named.astype(jnp.bfloat16), earlier, preferred_element_type=jnp.float32
            )
            rank = jnp.sum(before * named, axis=0, keepdims=True).astype(jnp.int32)
            tell[k : k + 1, :] = owners * capacity + rank
        places[me] = tell[...]

    greet_all(n, find_slots)
    w_swap.start()
    for copy in questions:
        copy.start()
    c_swap.start()

    def plane_copies(d):
        copies = []
        for j in range(1, minor):
            to = lax.rem(place + j, minor)
            copies.append(
                remote(
                    rows_of(looked, d * minor + to, capacity),
                    rows_of(y_ref, d * minor + place, capacity),
                    xs.at[d * minor + j], xr.at[d * minor + j], {"table": row * minor + to},
                )
            )
        return copies

    def stay(d):
        return pltpu.make_async_copy(
            rows_of(looked, d * minor + place, capacity),
            rows_of(y_ref, d * minor + place, capacity),
            still.at[d],
        )

    ends = [(d, way) for d in range(major - 1, 0, -1) for way in (1, -1)]

    def target(d, way):
        return lax.rem(row + way * d + major, major)

    def plane_go(d):
        for copy in plane_copies(d) + [stay(d)]:
            copy.start()

    group = 128 // capacity

    def find_rows():
        for copy in questions:
            copy.wait_recv()
        ours = lax.broadcasted_iota(jnp.int32, (capacity, tokens), 0) + me * capacity
        spots = lax.broadcasted_iota(jnp.int32, (128, rows), 1).astype(jnp.float32) + 1.0
        down = lax.broadcasted_iota(jnp.int32, (128, 128), 0)
        same = down == lax.broadcasted_iota(jnp.int32, (128, 128), 1)
        for k in range(ngram):
            for q in range(n // group):
                wanted = []
                for d in range(q * group, (q + 1) * group):
                    offsets = places[d, ngram + k : ngram + k + 1, :].astype(jnp.float32) + 1.0
                    named = ours == places[d, k : k + 1, :]
                    wanted.append(
                        jnp.sum(jnp.where(named, offsets, 0.0), axis=1, keepdims=True)
                    )
                wanted = jnp.concatenate(wanted, axis=0)
                wanted_ref[k : k + 1, q * 128 : (q + 1) * 128] = jnp.sum(
                    jnp.where(same, wanted, 0.0), axis=0, keepdims=True
                )
                full[q * 128 : (q + 1) * 128, k * rows : (k + 1) * rows] = (
                    (spots == wanted).astype(jnp.float32).astype(jnp.bfloat16)
                )

    def look_up():
        for load in loads:
            load.wait()
        for k in range(ngram):
            @pl.loop(0, 8)
            def _(c):
                columns = piece(c, width // 8)
                looked[k, :, columns] = jnp.dot(
                    full[:, k * rows : (k + 1) * rows],
                    table[k, :, columns],
                    preferred_element_type=jnp.float32,
                ).astype(looked.dtype)

    def arrive(d):
        for copy in plane_copies(d):
            copy.wait_recv()
        stay(d).wait()

    def part_of(d, columns):
        total = None
        for k in range(ngram):
            mark = slot_marks(places[d * minor + place, k : k + 1, :], row * plane, plane)
            term = lax.dot_general(
                mark,
                y_ref[k, piece(d, plane), columns],
                (((0,), (0,)), ((), ())),
                preferred_element_type=jnp.float32,
            )
            total = term if total is None else total + term
        return total

    def chain_copy(d, way, h):
        to = lax.rem(row + way + major, major) * minor + place
        spot = ((d - 1) * 2 + (0 if way == 1 else 1)) * CUTS + h
        land = major if d == 1 and way == -1 else target(d, way)
        columns = piece(h, width // CUTS)
        return remote(
            chain.at[target(d, way), :, columns], chain.at[land, :, columns],
            zs.at[spot], zr.at[spot], {"table": to},
        )

    def hop(d, way, among=None):
        goes = has(way * d)

        @pl.when(goes if among is None else jnp.logical_and(goes, among))
        def _():
            end = target(d, way)
            arrive(end)

            for h in range(CUTS):
                if d < major - 1:
                    pl.when(has(-way))(chain_copy(d + 1, way, h).wait_recv)

                @pl.loop(h * 4 // CUTS, (h + 1) * 4 // CUTS)
                def _(c):
                    columns = piece(c, tile)
                    total = part_of(end, columns) + chain[end, :, columns].astype(jnp.float32)
                    chain[end, :, columns] = total.astype(chain.dtype)

                chain_copy(d, way, h).start()

    def hand_out(d):
        if d == 0:
            plane_go(row)
        else:
            for way in (1, -1):
                pl.when(has(way * d))(functools.partial(plane_go, target(d, way)))

    def between(i):
        if i == 0:
            look_up()
            hand_out(major - 1)
            hand_out(major - 2)
            for way in (1, -1):
                @pl.when(jnp.logical_not(has(-way)))
                def _():
                    for d in range(0, major):
                        land = major if d == 0 and way == -1 else target(d, way)
                        chain[land] = jnp.zeros(chain.shape[1:], chain.dtype)

            c_swap.wait_recv()
            keep[1].wait()
        else:
            for way in (1, -1):
                head = jnp.logical_not(has(-way))
                if i == 1:
                    hop(major - 1, way)
                else:
                    hop(major - i, way, has(-way))
                if i < major - 1:
                    hop(major - 1 - i, way, head)
            if i < major - 1:
                hand_out(major - 2 - i)

    totals = remote(sums.at[0], sums.at[1], ms.at[0], mr.at[0], twin)
    inners = remote(sums.at[2], sums.at[3], ms.at[1], mr.at[1], twin)

    def embed():
        arrive(row)
        sums[0] = jnp.zeros(sums.shape[1:], jnp.float32)
        picks = slot_marks(ids[...], 0, bytes_ref.shape[0])
        for h in range(CUTS):
            for way in (1, -1):
                pl.when(has(-way))(chain_copy(1, way, h).wait_recv)

            @pl.loop(h * 4 // CUTS, (h + 1) * 4 // CUTS)
            def _(c):
                columns = piece(c, tile)
                total = lax.dot_general(
                    picks,
                    bytes_ref[:, columns],
                    (((0,), (0,)), ((), ())),
                    preferred_element_type=jnp.float32,
                )
                total = total + part_of(row, columns)
                total = total + chain[row, :, columns].astype(jnp.float32)
                total = total + chain[major, :, columns].astype(jnp.float32)
                rounded = total.astype(half_ref.dtype)
                half_ref[:, columns] = rounded
                values = rounded.astype(jnp.float32)
                sums[0] += jnp.broadcast_to(
                    jnp.sum(values * values, axis=1, keepdims=True), sums.shape[1:]
                )

        totals.start()

    chunk = min(512, span)

    pieces = span // chunk

    def to_twin(block, c):
        spot = lax.rem(block, each)
        return remote(
            part.at[:, pl.ds(pl.multiple_of(block * span + c * chunk, chunk), chunk)],
            beside.at[:, pl.ds(pl.multiple_of(spot * span + c * chunk, chunk), chunk)],
            cs.at[spot * pieces + c],
            cr.at[spot * pieces + c],
            twin,
        )

    def to_mate(spot, c):
        at = pl.ds(pl.multiple_of(spot * span + c * chunk, chunk), chunk)
        i = spot * pieces + c
        return remote(away.at[:, at], across.at[:, at], gs.at[i], gr.at[i], mate)

    def finish(block):
        spot = lax.rem(block, each)
        theirs, ours = piece(1 - side, tokens), piece(side, tokens)

        @pl.when(block // each == core)
        def _():
            for c in range(pieces):
                to_twin(block, c).wait_recv()
                come = pl.ds(pl.multiple_of(block * span + c * chunk, chunk), chunk)
                go = pl.ds(pl.multiple_of(spot * span + c * chunk, chunk), chunk)
                away[:, go] = (part[theirs, come] + beside[theirs, go]).astype(away.dtype)
                to_mate(spot, c).start()
            for c in range(pieces):
                come = pl.ds(pl.multiple_of(block * span + c * chunk, chunk), chunk)
                go = pl.ds(pl.multiple_of(spot * span + c * chunk, chunk), chunk)
                own[:, go] = part[ours, come] + beside[ours, go]

    waiting = []

    def done(block, when):
        @when
        def _():
            for c in range(pieces):
                some = pl.ds(pl.multiple_of(block * span + c * chunk, chunk), chunk)
                part[:, some] = lax.dot_general(
                    cots[...],
                    w_all[some, :],
                    (((1,), (1,)), ((), ())),
                    preferred_element_type=jnp.float32,
                )
                pl.when(block // each == other)(to_twin(block, c).start)

        waiting.append((block, when))
        if len(waiting) > 1:
            settle()

    def settle():
        block, when = waiting.pop(0)
        when(functools.partial(finish, block))

    keep[0].wait()
    started = run_gather(
        n // 2, w_all, 2 * depth, ws, wr, find_rows, w_swap.wait_recv, between, done, embed
    )
    while waiting:
        settle()

    totals.wait_recv()
    full_width = 2 * width
    sums[4] = lax.rsqrt((sums[0] + sums[1]) / full_width + eps)

    def block_of(whose):
        return full.at[piece(whose, tokens), piece(core, width)]

    swap = remote(block_of(side), block_of(side), ns.at[0], nr.at[0], mate)
    lend = remote(block_of(side), block_of(side), ns.at[1], nr.at[1], twin)
    pass_on = remote(block_of(1 - side), block_of(1 - side), ns.at[2], nr.at[2], twin)
    back = remote(away.at[:, :quarter], back_in, ns.at[3], nr.at[3], mate)

    def gain_of(c):
        return gain_ref[:, pl.ds(pl.multiple_of(core * width + c * tile, tile), tile)]

    @pl.loop(0, 4)
    def _(c):
        values = half_ref[:, piece(c, tile)].astype(jnp.float32)
        there = pl.ds(pl.multiple_of(core * width + c * tile, tile), tile)
        full[piece(side, tokens), there] = (values * sums[4][:, :1] * gain_of(c)).astype(
            full.dtype
        )

    swap.start()
    lend.start()
    sums[2] = jnp.zeros(sums.shape[1:], jnp.float32)
    for spot in range(each):
        for c in range(pieces):
            to_mate(spot, c).wait_recv()

    @pl.loop(0, 4)
    def _(c):
        columns = piece(c, tile)
        scaled = (own[:, columns] + across[:, columns].astype(jnp.float32)) * gain_of(c)
        own[:, columns] = scaled
        values = half_ref[:, columns].astype(jnp.float32)
        sums[2] += jnp.broadcast_to(
            jnp.sum(values * scaled, axis=1, keepdims=True), sums.shape[1:]
        )

    inners.start()
    for d in range(major):
        for copy in plane_copies(d):
            copy.wait_send()
    inners.wait_recv()

    per = rows // tokens
    broad = width // 2

    def line_of(origin, h):
        return table.at[origin // per, piece(lax.rem(origin, per), tokens), piece(h, broad)]

    def line_copy(step, way, h):
        origin = lax.rem(row - way * (step - 1) + major, major)
        to = lax.rem(row + way + major, major) * minor + place
        spot = ((step - 1) * 2 + (0 if way == 1 else 1)) * 2 + h
        here = line_of(origin, h)
        return remote(here, here, ds.at[spot], dr.at[spot], {"table": to})

    def leaves(step, way):
        return jnp.logical_and(has(-way * (step - 1)), has(way))

    def give_copies(i, origin, h):
        copies = []
        for j in range(1, minor):
            to = lax.rem(place + j, minor)
            spot = (i * minor + j) * 2 + h
            copies.append(
                remote(
                    looked.at[:, piece(origin * minor + to, capacity), piece(h, broad)],
                    arrived.at[:, piece(origin * minor + place, capacity), piece(h, broad)],
                    es.at[spot], er.at[spot], {"table": row * minor + to},
                )
            )
        return copies

    def keep_own(origin, h):
        at = piece(origin * minor + place, capacity)
        return pltpu.make_async_copy(
            looked.at[:, at, piece(h, broad)],
            arrived.at[:, at, piece(h, broad)],
            kept.at[origin * 2 + h],
        )

    def give(i, origin, h):
        for k in range(ngram):
            mark = slot_marks(
                places[origin * minor + place, k : k + 1, :], row * plane, plane
            )
            looked[k, piece(origin, plane), h * broad : (h + 1) * broad] = jnp.dot(
                mark,
                table[
                    origin // per,
                    piece(lax.rem(origin, per), tokens),
                    h * broad : (h + 1) * broad,
                ],
                preferred_element_type=jnp.float32,
            ).astype(looked.dtype)
        for copy in give_copies(i, origin, h) + [keep_own(origin, h)]:
            copy.start()

    for h in range(2):
        @pl.loop(0, 2)
        def _(c):
            columns = pl.ds(pl.multiple_of(h * broad + c * tile, tile), tile)
            scale = sums[4][:, :1]
            inner = (sums[2][:, :1] + sums[3][:, :1]) / full_width
            values = half_ref[:, columns].astype(jnp.float32)
            table[row // per, piece(lax.rem(row, per), tokens), columns] = (
                scale * own[:, columns] - values * scale * scale * scale * inner
            ).astype(table.dtype)

        for way in (1, -1):
            pl.when(leaves(1, way))(line_copy(1, way, h).start)

    step_of = min(256, quarter)

    def project(whose, out):
        @pl.loop(0, quarter // step_of)
        def _(c):
            columns = piece(c, step_of)
            out(
                c,
                jnp.dot(
                    full[piece(whose, tokens), :],
                    w_all[:, columns],
                    preferred_element_type=jnp.float32,
                ),
            )

    def put_away(c, values):
        away[:, piece(c, step_of)] = values.astype(away.dtype)

    def put_own(c, values):
        there = pl.ds(pl.multiple_of(side * quarter + c * step_of, step_of), step_of)
        proj_ref[:, there] = values.astype(proj_ref.dtype)

    def project_away():
        lend.wait_recv()
        pass_on.wait_recv()
        for spot in range(each):
            for c in range(pieces):
                to_mate(spot, c).wait_send()
        project(1 - side, put_away)
        back.start()

    for h in range(2):
        give(0, row, h)
    swap.wait_recv()
    pass_on.start()
    blocks = [(0, row, None)]
    for s in range(1, major):
        new = []
        for way in (1, -1):
            new.append((len(blocks), lax.rem(row - way * s + major, major), has(-way * s)))
            blocks.append(new[-1])
        for h in range(2):
            for way in (1, -1):
                pl.when(has(-way * s))(line_copy(s, way, h).wait_recv)
                if s + 1 < major:
                    pl.when(leaves(s + 1, way))(line_copy(s + 1, way, h).start)
            for i, origin, present in new:
                pl.when(present)(functools.partial(give, i, origin, h))
        if s == 1:
            project_away()
        if s == min(2, major - 1):
            project(side, put_own)

    back.wait_recv()
    proj_ref[:, piece(1 - side, quarter)] = back_in[...]
    for i, origin, present in blocks:

        def end():
            for h in range(2):
                for copy in give_copies(i, origin, h):
                    copy.wait_recv()
                    copy.wait_send()
                keep_own(origin, h).wait()

        if present is None:
            end()
        else:
            pl.when(present)(end)
    for copy in questions + [w_swap, c_swap, totals, inners, swap, lend, pass_on, back]:
        copy.wait_send()
    for d, way in ends:
        for h in range(CUTS):
            pl.when(has(way * d))(chain_copy(d, way, h).wait_send)
    for spot in range(each):
        for c in range(pieces):
            to_twin(other * each + spot, c).wait_send()
    for when, copy in started:
        when(copy.wait_send)
    for s in range(1, major):
        for way in (1, -1):
            for h in range(2):
                pl.when(leaves(s, way))(line_copy(s, way, h).wait_send)


def gather_and_exchange(w, owners, offsets, ids, table, cot, codes, gain, capacity, n):
    steps = gather_steps(n // 2)
    lines = factors(n // 2)[0]
    major, minor = factors(n)
    ngram, _, width = table.shape
    levels = -(-ngram // 8) * 8
    span = n * w.shape[0] // lines
    pieces = lines // 2 * (span // min(512, span))
    tokens = cot.shape[0]
    depth = w.shape[0]
    half = (tokens, width)
    told = (-(-2 * ngram // 8) * 8, tokens)
    f32, bf16 = jnp.float32, jnp.bfloat16
    dma = pltpu.SemaphoreType.DMA
    return pl.pallas_call(
        functools.partial(gather_kernel, n),
        out_shape=(
            jax.ShapeDtypeStruct((ngram, n * capacity, width), bf16),
            jax.ShapeDtypeStruct((levels, n * capacity), f32),
            jax.ShapeDtypeStruct(half, bf16),
        ),
        in_specs=[ANY, ANY, ANY, ANY, ANY, ANY, WHOLE, WHOLE],
        out_specs=(ANY, WHOLE, WHOLE),
        scratch_shapes=[
            pltpu.VMEM((n * depth, width // 2), w.dtype),
            pltpu.VMEM(told, owners.dtype),
            pltpu.VMEM(owners.shape, owners.dtype),
            pltpu.VMEM(offsets.shape, offsets.dtype),
            pltpu.VMEM(ids.shape, ids.dtype),
            pltpu.VMEM(table.shape, table.dtype),
            pltpu.VMEM((ngram, n * capacity, width), table.dtype),
            pltpu.VMEM((ngram, n * capacity, width), table.dtype),
            pltpu.VMEM((2 * tokens, width // 2), cot.dtype),
            pltpu.VMEM((2 * tokens, n * depth), f32),
            pltpu.VMEM((2 * tokens, width), f32),
            pltpu.VMEM(half, f32),
            pltpu.VMEM(half, bf16),
            pltpu.VMEM(half, bf16),
            pltpu.VMEM(half, bf16),
            pltpu.VMEM((5, tokens, 128), f32),
            pltpu.VMEM((major + 1, *half), bf16),
            pltpu.VMEM((n, *told), owners.dtype),
            pltpu.VMEM((2 * tokens, 2 * width), bf16),
            pltpu.VMEM((tokens, width // 2), bf16),
            dma((steps,)),
            dma((steps,)),
            dma((n,)),
            dma((n,)),
            dma((n,)),
            dma((n,)),
            dma((2 * (major - 1) * CUTS,)),
            dma((2 * (major - 1) * CUTS,)),
            dma((ngram,)),
            dma((2,)),
            dma((2,)),
            dma((pieces,)),
            dma((pieces,)),
            dma((pieces,)),
            dma((pieces,)),
            dma((2,)),
            dma((2,)),
            dma((4 * (major - 1),)),
            dma((4 * (major - 1),)),
            dma((2 * (2 * major - 1) * minor,)),
            dma((2 * (2 * major - 1) * minor,)),
            dma((4,)),
            dma((4,)),
            dma((2,)),
            dma((major,)),
            dma((2 * major,)),
            dma((3,)),
        ],
        compiler_params=pltpu.CompilerParams(
            collective_id=1, has_side_effects=True, vmem_limit_bytes=VMEM_LIMIT
        ),
    )(w, owners, offsets, ids, table, cot, codes, gain)


def sum_kernel(wanted_ref, arrived_ref, proj_ref, out_ref, proj_out, hits):
    k = pl.program_id(0)
    rows, slots = hits.shape
    proj_out[...] = proj_ref[...]

    @pl.when(pl.program_id(1) == 0)
    def _():
        spots = lax.broadcasted_iota(jnp.int32, (rows, slots), 0).astype(jnp.float32) + 1.0
        wanted = wanted_ref[pl.ds(k, 1), :]
        hits[...] = (spots == wanted).astype(jnp.float32).astype(hits.dtype)

    out_ref[0] = jnp.dot(
        hits[...], arrived_ref[0], preferred_element_type=jnp.float32
    ).astype(out_ref.dtype)


def sum_rows(wanted, arrived, projected, rows):
    ngram, slots, width = arrived.shape
    tile = min(2048, width)
    across = width // tile
    some = pl.BlockSpec(
        (projected.shape[0] // (ngram * across), width), lambda k, c: (k * across + c, 0)
    )
    return pl.pallas_call(
        sum_kernel,
        grid=(ngram, width // tile),
        out_shape=(
            jax.ShapeDtypeStruct((ngram, rows, width), arrived.dtype),
            jax.ShapeDtypeStruct(projected.shape, projected.dtype),
        ),
        in_specs=[
            pl.BlockSpec(wanted.shape, lambda k, c: (0, 0)),
            pl.BlockSpec((1, slots, tile), lambda k, c: (k, 0, c)),
            some,
        ],
        out_specs=(pl.BlockSpec((1, rows, tile), lambda k, c: (k, 0, c)), some),
        scratch_shapes=[pltpu.VMEM((rows, slots), jnp.bfloat16)],
        compiler_params=pltpu.CompilerParams(vmem_limit_bytes=VMEM_LIMIT),
    )(wanted, arrived, projected)


def on_device(
    hash_tables, byte_table, byte_ids, hash_owner, hash_offset, gain, proj_weight, cotangent
):
    groups = lax.axis_size("table")
    ngram, rows_dev, _ = hash_tables.shape
    tokens = byte_ids.shape[0]
    capacity = 2 * tokens // groups
    arrived, wanted, projected = gather_and_exchange(
        proj_weight, hash_owner[:, :, 0], hash_offset, byte_ids[None, :], hash_tables, cotangent,
        byte_table, gain[None, :], capacity, groups,
    )
    grads, projected = sum_rows(wanted, arrived, projected, rows_dev)
    return (projected, grads)


def solution(mesh):
    return jax.shard_map(
        on_device,
        mesh=mesh,
        in_specs=(
            P(None, "table", "mp"),
            P(None, "mp"),
            P("table"),
            P(None, "table", None),
            P(None, "table"),
            P(),
            P("table", "mp"),
            P("table", "mp"),
        ),
        out_specs=(P("table", "mp"), P(None, "table", "mp")),
        check_vma=False,
    )
```
